32 devices in a mesh: gx: 8 (over z, y), gy: 4 (over x, core).
Axes of the slice: x: 2, y: 2, z: 4, core: 2. Of those that a mesh axis runs over, the one named last changes fastest.
Arguments:
- density: float32 [4, 128, 512], P(None, 'gx', 'gy'), may hold values from 0 to 1
- tile_mask: int32 [16, 64], P('gx', 'gy'), may hold values 0 or 1
- material: int32 [8, 128, 512], P(None, 'gx', 'gy'), may hold values from 0 to 3
- material_table: float32 [3, 4], replicated, may hold values from 1 to 4
- contrast: float32 [3], replicated, may hold values from 1 to 3
- electric: float32 [3, 8, 128, 512], P(None, None, 'gx', 'gy'), may hold values from -6 to 6
- magnetic: float32 [3, 8, 128, 512], P(None, None, 'gx', 'gy'), may hold values from -6 to 6
- forward_fields: bfloat16 [4, 3, 8, 128, 512], P(None, None, None, 'gx', 'gy'), may hold values from -6 to 6
Outputs:
- electric_final: float32 [3, 8, 128, 512], P(None, None, 'gx', 'gy')
- magnetic_final: float32 [3, 8, 128, 512], P(None, None, 'gx', 'gy')
- design_gradient: float32 [4, 128, 512], P(None, 'gx', 'gy')
The draws below stay inside these ranges and needn't reach their ends.
All inputs are finite; a program needn't handle non-finite values. No bound on the sum of `tile_mask` on one device may be relied on, other than what follows from the above.
Results may differ from the reference program's by a relative error of at most 0.00065.
Values sent between devices are 32-bit elements; how exact they have to be, the bound alone decides.
No kernel may reach another device: no remote copies, remote signals or barrier semaphores. Data moves between devices by JAX's collectives and lax.ppermute only.
A program may use at most 64 MiB of HBM per device.

```python
import jax
import jax.numpy as jnp
from jax import lax

CY = 128
Z = 8
DZ = 4
STEPS = 4
TILE = 8
MATS = 4
NX = 128
NY = 512


def plant(values, key, low, largest):
    longest = values.shape.index(max(values.shape))
    spots = []
    for shift in (0, 1):
        where = [jax.random.randint(jax.random.fold_in(key, axis), (), 0, length) for axis, length in enumerate(values.shape)]
        where[longest] = (where[longest] + shift) % values.shape[longest]
        spots.append(tuple(where))
    return values.at[spots[0]].set(low).at[spots[1]].set(largest)


def block_scale(own_key, shape, split, least, high):
    def one(dim, blocks):
        heights = jax.random.uniform(jax.random.fold_in(jax.random.fold_in(own_key, 6), dim), (blocks,), jnp.float32, least / len(split), high / len(split))
        return jnp.repeat(jnp.exp(heights), shape[dim] // blocks).reshape((-1,) + (1,) * (len(shape) - dim - 1))

    loudness = one(*split[0])
    for cut in split[1:]:
        loudness = loudness * one(*cut)
    return loudness


def scatter_about(stream_key, shape, scale, bound, split=(), held_as=jnp.bfloat16):
    drawn = jax.random.normal(stream_key, shape, jnp.float32) * scale
    if len(split) > 0:
        drawn = block_scale(stream_key, shape, split, -0.22, 0.18) * drawn
    return jnp.clip(drawn, min=-bound, max=bound).astype(held_as)


def setup_inputs(seed: int = 0) -> dict:
    key_list = jax.random.split(jax.random.key(seed), 9)
    return {
        "density": jnp.clip(1.0 * jax.random.uniform(key_list[0], (DZ, NX, NY), jnp.float32) ** block_scale(key_list[0], (DZ, NX, NY), ((1, 8), (2, 4)), -0.2, 0.2), 0.0, 1.0),
        "tile_mask": plant((jax.random.randint(key_list[1], (NX // TILE, NY // TILE), 0, 4) < 3).astype(jnp.int32), jax.random.fold_in(key_list[1], 1), 0, 1),
        "material": plant(jax.random.randint(key_list[2], (Z, NX, NY), 0, MATS), jax.random.fold_in(key_list[2], 1), 0, MATS - 1).astype(jnp.int32),
        "material_table": jnp.clip(jax.random.uniform(key_list[3], (3, MATS), jnp.float32, 1.0, 4.0), 1.0, 4.0),
        "contrast": jnp.clip(jax.random.uniform(key_list[4], (3,), jnp.float32, 1.0, 3.0), 1.0, 3.0),
        "electric": scatter_about(key_list[5], (3, Z, NX, NY), 1.0, 6.0, ((2, 8), (3, 4)), jnp.float32),
        "magnetic": scatter_about(key_list[6], (3, Z, NX, NY), 1.0, 6.0, ((2, 8), (3, 4)), jnp.float32),
        "forward_fields": scatter_about(key_list[7], (STEPS, 3, Z, NX, NY), 1.0, 6.0, ((3, 8), (4, 4))),
    }


courant = 0.5
sharpness = 4.0
threshold = 0.5


def kernel_weights(source, target, count, reach):
    offsets = target[None, :] - source[:, None]
    ahead = jnp.mod(offsets, count).astype(jnp.float32)
    behind = jnp.mod(-offsets, count).astype(jnp.float32)
    return jnp.exp(-ahead / reach) + jnp.exp(-behind / reach)


def project(values):
    bottom = jnp.tanh(sharpness * threshold) + jnp.tanh(sharpness * (1.0 - threshold))
    level = jnp.tanh(sharpness * (values - threshold))
    return (jnp.tanh(sharpness * threshold) + level) / bottom, sharpness * (1.0 - level * level) / bottom


def inverse_permittivity(projected, cell_mask, material, material_table, contrast):
    layered = jnp.repeat(projected, Z // DZ, axis=0)
    design = cell_mask[None] * layered
    result = []
    for channel in range(3):
        background = jnp.zeros(material.shape, jnp.float32)
        for index in range(MATS):
            background = background + jnp.where(material == index, material_table[channel, index], 0.0)
        result.append(1.0 / (background + design * contrast[channel]))
    return jnp.stack(result)


def z_ahead(values):
    return jnp.concatenate([values[1:], jnp.zeros_like(values[:1])], 0) - values


def z_behind(values):
    return values - jnp.concatenate([jnp.zeros_like(values[:1]), values[:-1]], 0)


def lateral_ahead(values, axis):
    return jnp.roll(values, -1, axis) - values


def lateral_behind(values, axis):
    return values - jnp.roll(values, 1, axis)


def curl_ahead(field):
    part_x, part_y, part_z = field[0], field[1], field[2]
    return jnp.stack([lateral_ahead(part_z, 2) - z_ahead(part_y), z_ahead(part_x) - lateral_ahead(part_z, 1), lateral_ahead(part_y, 1) - lateral_ahead(part_x, 2)])


def curl_behind(field):
    part_x, part_y, part_z = field[0], field[1], field[2]
    return jnp.stack([lateral_behind(part_z, 2) - z_behind(part_y), z_behind(part_x) - lateral_behind(part_z, 1), lateral_behind(part_y, 1) - lateral_behind(part_x, 2)])


def accumulate(gained, contrast, electric, forward_step):
    return gained + jnp.sum(contrast[:, None, None, None] * electric * forward_step.astype(jnp.float32), axis=0)


def reference(density, tile_mask, material, material_table, contrast, electric, magnetic, forward_fields):
    count = density.shape[2]
    reach = 4.0 * CY
    positions = jnp.arange(count, dtype=jnp.int32)
    weights = kernel_weights(positions, positions, count, reach)
    norm_total = 2.0 * jnp.sum(jnp.exp(-positions.astype(jnp.float32) / reach))
    smooth = jnp.dot(density.reshape(-1, count), weights, precision=lax.Precision.HIGHEST, preferred_element_type=jnp.float32).reshape(density.shape)
    filtered = 0.5 * density + 0.5 * smooth / norm_total
    projected, slope = project(filtered)
    cell_mask = jnp.repeat(jnp.repeat(tile_mask, TILE, 0), TILE, 1).astype(jnp.float32)
    inverse = inverse_permittivity(projected, cell_mask, material, material_table, contrast)
    gained = jnp.zeros(material.shape, jnp.float32)
    for step in range(STEPS):
        magnetic = magnetic - courant * curl_ahead(electric)
        electric = electric + courant * inverse * curl_behind(magnetic)
        gained = accumulate(gained, contrast, electric, forward_fields[step])
    layered = gained.reshape(DZ, Z // DZ, gained.shape[1], gained.shape[2]).sum(axis=1)
    design_gradient = cell_mask[None] * slope * layered
    return electric, magnetic, design_gradient
```

```python
import math

import jax
import jax.numpy as jnp
import numpy as np
from jax import lax
from jax.experimental import pallas as pl
from jax.experimental.pallas import tpu as pltpu
from jax.sharding import PartitionSpec as P

CY = 128
Z = 8
DZ = 4
STEPS = 4
TILE = 8
MATS = 4

courant = 0.5
sharpness = 4.0
threshold = 0.5

ROWS = 24
OWN = 16
SLOT = 64


def in_vmem(x):
    return pltpu.with_memory_space_constraint(x, pltpu.VMEM)


def call(kernel, outs, ins, aliases=None, scratch=()):
    return pl.pallas_call(
        kernel,
        out_shape=outs,
        in_specs=[pl.BlockSpec(memory_space=pltpu.VMEM)] * len(ins),
        out_specs=[pl.BlockSpec(memory_space=pltpu.VMEM)] * len(outs),
        scratch_shapes=list(scratch),
        input_output_aliases=aliases or {},
        compiler_params=pltpu.CompilerParams(vmem_limit_bytes=32 * 1024 * 1024),
    )(*[in_vmem(x) for x in ins])


def vmem(*shape):
    return pltpu.VMEM(shape, jnp.float32)


def lanes(rows):
    return lax.broadcasted_iota(jnp.int32, (rows, 128), 1)


def roll(x, by):
    return pltpu.roll(x, by % x.shape[1], 1)


def roll_rows(x, by):
    return pltpu.roll(x, by % x.shape[0], 0)


def passed_along(x, axis, by):
    size = lax.axis_size(axis)
    return lax.ppermute(x, axis, [(i, (i + by) % size) for i in range(size)])


def weight(offset, count, reach):
    ahead = np.mod(offset, count).astype(np.float64)
    behind = np.mod(-offset, count).astype(np.float64)
    return np.exp(-ahead / reach) + np.exp(-behind / reach)


def filter_constants(count, reach):
    source = np.arange(CY)
    strip = np.concatenate([np.arange(-4, 4), np.arange(CY - 4, CY + 4)])
    targets = np.concatenate([source, np.tile(strip, Z)])
    table = weight(targets[None, :] - source[:, None], count, reach)
    rows = np.zeros((8, 256))
    rows[0] = np.exp(-targets / reach)
    rows[1] = np.exp(targets / reach)
    rows[2, :CY] = np.exp(source / reach)
    rows[3, :CY] = np.exp(-source / reach)
    spread = np.zeros((16, 128))
    spread[np.arange(128) // TILE, np.arange(128)] = 1.0
    return (
        jnp.asarray(table, jnp.float32),
        jnp.asarray(rows, jnp.float32),
        jnp.asarray(spread, jnp.float32),
    )


def pack_rows_kernel(electric, magnetic, density, material, mask, spread, to_prev, to_next):
    cells = jnp.dot(
        mask[...].astype(jnp.float32), spread[...], preferred_element_type=jnp.float32
    )

    def e(channel, row):
        return electric[pl.ds(channel * 128 + row, Z, stride=OWN), :]

    def h(channel, row):
        return magnetic[pl.ds(channel * 128 + row, Z, stride=OWN), :]

    def ahead_part(row):
        part_y = h(1, row) + courant * (e(2, row + 1) - e(2, row))
        part_z = h(2, row) - courant * (e(1, row + 1) - e(1, row))
        return part_y, part_z

    for out, first, mask_row in ((to_prev, 0, 0), (to_next, OWN - 3, 1)):
        for slot in range(3):
            row, at = first + slot, slot * SLOT
            for channel in range(3):
                out[at + 8 * channel : at + 8 * channel + 8, :] = e(channel, row)
                out[at + 24 + 8 * channel : at + 32 + 8 * channel, :] = h(channel, row)
            out[at + 48 : at + 56, :] = material[pl.ds(row, Z, stride=OWN), :].astype(jnp.float32)
            out[at + 56 : at + 60, :] = density[pl.ds(row, DZ, stride=OWN), :]
            out[at + 60 : at + 64, :] = jnp.broadcast_to(cells[mask_row : mask_row + 1], (4, 128))
    part_y, part_z = ahead_part(2)
    to_prev[2 * SLOT + 32 : 2 * SLOT + 40, :] = part_y
    to_prev[2 * SLOT + 40 : 2 * SLOT + 48, :] = part_z
    part_y, part_z = ahead_part(OWN - 4)
    to_next[3 * SLOT : 3 * SLOT + 8, :] = e(0, OWN - 4)
    to_next[3 * SLOT + 8 : 3 * SLOT + 16, :] = part_y
    to_next[3 * SLOT + 16 : 3 * SLOT + 24, :] = part_z


def edge_window(planes):
    rows = planes[0].shape[0]
    lane = lanes(rows)
    window = (lane < 4) | (lane >= 124)
    gathered = planes[7]
    for z in range(6, -1, -1):
        gathered = jnp.where(window, planes[z], roll(gathered, 16))
    return gathered


def edge_pairs(groups):
    lane = lanes(groups[0][0].shape[0])
    first = (lane & 15) < 8
    found = [edge_window(planes) for planes in groups]
    return [
        jnp.where(first, roll(found[2 * i], 4), roll(found[2 * i + 1], 12)) for i in range(4)
    ]


def edge_messages(pairs):
    quarter = (lanes(pairs[0].shape[0]) >> 2) & 3

    def pick(a, b, c, d):
        return jnp.where(quarter < 2, jnp.where(quarter == 0, a, b), jnp.where(quarter == 2, c, d))

    left, right = [], []
    for one, two in ((pairs[0], pairs[1]), (pairs[2], pairs[3])):
        left.append(pick(roll(one, -4), roll(one, -8), roll(two, 4), two))
        right.append(pick(one, roll(one, -4), roll(two, 8), roll(two, 4)))
    return left, right


def density_planes(layers, cells, rising, falling):
    place = lanes(cells.shape[0]) & 3
    planes = []
    for layer in layers:
        up = jnp.sum(layer * rising, axis=1, keepdims=True)
        down = jnp.sum(layer * falling, axis=1, keepdims=True)
        planes += [layer, jnp.where(place == 0, up, jnp.where(place == 1, down, cells))]
    return planes


def own_kernel(
    electric, magnetic, density, material, mask, table, factors, spread,
    e_all, h_all, m_all, d_all, c_all, local, pairs_out, left_out, right_out,
):
    cells2 = jnp.dot(
        mask[...].astype(jnp.float32), spread[...], preferred_element_type=jnp.float32
    )
    cells = jnp.concatenate(
        [jnp.broadcast_to(cells2[i : i + 1], (TILE, 128)) for i in range(2)], 0
    )
    c_all[0:OWN, :] = cells
    groups = []
    for source, target in ((electric, e_all), (magnetic, h_all)):
        for channel in range(3):
            planes = []
            for z in range(Z):
                p = channel * Z + z
                plane = source[p * OWN : (p + 1) * OWN, :]
                target[p * ROWS : p * ROWS + OWN, :] = plane
                planes.append(plane)
            groups.append(planes)
    planes = []
    for z in range(Z):
        plane = material[z * OWN : (z + 1) * OWN, :].astype(jnp.float32)
        m_all[z * ROWS : z * ROWS + OWN, :] = plane
        planes.append(plane)
    groups.append(planes)
    layers = []
    for layer in range(DZ):
        plane = density[layer * OWN : (layer + 1) * OWN, :]
        d_all[layer * ROWS : layer * ROWS + OWN, :] = plane
        layers.append(plane)
    groups.append(density_planes(layers, cells, factors[2:3, 0:128], factors[3:4, 0:128]))
    pairs = edge_pairs(groups)
    left, right = edge_messages(pairs)
    for i in range(4):
        pairs_out[i * ROWS : i * ROWS + OWN, :] = pairs[i]
    for i in range(2):
        left_out[i * ROWS : i * ROWS + OWN, :] = left[i]
        right_out[i * ROWS : i * ROWS + OWN, :] = right[i]
    smooth = jnp.dot(
        density[...], table[...], precision=lax.Precision.HIGHEST,
        preferred_element_type=jnp.float32,
    )
    for layer in range(DZ):
        local[layer * ROWS : layer * ROWS + OWN, :] = smooth[layer * OWN : (layer + 1) * OWN]


def halo_kernel(
    from_next, from_prev, e_in, h_in, m_in, d_in, c_in, pairs_in, left_in, right_in, factors,
    e_all, h_all, m_all, d_all, c_all, pairs_out, left_out, right_out, sums_out,
):
    for got, first in ((from_next, 16), (from_prev, 21)):
        for slot in range(3):
            at, row = slot * SLOT, first + slot
            for channel in range(3):
                where = pl.ds(channel * Z * ROWS + row, Z, stride=ROWS)
                e_all[where, :] = got[at + 8 * channel : at + 8 * channel + 8, :]
                h_all[where, :] = got[at + 24 + 8 * channel : at + 32 + 8 * channel, :]
            m_all[pl.ds(row, Z, stride=ROWS), :] = got[at + 48 : at + 56, :]
            d_all[pl.ds(row, DZ, stride=ROWS), :] = got[at + 56 : at + 60, :]
            c_all[row : row + 1, :] = got[at + 60 : at + 61, :]
    zeros = jnp.zeros((Z, 128), jnp.float32)
    for channel in range(3):
        at = channel * Z * ROWS
        e_all[pl.ds(at + 19, Z, stride=ROWS), :] = from_next[
            2 * SLOT + 8 * channel : 2 * SLOT + 8 * channel + 8, :
        ]
        h_all[pl.ds(at + 19, Z, stride=ROWS), :] = zeros
        if channel > 0:
            e_all[pl.ds(at + 20, Z, stride=ROWS), :] = from_prev[8 * channel : 8 * channel + 8, :]
            h_all[pl.ds(at + 20, Z, stride=ROWS), :] = from_prev[
                3 * SLOT + 8 * channel : 3 * SLOT + 8 * channel + 8, :
            ]
        else:
            e_all[pl.ds(at + 20, Z, stride=ROWS), :] = from_prev[3 * SLOT : 3 * SLOT + 8, :]
            h_all[pl.ds(at + 20, Z, stride=ROWS), :] = zeros
    for row in (19, 20):
        m_all[pl.ds(row, Z, stride=ROWS), :] = zeros
        d_all[pl.ds(row, DZ, stride=ROWS), :] = zeros[0:DZ]
        c_all[row : row + 1, :] = zeros[0:1]

    groups = []
    for target in (e_all, h_all):
        for channel in range(3):
            groups.append(
                [target[(channel * Z + z) * ROWS + OWN : (channel * Z + z + 1) * ROWS, :] for z in range(Z)]
            )
    groups.append([m_all[z * ROWS + OWN : (z + 1) * ROWS, :] for z in range(Z)])
    layers = [d_all[layer * ROWS + OWN : (layer + 1) * ROWS, :] for layer in range(DZ)]
    cells = c_all[OWN:ROWS, :]
    groups.append(density_planes(layers, cells, factors[2:3, 0:128], factors[3:4, 0:128]))
    pairs = edge_pairs(groups)
    left, right = edge_messages(pairs)
    for i in range(4):
        pairs_out[i * ROWS + OWN : (i + 1) * ROWS, :] = pairs[i]
    for i in range(2):
        left_out[i * ROWS + OWN : (i + 1) * ROWS, :] = left[i]
        right_out[i * ROWS + OWN : (i + 1) * ROWS, :] = right[i]
    sums_out[0:OWN, :] = left_in[ROWS : ROWS + OWN, :]
    sums_out[OWN:ROWS, :] = left[1]


def project(values):
    base = math.tanh(sharpness * threshold)
    bottom = base + math.tanh(sharpness * (1.0 - threshold))
    level = jnp.tanh(sharpness * (values - threshold))
    return (base + level) * (1.0 / bottom), (sharpness / bottom) * (1.0 - level * level)


def step_kernel(count, reach, others):
    devices = count // CY
    norm_total = 2.0 * float(np.sum(np.exp(-np.arange(count) / reach)))

    def factor(m):
        return math.exp(-CY * m / reach), math.exp(-(count - CY * m) / reach)

    def fix(delta):
        if delta == 0:
            return 1.0 - math.exp(-count / reach)
        return (
            math.exp(-delta / reach) + math.exp(-(count - delta) / reach)
            - math.exp(-(count + delta) / reach) - math.exp(delta / reach)
        )

    def kernel(*refs):
        material_table, contrast, from_right, from_left = refs[:4]
        rest = refs[4 : 4 + others]
        (e_in, h_in, m_all, d_all, c_all, pairs, local, table, factors, forward,
         e_final, h_final, gradient, e_all, h_all, inverse, se, sh, si, gained) = refs[4 + others :]
        lane = lanes(ROWS)
        place = lane & 15
        odd = ((lane >> 4) & 1) == 1
        layer_of = lane >> 5
        part = place >> 2

        got_left = [from_left[i * ROWS : (i + 1) * ROWS, :] for i in range(2)]
        got_right = [from_right[i * ROWS : (i + 1) * ROWS, :] for i in range(2)]

        def strip(index):
            tile, q = index // 4, index % 4
            pair = pairs[(index // 2) * ROWS : (index // 2 + 1) * ROWS, :]
            if index % 2 == 0:
                own_l, own_r = pair, roll(pair, 8)
            else:
                own_l, own_r = roll(pair, -8), pair
            outer = jnp.where(part == 0, roll(got_left[tile], -4 * q), roll(got_right[tile], 12 - 4 * q))
            return jnp.where(part == 1, own_l, jnp.where(part == 2, own_r, outer))

        for channel in range(3):
            se[channel * ROWS : (channel + 1) * ROWS, :] = strip(channel)
            sh[channel * ROWS : (channel + 1) * ROWS, :] = strip(3 + channel)
        strip_material = strip(6)
        raw = strip(7)
        strip_density = jnp.where(odd, roll(raw, 16), raw)
        marks = jnp.where(odd, raw, roll(raw, -16))
        strip_cells = jnp.where((place & 2) == 2, marks, roll(marks, -2))

        def lane_factor(m):
            up, down = factor(m)
            return jnp.where(place == 12, up, down)

        sums = lane_factor(1) * got_left[1] + lane_factor(devices - 1) * got_right[1]
        for i, other in enumerate(rest):
            sums = sums + lane_factor(2 + i) * other[...]
        halo_local = jnp.dot(
            jnp.concatenate([d_all[l * ROWS + OWN : (l + 1) * ROWS, :] for l in range(DZ)], 0),
            table[...], precision=lax.Precision.HIGHEST, preferred_element_type=jnp.float32,
        )
        strip_smooth = jnp.zeros((ROWS, 128), jnp.float32)
        designs, slopes = [], []
        cells = c_all[...]
        for l in range(DZ):
            at = (2 * l + 1) * 16 + 12
            up = jnp.broadcast_to(sums[:, at : at + 1], (ROWS, 128))
            down = jnp.broadcast_to(sums[:, at + 1 : at + 2], (ROWS, 128))
            own = local[l * ROWS : l * ROWS + OWN, :]
            both = jnp.concatenate([own, halo_local[l * 8 : (l + 1) * 8]], 0)
            smooth = both[:, :128] + factors[0:1, :128] * up + factors[1:2, :128] * down
            far = both[:, 128:] + factors[0:1, 128:] * up + factors[1:2, 128:] * down
            strip_smooth = jnp.where(layer_of == l, far, strip_smooth)
            filtered = 0.5 * d_all[l * ROWS : (l + 1) * ROWS, :] + (0.5 / norm_total) * smooth
            projected, slope = project(filtered)
            designs.append(cells * projected)
            slopes.append(slope[:OWN] * cells[:OWN])
        for delta in range(4):
            value = fix(delta) * strip_density
            ahead = value if delta == 0 else roll(value, delta)
            behind = value if delta == 0 else roll(value, -delta)
            strip_smooth = strip_smooth + jnp.where(place >= 12 + delta, ahead, 0.0)
            strip_smooth = strip_smooth + jnp.where(place < 4 - delta, behind, 0.0)
        projected, _ = project(0.5 * strip_density + (0.5 / norm_total) * strip_smooth)
        strip_design = strip_cells * projected

        def invert(kind, design, channel):
            background = jnp.where(
                kind < 1.5,
                jnp.where(kind < 0.5, material_table[channel, 0], material_table[channel, 1]),
                jnp.where(kind < 2.5, material_table[channel, 2], material_table[channel, 3]),
            )
            return courant / (background + design * contrast[channel])

        for channel in range(3):
            si[channel * ROWS : (channel + 1) * ROWS, :] = invert(strip_material, strip_design, channel)
        for z in range(Z):
            kind = m_all[z * ROWS : (z + 1) * ROWS, :]
            for channel in range(3):
                p = channel * Z + z
                inverse[p * ROWS : (p + 1) * ROWS, :] = invert(kind, designs[z // 2], channel)
        gained[...] = jnp.zeros_like(gained)

        zero = jnp.zeros((ROWS, 128), jnp.float32)
        last, first = lane == 127, lane == 0

        def e_at(channel, z):
            p = channel * Z + z
            return e_all[p * ROWS : (p + 1) * ROWS, :]

        def h_at(channel, z):
            p = channel * Z + z
            return h_all[p * ROWS : (p + 1) * ROWS, :]

        def s_at(ref, channel):
            return ref[channel * ROWS : (channel + 1) * ROWS, :]

        def step(t, carry):
            sx, sy, sz = s_at(se, 0), s_at(se, 1), s_at(se, 2)
            for z in range(Z):
                ex, ey, ez = e_at(0, z), e_at(1, z), e_at(2, z)
                ex_up = e_at(0, z + 1) if z + 1 < Z else zero
                ey_up = e_at(1, z + 1) if z + 1 < Z else zero
                to = 115 - 16 * z
                dy_ez = jnp.where(last, roll(sz, to), roll(ez, -1)) - ez
                dy_ex = jnp.where(last, roll(sx, to), roll(ex, -1)) - ex
                dx_ez = roll_rows(ez, -1) - ez
                dx_ey = roll_rows(ey, -1) - ey
                for channel, curl in enumerate(
                    (dy_ez - (ey_up - ey), (ex_up - ex) - dx_ez, dx_ey - dy_ex)
                ):
                    p = channel * Z + z
                    h_all[p * ROWS : (p + 1) * ROWS, :] = h_at(channel, z) - courant * curl
            up_x = jnp.where(lane < 112, roll(sx, -16), 0.0)
            up_y = jnp.where(lane < 112, roll(sy, -16), 0.0)
            for channel, curl in enumerate(
                (
                    (roll(sz, -1) - sz) - (up_y - sy),
                    (up_x - sx) - (roll_rows(sz, -1) - sz),
                    (roll_rows(sy, -1) - sy) - (roll(sx, -1) - sx),
                )
            ):
                sh[channel * ROWS : (channel + 1) * ROWS, :] = s_at(sh, channel) - courant * curl
            sx, sy, sz = s_at(sh, 0), s_at(sh, 1), s_at(sh, 2)
            for z in range(Z):
                hx, hy, hz = h_at(0, z), h_at(1, z), h_at(2, z)
                hx_down = h_at(0, z - 1) if z > 0 else zero
                hy_down = h_at(1, z - 1) if z > 0 else zero
                to = -(16 * z + 3)
                dy_hz = hz - jnp.where(first, roll(sz, to), roll(hz, 1))
                dy_hx = hx - jnp.where(first, roll(sx, to), roll(hx, 1))
                dx_hz = hz - roll_rows(hz, 1)
                dx_hy = hy - roll_rows(hy, 1)
                total = jnp.zeros((OWN, 128), jnp.float32)
                for channel, curl in enumerate(
                    (dy_hz - (hy - hy_down), (hx - hx_down) - dx_hz, dx_hy - dy_hx)
                ):
                    p = channel * Z + z
                    value = e_at(channel, z) + inverse[p * ROWS : (p + 1) * ROWS, :] * curl
                    e_all[p * ROWS : (p + 1) * ROWS, :] = value
                    stored = forward[t, p].astype(jnp.float32)
                    total = total + contrast[channel] * (value[:OWN] * stored)
                l = z // 2
                gained[l * OWN : (l + 1) * OWN, :] = gained[l * OWN : (l + 1) * OWN, :] + total
            down_x = jnp.where(lane >= 16, roll(sx, 16), 0.0)
            down_y = jnp.where(lane >= 16, roll(sy, 16), 0.0)
            for channel, curl in enumerate(
                (
                    (sz - roll(sz, 1)) - (sy - down_y),
                    (sx - down_x) - (sz - roll_rows(sz, 1)),
                    (sy - roll_rows(sy, 1)) - (sx - roll(sx, 1)),
                )
            ):
                se[channel * ROWS : (channel + 1) * ROWS, :] = (
                    s_at(se, channel) + s_at(si, channel) * curl
                )
            return carry

        lax.fori_loop(0, STEPS, step, 0)
        for p in range(3 * Z):
            e_final[p * OWN : (p + 1) * OWN, :] = e_all[p * ROWS : p * ROWS + OWN, :]
            h_final[p * OWN : (p + 1) * OWN, :] = h_all[p * ROWS : p * ROWS + OWN, :]
        for l in range(DZ):
            gradient[l * OWN : (l + 1) * OWN, :] = slopes[l] * gained[l * OWN : (l + 1) * OWN, :]

    return kernel


def body(
    density, tile_mask, material, material_table, contrast, electric, magnetic, forward_fields
):
    devices = lax.axis_size("gy")
    count = density.shape[2] * devices
    reach = 4.0 * CY
    table, factors, spread = filter_constants(count, reach)
    e2 = electric.reshape(-1, 128)
    h2 = magnetic.reshape(-1, 128)
    d2 = density.reshape(-1, 128)
    m2 = material.reshape(-1, 128)
    f2 = forward_fields.reshape(STEPS, 3 * Z, OWN, 128)

    to_prev, to_next = call(
        pack_rows_kernel, [vmem(3 * SLOT, 128), vmem(3 * SLOT + 24, 128)],
        [e2, h2, d2, m2, tile_mask, spread],
    )
    from_prev = passed_along(to_next, "gx", 1)
    from_next = passed_along(to_prev, "gx", -1)
    e_all, h_all, m_all, d_all, c_all, local, pairs, left, right = call(
        own_kernel,
        [vmem(3 * Z * ROWS, 128), vmem(3 * Z * ROWS, 128), vmem(Z * ROWS, 128),
         vmem(DZ * ROWS, 128), vmem(ROWS, 128), vmem(DZ * ROWS, 256), vmem(4 * ROWS, 128),
         vmem(2 * ROWS, 128), vmem(2 * ROWS, 128)],
        [e2, h2, d2, m2, tile_mask, table, factors, spread],
    )
    e_all, h_all, m_all, d_all, c_all, pairs, left, right, sums = call(
        halo_kernel,
        [vmem(3 * Z * ROWS, 128), vmem(3 * Z * ROWS, 128), vmem(Z * ROWS, 128),
         vmem(DZ * ROWS, 128), vmem(ROWS, 128), vmem(4 * ROWS, 128),
         vmem(2 * ROWS, 128), vmem(2 * ROWS, 128), vmem(ROWS, 128)],
        [from_next, from_prev, e_all, h_all, m_all, d_all, c_all, pairs, left, right, factors],
        aliases={2: 0, 3: 1, 4: 2, 5: 3, 6: 4, 7: 5, 8: 6, 9: 7},
    )
    from_left = passed_along(right, "gy", 1)
    from_right = passed_along(left, "gy", -1)
    rest = [passed_along(sums, "gy", m) for m in range(2, devices - 1)]
    smem = pl.BlockSpec(memory_space=pltpu.SMEM)
    in_v = pl.BlockSpec(memory_space=pltpu.VMEM)
    operands = [from_right, from_left] + rest + [
        e_all, h_all, m_all, d_all, c_all, pairs, local, table, factors, f2,
    ]
    at = 4 + len(rest)
    outs = pl.pallas_call(
        step_kernel(count, reach, len(rest)),
        out_shape=[
            jax.ShapeDtypeStruct(e2.shape, jnp.float32),
            jax.ShapeDtypeStruct(h2.shape, jnp.float32),
            jax.ShapeDtypeStruct(d2.shape, jnp.float32),
            vmem(3 * Z * ROWS, 128),
            vmem(3 * Z * ROWS, 128),
        ],
        in_specs=[smem, smem] + [in_v] * len(operands),
        out_specs=[in_v] * 5,
        scratch_shapes=[
            vmem(3 * Z * ROWS, 128), vmem(3 * ROWS, 128), vmem(3 * ROWS, 128), vmem(3 * ROWS, 128),
            vmem(DZ * OWN, 128),
        ],
        input_output_aliases={at: 3, at + 1: 4},
        compiler_params=pltpu.CompilerParams(vmem_limit_bytes=32 * 1024 * 1024),
    )(material_table, contrast, *[in_vmem(x) for x in operands])
    return (
        outs[0].reshape(electric.shape), outs[1].reshape(magnetic.shape),
        outs[2].reshape(density.shape),
    )


def solution(mesh):
    return jax.shard_map(
        body,
        mesh=mesh,
        in_specs=(
            P(None, "gx", "gy"),
            P("gx", "gy"),
            P(None, "gx", "gy"),
            P(),
            P(),
            P(None, None, "gx", "gy"),
            P(None, None, "gx", "gy"),
            P(None, None, None, "gx", "gy"),
        ),
        out_specs=(P(None, None, "gx", "gy"), P(None, None, "gx", "gy"), P(None, "gx", "gy")),
        check_vma=False,
    )
```

```python
import math

import jax
import jax.numpy as jnp
import numpy as np
from jax import lax
from jax.experimental import pallas as pl
from jax.experimental.pallas import tpu as pltpu
from jax.sharding import PartitionSpec as P

CY = 128
Z = 8
DZ = 4
STEPS = 4
TILE = 8
MATS = 4

courant = 0.5
sharpness = 4.0
threshold = 0.5

ROWS = 24
OWN = 16
SLOT = 64
PLANES = 3 * Z

VM = pl.BlockSpec(memory_space=pltpu.VMEM)
ANY = pl.BlockSpec(memory_space=pl.ANY)


def vmem(*shape, dtype=jnp.float32):
    return pltpu.VMEM(shape, dtype)


def call(kernel, outs, ins, aliases=None, scratch=(), in_specs=None):
    space = pltpu.VMEM if in_specs is None else pltpu.HBM
    in_specs = in_specs or [VM] * len(ins)
    ins = [pltpu.with_memory_space_constraint(x, space) for x in ins]
    return pl.pallas_call(
        kernel,
        out_shape=outs,
        in_specs=in_specs,
        out_specs=[VM] * len(outs),
        scratch_shapes=list(scratch),
        input_output_aliases=aliases or {},
        compiler_params=pltpu.CompilerParams(vmem_limit_bytes=32 * 1024 * 1024),
    )(*ins)


def lanes(rows):
    return lax.broadcasted_iota(jnp.int32, (rows, 128), 1)


def roll(x, by):
    return pltpu.roll(x, by % x.shape[1], 1)


def roll_rows(x, by):
    return pltpu.roll(x, by % x.shape[0], 0)


def sent(x, axis, by):
    size = lax.axis_size(axis)
    return lax.ppermute(x, axis, [(i, (i + by) % size) for i in range(size)])


def weight(offset, count, reach):
    ahead = np.mod(offset, count).astype(np.float64)
    behind = np.mod(-offset, count).astype(np.float64)
    return np.exp(-ahead / reach) + np.exp(-behind / reach)


def filter_constants(count, reach):
    source = np.arange(CY)
    strip = np.concatenate([np.arange(-4, 4), np.arange(CY - 4, CY + 4)])
    targets = np.concatenate([source, np.tile(strip, Z)])
    table = weight(targets[None, :] - source[:, None], count, reach)
    rows = np.zeros((8, 256))
    rows[0] = np.exp(-targets / reach)
    rows[1] = np.exp(targets / reach)
    rows[2, :CY] = np.exp(source / reach)
    rows[3, :CY] = np.exp(-source / reach)
    return np.concatenate([table, rows], 0).astype(np.float32)


def edge_window(planes):
    rows = planes[0].shape[0]
    lane = lanes(rows)
    window = (lane < 4) | (lane >= 124)
    gathered = planes[7]
    for z in range(6, -1, -1):
        gathered = jnp.where(window, planes[z], roll(gathered, 16))
    return gathered


def edge_pairs(groups):
    lane = lanes(groups[0][0].shape[0])
    first = (lane & 15) < 8
    found = [edge_window(planes) for planes in groups]
    return [
        jnp.where(first, roll(found[2 * i], 4), roll(found[2 * i + 1], 12)) for i in range(4)
    ]


def edge_messages(pairs):
    quarter = (lanes(pairs[0].shape[0]) >> 2) & 3

    def pick(a, b, c, d):
        return jnp.where(quarter < 2, jnp.where(quarter == 0, a, b), jnp.where(quarter == 2, c, d))

    left, right = [], []
    for one, two in ((pairs[0], pairs[1]), (pairs[2], pairs[3])):
        left.append(pick(roll(one, -4), roll(one, -8), roll(two, 4), two))
        right.append(pick(one, roll(one, -4), roll(two, 8), roll(two, 4)))
    return left, right


def density_planes(layers, cells, rising, falling):
    place = lanes(cells.shape[0]) & 3
    planes = []
    for layer in layers:
        up = jnp.sum(layer * rising, axis=1, keepdims=True)
        down = jnp.sum(layer * falling, axis=1, keepdims=True)
        planes += [layer, jnp.where(place == 0, up, jnp.where(place == 1, down, cells))]
    return planes


def pack_kernel(
    electric, magnetic, density, material, mask, table_in, mtable_in, contrast_in,
    to_prev, to_next, e_all, h_all, d_all, m_own, c_all, table, mtable, contrast,
    mask_v, sems,
):
    copies = []
    for i, (source, target) in enumerate(
        (
            (electric, e_all.reshape(PLANES, ROWS, 128).at[:, 0:OWN, :]),
            (magnetic, h_all.reshape(PLANES, ROWS, 128).at[:, 0:OWN, :]),
            (density, d_all.reshape(DZ, ROWS, 128).at[:, 0:OWN, :]),
            (material, m_own),
            (mask, mask_v),
            (table_in, table),
            (mtable_in, mtable),
            (contrast_in, contrast),
        )
    ):
        copy = pltpu.make_async_copy(source, target, sems.at[i])
        copy.start()
        copies.append(copy)
    for copy in copies:
        copy.wait()

    cells = cell_rows(mask_v[...])
    c_all[0:TILE, :] = jnp.broadcast_to(cells[0:1], (TILE, 128))
    c_all[TILE:OWN, :] = jnp.broadcast_to(cells[1:2], (TILE, 128))

    def e(channel, row):
        return e_all[pl.ds(channel * Z * ROWS + row, Z, stride=ROWS), :]

    def h(channel, row):
        return h_all[pl.ds(channel * Z * ROWS + row, Z, stride=ROWS), :]

    def ahead_part(row):
        part_y = h(1, row) + courant * (e(2, row + 1) - e(2, row))
        part_z = h(2, row) - courant * (e(1, row + 1) - e(1, row))
        return part_y, part_z

    for out, first, mask_row in ((to_next, OWN - 3, 1), (to_prev, 0, 0)):
        for slot in range(3):
            row, at = first + slot, slot * SLOT
            for channel in range(3):
                out[at + 8 * channel : at + 8 * channel + 8, :] = e(channel, row)
                out[at + 24 + 8 * channel : at + 32 + 8 * channel, :] = h(channel, row)
            out[at + 48 : at + 56, :] = m_own[pl.ds(row, Z, stride=OWN), :].astype(jnp.float32)
            out[at + 56 : at + 60, :] = d_all[pl.ds(row, DZ, stride=ROWS), :]
            out[at + 60 : at + 64, :] = jnp.broadcast_to(cells[mask_row : mask_row + 1], (4, 128))
    part_y, part_z = ahead_part(2)
    to_prev[2 * SLOT + 32 : 2 * SLOT + 40, :] = part_y
    to_prev[2 * SLOT + 40 : 2 * SLOT + 48, :] = part_z
    part_y, part_z = ahead_part(OWN - 4)
    to_next[3 * SLOT : 3 * SLOT + 8, :] = e(0, OWN - 4)
    to_next[3 * SLOT + 8 : 3 * SLOT + 16, :] = part_y
    to_next[3 * SLOT + 16 : 3 * SLOT + 24, :] = part_z


def own_kernel(
    e_all, h_all, d_all, m_own, c_all, table,
    pairs_out, left_out, right_out, m_all, local,
):
    groups = []
    for ref in (e_all, h_all):
        for channel in range(3):
            groups.append(
                [ref[(channel * Z + z) * ROWS : (channel * Z + z) * ROWS + OWN, :] for z in range(Z)]
            )
    planes = []
    for z in range(Z):
        plane = m_own[z * OWN : (z + 1) * OWN, :].astype(jnp.float32)
        m_all[z * ROWS : z * ROWS + OWN, :] = plane
        planes.append(plane)
    groups.append(planes)
    layers = [d_all[l * ROWS : l * ROWS + OWN, :] for l in range(DZ)]
    groups.append(
        density_planes(layers, c_all[0:OWN, :], table[130:131, 0:128], table[131:132, 0:128])
    )
    pairs = edge_pairs(groups)
    left, right = edge_messages(pairs)
    for i in range(4):
        pairs_out[i * ROWS : i * ROWS + OWN, :] = pairs[i]
    for i in range(2):
        left_out[i * ROWS : i * ROWS + OWN, :] = left[i]
        right_out[i * ROWS : i * ROWS + OWN, :] = right[i]
    smooth = jnp.dot(
        jnp.concatenate(layers, 0), table[0:128, :], precision=lax.Precision.HIGHEST,
        preferred_element_type=jnp.float32,
    )
    for l in range(DZ):
        local[l * ROWS : l * ROWS + OWN, :] = smooth[l * OWN : (l + 1) * OWN]


def halo_kernel(
    from_next, from_prev, e_in, h_in, d_in, c_in, m_in, pairs_in, left_in, right_in, table,
    e_all, h_all, d_all, c_all, m_all, pairs_out, left_out, right_out, sums_out,
):
    for got, first in ((from_next, 16), (from_prev, 21)):
        for slot in range(3):
            at, row = slot * SLOT, first + slot
            for channel in range(3):
                where = pl.ds(channel * Z * ROWS + row, Z, stride=ROWS)
                e_all[where, :] = got[at + 8 * channel : at + 8 * channel + 8, :]
                h_all[where, :] = got[at + 24 + 8 * channel : at + 32 + 8 * channel, :]
            m_all[pl.ds(row, Z, stride=ROWS), :] = got[at + 48 : at + 56, :]
            d_all[pl.ds(row, DZ, stride=ROWS), :] = got[at + 56 : at + 60, :]
            c_all[row : row + 1, :] = got[at + 60 : at + 61, :]
    zeros = jnp.zeros((Z, 128), jnp.float32)
    for channel in range(3):
        at = channel * Z * ROWS
        e_all[pl.ds(at + 19, Z, stride=ROWS), :] = from_next[
            2 * SLOT + 8 * channel : 2 * SLOT + 8 * channel + 8, :
        ]
        h_all[pl.ds(at + 19, Z, stride=ROWS), :] = zeros
        if channel > 0:
            e_all[pl.ds(at + 20, Z, stride=ROWS), :] = from_prev[8 * channel : 8 * channel + 8, :]
            h_all[pl.ds(at + 20, Z, stride=ROWS), :] = from_prev[
                3 * SLOT + 8 * channel : 3 * SLOT + 8 * channel + 8, :
            ]
        else:
            e_all[pl.ds(at + 20, Z, stride=ROWS), :] = from_prev[3 * SLOT : 3 * SLOT + 8, :]
            h_all[pl.ds(at + 20, Z, stride=ROWS), :] = zeros
    for row in (19, 20):
        m_all[pl.ds(row, Z, stride=ROWS), :] = zeros
        d_all[pl.ds(row, DZ, stride=ROWS), :] = zeros[0:DZ]
        c_all[row : row + 1, :] = zeros[0:1]

    groups = []
    for target in (e_all, h_all):
        for channel in range(3):
            groups.append(
                [target[(channel * Z + z) * ROWS + OWN : (channel * Z + z + 1) * ROWS, :] for z in range(Z)]
            )
    groups.append([m_all[z * ROWS + OWN : (z + 1) * ROWS, :] for z in range(Z)])
    layers = [d_all[l * ROWS + OWN : (l + 1) * ROWS, :] for l in range(DZ)]
    groups.append(
        density_planes(layers, c_all[OWN:ROWS, :], table[130:131, 0:128], table[131:132, 0:128])
    )
    pairs = edge_pairs(groups)
    left, right = edge_messages(pairs)
    for i in range(4):
        pairs_out[i * ROWS + OWN : (i + 1) * ROWS, :] = pairs[i]
    for i in range(2):
        left_out[i * ROWS + OWN : (i + 1) * ROWS, :] = left[i]
        right_out[i * ROWS + OWN : (i + 1) * ROWS, :] = right[i]
    sums_out[0:OWN, :] = left_in[ROWS : ROWS + OWN, :]
    sums_out[OWN:ROWS, :] = left[1]


def background_kernel(m_all, d_all, mtable, table, local_in, background, local):
    smooth = jnp.dot(
        jnp.concatenate([d_all[l * ROWS + OWN : (l + 1) * ROWS, :] for l in range(DZ)], 0),
        table[0:128, :], precision=lax.Precision.HIGHEST, preferred_element_type=jnp.float32,
    )
    for l in range(DZ):
        local[l * ROWS + OWN : (l + 1) * ROWS, :] = smooth[l * 8 : (l + 1) * 8]
    entries = mtable[...]
    for z in range(Z):
        kind = m_all[z * ROWS : (z + 1) * ROWS, :]
        for channel in range(3):
            p = channel * Z + z
            background[p * ROWS : (p + 1) * ROWS, :] = looked_up(kind, entries, channel)


def looked_up(kind, entries, channel):
    one = [entries[channel : channel + 1, i : i + 1] for i in range(MATS)]
    return jnp.where(
        kind < 1.5, jnp.where(kind < 0.5, one[0], one[1]), jnp.where(kind < 2.5, one[2], one[3])
    )


def cell_rows(mask):
    spread = lax.broadcasted_iota(jnp.int32, (mask.shape[1], 128), 0) == (
        lanes(mask.shape[1]) // TILE
    )
    return jnp.dot(
        mask.astype(jnp.float32), spread.astype(jnp.float32), preferred_element_type=jnp.float32
    )


def project(values):
    base = math.tanh(sharpness * threshold)
    bottom = base + math.tanh(sharpness * (1.0 - threshold))
    level = jnp.tanh(sharpness * (values - threshold))
    return (base + level) * (1.0 / bottom), (sharpness / bottom) * (1.0 - level * level)


def step_kernel(count, reach, others):
    devices = count // CY
    norm_total = 2.0 * float(np.sum(np.exp(-np.arange(count) / reach)))

    def factor(m):
        return math.exp(-CY * m / reach), math.exp(-(count - CY * m) / reach)

    def fix(delta):
        if delta == 0:
            return 1.0 - math.exp(-count / reach)
        return (
            math.exp(-delta / reach) + math.exp(-(count - delta) / reach)
            - math.exp(-(count + delta) / reach) - math.exp(delta / reach)
        )

    def kernel(*refs):
        from_right, from_left = refs[:2]
        rest = refs[2 : 2 + others]
        (e_in, h_in, d_all, c_all, background, pairs, local, table, mtable, contrast_in, forward,
         e_final, h_final, gradient, e_all, h_all, inverse, se, sh, si, gained) = refs[2 + others :]
        entries = mtable[...]
        contrast = [contrast_in[0:1, c : c + 1] for c in range(3)]
        lane = lanes(ROWS)
        place = lane & 15
        odd = ((lane >> 4) & 1) == 1
        layer_of = lane >> 5
        part = place >> 2

        got_left = [from_left[i * ROWS : (i + 1) * ROWS, :] for i in range(2)]
        got_right = [from_right[i * ROWS : (i + 1) * ROWS, :] for i in range(2)]

        def strip(index):
            tile, q = index // 4, index % 4
            pair = pairs[(index // 2) * ROWS : (index // 2 + 1) * ROWS, :]
            if index % 2 == 0:
                own_l, own_r = pair, roll(pair, 8)
            else:
                own_l, own_r = roll(pair, -8), pair
            outer = jnp.where(part == 0, roll(got_left[tile], -4 * q), roll(got_right[tile], 12 - 4 * q))
            return jnp.where(part == 1, own_l, jnp.where(part == 2, own_r, outer))

        for channel in range(3):
            se[channel * ROWS : (channel + 1) * ROWS, :] = strip(channel)
            sh[channel * ROWS : (channel + 1) * ROWS, :] = strip(3 + channel)
        strip_material = strip(6)
        raw = strip(7)
        strip_density = jnp.where(odd, roll(raw, 16), raw)
        marks = jnp.where(odd, raw, roll(raw, -16))
        strip_cells = jnp.where((place & 2) == 2, marks, roll(marks, -2))

        def lane_factor(m):
            up, down = factor(m)
            return jnp.where(place == 12, up, down)

        sums = lane_factor(1) * got_left[1] + lane_factor(devices - 1) * got_right[1]
        for i, other in enumerate(rest):
            sums = sums + lane_factor(2 + i) * other[...]
        strip_smooth = jnp.zeros((ROWS, 128), jnp.float32)
        designs, slopes = [], []
        cells = c_all[...]
        for l in range(DZ):
            at = (2 * l + 1) * 16 + 12
            up = jnp.broadcast_to(sums[:, at : at + 1], (ROWS, 128))
            down = jnp.broadcast_to(sums[:, at + 1 : at + 2], (ROWS, 128))
            both = local[l * ROWS : (l + 1) * ROWS, :]
            smooth = both[:, :128] + table[128:129, :128] * up + table[129:130, :128] * down
            far = both[:, 128:] + table[128:129, 128:] * up + table[129:130, 128:] * down
            strip_smooth = jnp.where(layer_of == l, far, strip_smooth)
            filtered = 0.5 * d_all[l * ROWS : (l + 1) * ROWS, :] + (0.5 / norm_total) * smooth
            projected, slope = project(filtered)
            designs.append(cells * projected)
            slopes.append(slope[:OWN] * cells[:OWN])
        for delta in range(4):
            value = fix(delta) * strip_density
            ahead = value if delta == 0 else roll(value, delta)
            behind = value if delta == 0 else roll(value, -delta)
            strip_smooth = strip_smooth + jnp.where(place >= 12 + delta, ahead, 0.0)
            strip_smooth = strip_smooth + jnp.where(place < 4 - delta, behind, 0.0)
        projected, _ = project(0.5 * strip_density + (0.5 / norm_total) * strip_smooth)
        strip_design = strip_cells * projected

        for channel in range(3):
            own = looked_up(strip_material, entries, channel)
            si[channel * ROWS : (channel + 1) * ROWS, :] = courant / (
                own + strip_design * contrast[channel]
            )
        for z in range(Z):
            for channel in range(3):
                p = channel * Z + z
                inverse[p * ROWS : (p + 1) * ROWS, :] = courant / (
                    background[p * ROWS : (p + 1) * ROWS, :] + designs[z // 2] * contrast[channel]
                )
        gained[...] = jnp.zeros_like(gained)

        zero = jnp.zeros((ROWS, 128), jnp.float32)
        last, first = lane == 127, lane == 0

        def e_at(channel, z):
            p = channel * Z + z
            return e_all[p * ROWS : (p + 1) * ROWS, :]

        def h_at(channel, z):
            p = channel * Z + z
            return h_all[p * ROWS : (p + 1) * ROWS, :]

        def s_at(ref, channel):
            return ref[channel * ROWS : (channel + 1) * ROWS, :]

        def step(t, carry):
            sx, sy, sz = s_at(se, 0), s_at(se, 1), s_at(se, 2)
            for z in range(Z):
                ex, ey, ez = e_at(0, z), e_at(1, z), e_at(2, z)
                ex_up = e_at(0, z + 1) if z + 1 < Z else zero
                ey_up = e_at(1, z + 1) if z + 1 < Z else zero
                to = 115 - 16 * z
                dy_ez = jnp.where(last, roll(sz, to), roll(ez, -1)) - ez
                dy_ex = jnp.where(last, roll(sx, to), roll(ex, -1)) - ex
                dx_ez = roll_rows(ez, -1) - ez
                dx_ey = roll_rows(ey, -1) - ey
                for channel, curl in enumerate(
                    (dy_ez - (ey_up - ey), (ex_up - ex) - dx_ez, dx_ey - dy_ex)
                ):
                    p = channel * Z + z
                    h_all[p * ROWS : (p + 1) * ROWS, :] = h_at(channel, z) - courant * curl
            up_x = jnp.where(lane < 112, roll(sx, -16), 0.0)
            up_y = jnp.where(lane < 112, roll(sy, -16), 0.0)
            for channel, curl in enumerate(
                (
                    (roll(sz, -1) - sz) - (up_y - sy),
                    (up_x - sx) - (roll_rows(sz, -1) - sz),
                    (roll_rows(sy, -1) - sy) - (roll(sx, -1) - sx),
                )
            ):
                sh[channel * ROWS : (channel + 1) * ROWS, :] = s_at(sh, channel) - courant * curl
            sx, sy, sz = s_at(sh, 0), s_at(sh, 1), s_at(sh, 2)
            for z in range(Z):
                hx, hy, hz = h_at(0, z), h_at(1, z), h_at(2, z)
                hx_down = h_at(0, z - 1) if z > 0 else zero
                hy_down = h_at(1, z - 1) if z > 0 else zero
                to = -(16 * z + 3)
                dy_hz = hz - jnp.where(first, roll(sz, to), roll(hz, 1))
                dy_hx = hx - jnp.where(first, roll(sx, to), roll(hx, 1))
                dx_hz = hz - roll_rows(hz, 1)
                dx_hy = hy - roll_rows(hy, 1)
                total = jnp.zeros((OWN, 128), jnp.float32)
                for channel, curl in enumerate(
                    (dy_hz - (hy - hy_down), (hx - hx_down) - dx_hz, dx_hy - dy_hx)
                ):
                    p = channel * Z + z
                    value = e_at(channel, z) + inverse[p * ROWS : (p + 1) * ROWS, :] * curl
                    e_all[p * ROWS : (p + 1) * ROWS, :] = value
                    stored = forward[t, p].astype(jnp.float32)
                    total = total + contrast[channel] * (value[:OWN] * stored)
                l = z // 2
                gained[l * OWN : (l + 1) * OWN, :] = gained[l * OWN : (l + 1) * OWN, :] + total
            down_x = jnp.where(lane >= 16, roll(sx, 16), 0.0)
            down_y = jnp.where(lane >= 16, roll(sy, 16), 0.0)
            for channel, curl in enumerate(
                (
                    (sz - roll(sz, 1)) - (sy - down_y),
                    (sx - down_x) - (sz - roll_rows(sz, 1)),
                    (sy - roll_rows(sy, 1)) - (sx - roll(sx, 1)),
                )
            ):
                se[channel * ROWS : (channel + 1) * ROWS, :] = (
                    s_at(se, channel) + s_at(si, channel) * curl
                )
            return carry

        lax.fori_loop(0, STEPS, step, 0)
        for p in range(3 * Z):
            e_final[p * OWN : (p + 1) * OWN, :] = e_all[p * ROWS : p * ROWS + OWN, :]
            h_final[p * OWN : (p + 1) * OWN, :] = h_all[p * ROWS : p * ROWS + OWN, :]
        for l in range(DZ):
            gradient[l * OWN : (l + 1) * OWN, :] = slopes[l] * gained[l * OWN : (l + 1) * OWN, :]

    return kernel


def body(
    density, tile_mask, material, material_table, contrast, electric, magnetic, forward_fields
):
    devices = lax.axis_size("gy")
    count = density.shape[2] * devices
    reach = 4.0 * CY
    constants = filter_constants(count, reach)

    to_prev, to_next, e_all, h_all, d_all, m_own, c_all, table, mtable, contrasts = call(
        pack_kernel,
        [vmem(3 * SLOT, 128), vmem(3 * SLOT + 24, 128),
         vmem(PLANES * ROWS, 128), vmem(PLANES * ROWS, 128), vmem(DZ * ROWS, 128),
         vmem(Z * OWN, 128, dtype=jnp.int32), vmem(ROWS, 128), vmem(*constants.shape),
         vmem(3, MATS), vmem(1, 3)],
        [electric.reshape(PLANES, OWN, 128), magnetic.reshape(PLANES, OWN, 128), density,
         material.reshape(Z * OWN, 128), tile_mask, constants, material_table,
         contrast.reshape(1, 3)],
        scratch=[vmem(*tile_mask.shape, dtype=jnp.int32), pltpu.SemaphoreType.DMA((8,))],
        in_specs=[ANY] * 8,
    )
    from_prev = sent(to_next, "gx", 1)
    from_next = sent(to_prev, "gx", -1)
    pairs, left, right, m_all, local = call(
        own_kernel,
        [vmem(4 * ROWS, 128), vmem(2 * ROWS, 128), vmem(2 * ROWS, 128), vmem(Z * ROWS, 128),
         vmem(DZ * ROWS, 256)],
        [e_all, h_all, d_all, m_own, c_all, table],
    )
    e_all, h_all, d_all, c_all, m_all, pairs, left, right, sums = call(
        halo_kernel,
        [vmem(PLANES * ROWS, 128), vmem(PLANES * ROWS, 128), vmem(DZ * ROWS, 128),
         vmem(ROWS, 128), vmem(Z * ROWS, 128), vmem(4 * ROWS, 128),
         vmem(2 * ROWS, 128), vmem(2 * ROWS, 128), vmem(ROWS, 128)],
        [from_next, from_prev, e_all, h_all, d_all, c_all, m_all, pairs, left, right, table],
        aliases={2: 0, 3: 1, 4: 2, 5: 3, 6: 4, 7: 5, 8: 6, 9: 7},
    )
    from_left = sent(right, "gy", 1)
    from_right = sent(left, "gy", -1)
    rest = [sent(sums, "gy", m) for m in range(2, devices - 1)]
    background, local = call(
        background_kernel, [vmem(PLANES * ROWS, 128), vmem(DZ * ROWS, 256)],
        [m_all, d_all, mtable, table, local], aliases={4: 1},
    )
    at = 2 + len(rest)
    outs = call(
        step_kernel(count, reach, len(rest)),
        [jax.ShapeDtypeStruct((PLANES * OWN, 128), jnp.float32),
         jax.ShapeDtypeStruct((PLANES * OWN, 128), jnp.float32),
         jax.ShapeDtypeStruct((DZ * OWN, 128), jnp.float32),
         vmem(PLANES * ROWS, 128), vmem(PLANES * ROWS, 128)],
        [from_right, from_left] + rest + [
            e_all, h_all, d_all, c_all, background, pairs, local, table,
            mtable, contrasts, forward_fields.reshape(STEPS, PLANES, OWN, 128),
        ],
        aliases={at: 3, at + 1: 4},
        scratch=[vmem(PLANES * ROWS, 128), vmem(3 * ROWS, 128), vmem(3 * ROWS, 128),
                 vmem(3 * ROWS, 128), vmem(DZ * OWN, 128)],
    )
    return (
        outs[0].reshape(electric.shape), outs[1].reshape(magnetic.shape),
        outs[2].reshape(density.shape),
    )


def solution(mesh):
    return jax.shard_map(
        body,
        mesh=mesh,
        in_specs=(
            P(None, "gx", "gy"),
            P("gx", "gy"),
            P(None, "gx", "gy"),
            P(),
            P(),
            P(None, None, "gx", "gy"),
            P(None, None, "gx", "gy"),
            P(None, None, None, "gx", "gy"),
        ),
        out_specs=(P(None, None, "gx", "gy"), P(None, None, "gx", "gy"), P(None, "gx", "gy")),
        check_vma=False,
    )
```

```python
import math

import jax
import jax.numpy as jnp
import numpy as np
from jax import lax
from jax.experimental import pallas as pl
from jax.experimental.pallas import tpu as pltpu
from jax.sharding import PartitionSpec as P

CY = 128
Z = 8
DZ = 4
STEPS = 4
TILE = 8
MATS = 4

courant = 0.5
sharpness = 4.0
threshold = 0.5

ROWS = 24
OWN = 16
SLOT = 48
KINDS = 3 * SLOT
LAYERS = KINDS + 24
EXTRA = LAYERS + 16
PLANES = 3 * Z

VM = pl.BlockSpec(memory_space=pltpu.VMEM)
ANY = pl.BlockSpec(memory_space=pl.ANY)


def vmem(*shape, dtype=jnp.float32):
    return pltpu.VMEM(shape, dtype)


def call(kernel, outs, ins, aliases=None, scratch=(), in_specs=None):
    space = pltpu.VMEM if in_specs is None else pltpu.HBM
    in_specs = in_specs or [VM] * len(ins)
    ins = [pltpu.with_memory_space_constraint(x, space) for x in ins]
    return pl.pallas_call(
        kernel,
        out_shape=outs,
        in_specs=in_specs,
        out_specs=[VM] * len(outs),
        scratch_shapes=list(scratch),
        input_output_aliases=aliases or {},
        compiler_params=pltpu.CompilerParams(vmem_limit_bytes=32 * 1024 * 1024),
    )(*ins)


def lanes(rows):
    return lax.broadcasted_iota(jnp.int32, (rows, 128), 1)


def roll(x, by):
    return pltpu.roll(x, by % x.shape[1], 1)


def roll_rows(x, by):
    return pltpu.roll(x, by % x.shape[0], 0)


def sent(x, axis, by):
    size = lax.axis_size(axis)
    return lax.ppermute(x, axis, [(i, (i + by) % size) for i in range(size)])


def weight(offset, count, reach):
    ahead = np.mod(offset, count).astype(np.float64)
    behind = np.mod(-offset, count).astype(np.float64)
    return np.exp(-ahead / reach) + np.exp(-behind / reach)


def filter_constants(count, reach):
    source = np.arange(CY)
    strip = np.concatenate([np.arange(-4, 4), np.arange(CY - 4, CY + 4)])
    targets = np.concatenate([source, np.tile(strip, Z)])
    table = weight(targets[None, :] - source[:, None], count, reach)
    rows = np.zeros((8, 256))
    rows[0] = np.exp(-targets / reach)
    rows[1] = np.exp(targets / reach)
    rows[2, :CY] = np.exp(source / reach)
    rows[3, :CY] = np.exp(-source / reach)
    return np.concatenate([table, rows], 0).astype(np.float32)


def edge_window(planes):
    lane = lanes(planes[0].shape[0])
    width, by = 8, 16
    while len(planes) > 1:
        kept = ((lane + 4) & 127) < width
        planes = [
            jnp.where(kept, planes[i], roll(planes[i + 1], by)) for i in range(0, len(planes), 2)
        ]
        width, by = width + by, 2 * by
    return planes[0]


def edge_pairs(groups):
    lane = lanes(groups[0][0].shape[0])
    first = (lane & 15) < 8
    found = [edge_window(planes) for planes in groups]
    return [
        jnp.where(first, roll(found[2 * i], 4), roll(found[2 * i + 1], 12)) for i in range(4)
    ]


def edge_messages(pairs):
    quarter = (lanes(pairs[0].shape[0]) >> 2) & 3

    def pick(a, b, c, d):
        return jnp.where(quarter < 2, jnp.where(quarter == 0, a, b), jnp.where(quarter == 2, c, d))

    left, right = [], []
    for one, two in ((pairs[0], pairs[1]), (pairs[2], pairs[3])):
        left.append(pick(roll(one, -4), roll(one, -8), roll(two, 4), two))
        right.append(pick(one, roll(one, -4), roll(two, 8), roll(two, 4)))
    return left, right


def density_planes(layers, cells, rising, falling):
    place = lanes(cells.shape[0]) & 3
    planes = []
    for layer in layers:
        up = jnp.sum(layer * rising, axis=1, keepdims=True)
        down = jnp.sum(layer * falling, axis=1, keepdims=True)
        planes += [layer, jnp.where(place == 0, up, jnp.where(place == 1, down, cells))]
    return planes


def pack_kernel(
    electric, magnetic, density, material, mask, table_in, mtable_in, contrast_in,
    to_prev, to_next, e_own, h_own, d_own, m_own, c_all, table, mtable, contrast,
    mask_v, sems,
):
    copies = []
    moved = [
        (mask, mask_v), (electric, e_own), (magnetic, h_own), (density, d_own), (material, m_own),
    ]
    needed = len(moved)
    moved += [(table_in, table), (mtable_in, mtable), (contrast_in, contrast)]
    for i, (source, target) in enumerate(moved):
        copy = pltpu.make_async_copy(source, target, sems.at[i])
        copy.start()
        copies.append(copy)
    for copy in copies[:needed]:
        copy.wait()

    cells = cell_rows(mask_v[...])
    c_all[0:TILE, :] = jnp.broadcast_to(cells[0:1], (TILE, 128))
    c_all[TILE:OWN, :] = jnp.broadcast_to(cells[1:2], (TILE, 128))

    def e(channel, row):
        return e_own[pl.ds(channel * Z * OWN + row, Z, stride=OWN), :]

    def h(channel, row):
        return h_own[pl.ds(channel * Z * OWN + row, Z, stride=OWN), :]

    def ahead_part(row):
        part_y = h(1, row) + courant * (e(2, row + 1) - e(2, row))
        part_z = h(2, row) - courant * (e(1, row + 1) - e(1, row))
        return part_y, part_z

    for out, first, mask_row in ((to_next, OWN - 3, 1), (to_prev, 0, 0)):
        for slot in range(3):
            row, at = first + slot, slot * SLOT
            for channel in range(3):
                out[at + 8 * channel : at + 8 * channel + 8, :] = e(channel, row)
                out[at + 24 + 8 * channel : at + 32 + 8 * channel, :] = h(channel, row)
            out[KINDS + 8 * slot : KINDS + 8 * slot + 8, :] = (
                m_own[pl.ds(row, Z, stride=OWN), :].astype(jnp.float32)
            )
            out[LAYERS + 4 * slot : LAYERS + 4 * slot + 4, :] = (
                d_own[pl.ds(row, DZ, stride=OWN), :]
            )
        out[LAYERS + 12 : LAYERS + 16, :] = jnp.broadcast_to(
            cells[mask_row : mask_row + 1], (4, 128)
        )
    part_y, part_z = ahead_part(2)
    to_prev[2 * SLOT + 32 : 2 * SLOT + 40, :] = part_y
    to_prev[2 * SLOT + 40 : 2 * SLOT + 48, :] = part_z
    part_y, part_z = ahead_part(OWN - 4)
    to_next[EXTRA : EXTRA + 8, :] = e(0, OWN - 4)
    to_next[EXTRA + 8 : EXTRA + 16, :] = part_y
    to_next[EXTRA + 16 : EXTRA + 24, :] = part_z
    for copy in copies[needed:]:
        copy.wait()


def own_kernel(
    e_own, h_own, d_own, m_own, c_own, table,
    e_all, h_all, d_all, c_all, pairs_out, left_out, right_out, m_all, local,
):
    c_all[0:OWN, :] = c_own[...]
    groups = []
    for source, target in ((e_own, e_all), (h_own, h_all)):
        for channel in range(3):
            planes = []
            for z in range(Z):
                p = channel * Z + z
                plane = source[p * OWN : (p + 1) * OWN, :]
                target[p * ROWS : p * ROWS + OWN, :] = plane
                planes.append(plane)
            groups.append(planes)
    planes = []
    for z in range(Z):
        plane = m_own[z * OWN : (z + 1) * OWN, :].astype(jnp.float32)
        m_all[z * ROWS : z * ROWS + OWN, :] = plane
        planes.append(plane)
    groups.append(planes)
    layers = []
    for l in range(DZ):
        layers.append(d_own[l * OWN : (l + 1) * OWN, :])
        d_all[l * ROWS : l * ROWS + OWN, :] = layers[l]
    groups.append(
        density_planes(layers, c_own[...], table[130:131, 0:128], table[131:132, 0:128])
    )
    pairs = edge_pairs(groups)
    left, right = edge_messages(pairs)
    for i in range(4):
        pairs_out[i * ROWS : i * ROWS + OWN, :] = pairs[i]
    for i in range(2):
        left_out[i * ROWS : i * ROWS + OWN, :] = left[i]
        right_out[i * ROWS : i * ROWS + OWN, :] = right[i]
    smooth = jnp.dot(
        jnp.concatenate(layers, 0), table[0:128, :], precision=lax.Precision.HIGHEST,
        preferred_element_type=jnp.float32,
    )
    for l in range(DZ):
        local[l * ROWS : l * ROWS + OWN, :] = smooth[l * OWN : (l + 1) * OWN]


def halo_kernel(
    from_next, from_prev, e_in, h_in, d_in, c_in, m_in, pairs_in, left_in, right_in, table,
    e_all, h_all, d_all, c_all, m_all, pairs_out, left_out, right_out, sums_out,
):
    for got, first in ((from_next, 16), (from_prev, 21)):
        for slot in range(3):
            at, row = slot * SLOT, first + slot
            for channel in range(3):
                where = pl.ds(channel * Z * ROWS + row, Z, stride=ROWS)
                e_all[where, :] = got[at + 8 * channel : at + 8 * channel + 8, :]
                h_all[where, :] = got[at + 24 + 8 * channel : at + 32 + 8 * channel, :]
            m_all[pl.ds(row, Z, stride=ROWS), :] = got[KINDS + 8 * slot : KINDS + 8 * slot + 8, :]
            d_all[pl.ds(row, DZ, stride=ROWS), :] = got[LAYERS + 4 * slot : LAYERS + 4 * slot + 4, :]
            c_all[row : row + 1, :] = got[LAYERS + 12 : LAYERS + 13, :]
    zeros = jnp.zeros((Z, 128), jnp.float32)
    for channel in range(3):
        at = channel * Z * ROWS
        e_all[pl.ds(at + 19, Z, stride=ROWS), :] = from_next[
            2 * SLOT + 8 * channel : 2 * SLOT + 8 * channel + 8, :
        ]
        h_all[pl.ds(at + 19, Z, stride=ROWS), :] = zeros
        if channel > 0:
            e_all[pl.ds(at + 20, Z, stride=ROWS), :] = from_prev[8 * channel : 8 * channel + 8, :]
            h_all[pl.ds(at + 20, Z, stride=ROWS), :] = from_prev[
                EXTRA + 8 * channel : EXTRA + 8 * channel + 8, :
            ]
        else:
            e_all[pl.ds(at + 20, Z, stride=ROWS), :] = from_prev[EXTRA : EXTRA + 8, :]
            h_all[pl.ds(at + 20, Z, stride=ROWS), :] = zeros
    for row in (19, 20):
        m_all[pl.ds(row, Z, stride=ROWS), :] = zeros
        d_all[pl.ds(row, DZ, stride=ROWS), :] = zeros[0:DZ]
        c_all[row : row + 1, :] = zeros[0:1]

    groups = []
    for target in (e_all, h_all):
        for channel in range(3):
            groups.append(
                [target[(channel * Z + z) * ROWS + OWN : (channel * Z + z + 1) * ROWS, :] for z in range(Z)]
            )
    groups.append([m_all[z * ROWS + OWN : (z + 1) * ROWS, :] for z in range(Z)])
    layers = [d_all[l * ROWS + OWN : (l + 1) * ROWS, :] for l in range(DZ)]
    groups.append(
        density_planes(layers, c_all[OWN:ROWS, :], table[130:131, 0:128], table[131:132, 0:128])
    )
    pairs = edge_pairs(groups)
    left, right = edge_messages(pairs)
    for i in range(4):
        pairs_out[i * ROWS + OWN : (i + 1) * ROWS, :] = pairs[i]
    for i in range(2):
        left_out[i * ROWS + OWN : (i + 1) * ROWS, :] = left[i]
        right_out[i * ROWS + OWN : (i + 1) * ROWS, :] = right[i]
    place = lanes(8) & 15
    packed = left[1]
    packed = jnp.where(place < 12, roll(left_in[ROWS : ROWS + 8, :], -2), packed)
    sums_out[...] = jnp.where(place > 13, roll(left_in[ROWS + 8 : ROWS + OWN, :], 2), packed)


def background_kernel(m_all, d_all, mtable, table, local_in, background, local):
    smooth = jnp.dot(
        jnp.concatenate([d_all[l * ROWS + OWN : (l + 1) * ROWS, :] for l in range(DZ)], 0),
        table[0:128, :], precision=lax.Precision.HIGHEST, preferred_element_type=jnp.float32,
    )
    for l in range(DZ):
        local[l * ROWS + OWN : (l + 1) * ROWS, :] = smooth[l * 8 : (l + 1) * 8]
    entries = mtable[...]
    for z in range(Z):
        kind = m_all[z * ROWS : (z + 1) * ROWS, :]
        for channel in range(3):
            p = channel * Z + z
            background[p * ROWS : (p + 1) * ROWS, :] = looked_up(kind, entries, channel)


def looked_up(kind, entries, channel):
    one = [entries[channel : channel + 1, i : i + 1] for i in range(MATS)]
    return jnp.where(
        kind < 1.5, jnp.where(kind < 0.5, one[0], one[1]), jnp.where(kind < 2.5, one[2], one[3])
    )


def cell_rows(mask):
    spread = lax.broadcasted_iota(jnp.int32, (mask.shape[1], 128), 0) == (
        lanes(mask.shape[1]) // TILE
    )
    return jnp.dot(
        mask.astype(jnp.float32), spread.astype(jnp.float32), preferred_element_type=jnp.float32
    )


def project(values):
    base = math.tanh(sharpness * threshold)
    bottom = base + math.tanh(sharpness * (1.0 - threshold))
    level = jnp.tanh(sharpness * (values - threshold))
    return (base + level) * (1.0 / bottom), (sharpness / bottom) * (1.0 - level * level)


def step_kernel(count, reach, others):
    devices = count // CY
    norm_total = 2.0 * float(np.sum(np.exp(-np.arange(count) / reach)))

    def factor(m):
        return math.exp(-CY * m / reach), math.exp(-(count - CY * m) / reach)

    def fix(delta):
        if delta == 0:
            return 1.0 - math.exp(-count / reach)
        return (
            math.exp(-delta / reach) + math.exp(-(count - delta) / reach)
            - math.exp(-(count + delta) / reach) - math.exp(delta / reach)
        )

    def kernel(*refs):
        from_right, from_left = refs[:2]
        rest = refs[2 : 2 + others]
        (e_in, h_in, d_all, c_all, background, pairs, local, table, mtable, contrast_in, forward,
         e_final, h_final, gradient, e_all, h_all, inverse, se, sh, si, gained) = refs[2 + others :]
        entries = mtable[...]
        contrast = [contrast_in[0:1, c : c + 1] for c in range(3)]
        lane = lanes(ROWS)
        place = lane & 15
        odd = ((lane >> 4) & 1) == 1
        layer_of = lane >> 5
        part = place >> 2

        got_left = [from_left[i * ROWS : (i + 1) * ROWS, :] for i in range(2)]
        got_right = [from_right[i * ROWS : (i + 1) * ROWS, :] for i in range(2)]

        def strip(index):
            tile, q = index // 4, index % 4
            pair = pairs[(index // 2) * ROWS : (index // 2 + 1) * ROWS, :]
            if index % 2 == 0:
                own_l, own_r = pair, roll(pair, 8)
            else:
                own_l, own_r = roll(pair, -8), pair
            outer = jnp.where(part == 0, roll(got_left[tile], -4 * q), roll(got_right[tile], 12 - 4 * q))
            return jnp.where(part == 1, own_l, jnp.where(part == 2, own_r, outer))

        for channel in range(3):
            se[channel * ROWS : (channel + 1) * ROWS, :] = strip(channel)
            sh[channel * ROWS : (channel + 1) * ROWS, :] = strip(3 + channel)
        strip_material = strip(6)
        raw = strip(7)
        strip_density = jnp.where(odd, roll(raw, 16), raw)
        marks = jnp.where(odd, raw, roll(raw, -16))
        strip_cells = jnp.where((place & 2) == 2, marks, roll(marks, -2))

        def lane_factor(m):
            up, down = factor(m)
            return jnp.where(place == 12, up, down)

        sums = lane_factor(1) * got_left[1] + lane_factor(devices - 1) * got_right[1]
        for i, other in enumerate(rest):
            packed = other[...]
            sums = sums + lane_factor(2 + i) * jnp.concatenate(
                [roll(packed, 2), roll(packed, -2), packed], 0
            )
        strip_smooth = jnp.zeros((ROWS, 128), jnp.float32)
        designs, slopes = [], []
        cells = c_all[...]
        for l in range(DZ):
            at = (2 * l + 1) * 16 + 12
            up = jnp.broadcast_to(sums[:, at : at + 1], (ROWS, 128))
            down = jnp.broadcast_to(sums[:, at + 1 : at + 2], (ROWS, 128))
            both = local[l * ROWS : (l + 1) * ROWS, :]
            smooth = both[:, :128] + table[128:129, :128] * up + table[129:130, :128] * down
            far = both[:, 128:] + table[128:129, 128:] * up + table[129:130, 128:] * down
            strip_smooth = jnp.where(layer_of == l, far, strip_smooth)
            filtered = 0.5 * d_all[l * ROWS : (l + 1) * ROWS, :] + (0.5 / norm_total) * smooth
            projected, slope = project(filtered)
            designs.append(cells * projected)
            slopes.append(slope[:OWN] * cells[:OWN])
        for delta in range(4):
            value = fix(delta) * strip_density
            ahead = value if delta == 0 else roll(value, delta)
            behind = value if delta == 0 else roll(value, -delta)
            strip_smooth = strip_smooth + jnp.where(place >= 12 + delta, ahead, 0.0)
            strip_smooth = strip_smooth + jnp.where(place < 4 - delta, behind, 0.0)
        projected, _ = project(0.5 * strip_density + (0.5 / norm_total) * strip_smooth)
        strip_design = strip_cells * projected

        for channel in range(3):
            own = looked_up(strip_material, entries, channel)
            si[channel * ROWS : (channel + 1) * ROWS, :] = courant / (
                own + strip_design * contrast[channel]
            )
        for z in range(Z):
            for channel in range(3):
                p = channel * Z + z
                inverse[p * ROWS : (p + 1) * ROWS, :] = courant / (
                    background[p * ROWS : (p + 1) * ROWS, :] + designs[z // 2] * contrast[channel]
                )
        gained[...] = jnp.zeros_like(gained)

        zero = jnp.zeros((ROWS, 128), jnp.float32)
        last, first = lane == 127, lane == 0

        def at(ref, channel, z):
            p = channel * Z + z
            return ref[p * ROWS : (p + 1) * ROWS, :]

        def put(ref, channel, z, value):
            p = channel * Z + z
            ref[p * ROWS : p * ROWS + value.shape[0], :] = value

        def strip_at(ref, channel):
            return ref[channel * ROWS : (channel + 1) * ROWS, :]

        def step(t, starts=False, ends=False):
            ex, ey, ez = (strip_at(se, c) for c in range(3))
            e_mixed = jnp.where(place == 12, ez, roll(ex, 1))
            up_x = jnp.where(lane < 112, roll(ex, -16), 0.0)
            up_y = jnp.where(lane < 112, roll(ey, -16), 0.0)
            strips = []
            for channel, curl in enumerate(
                (
                    (roll(ez, -1) - ez) - (up_y - ey),
                    (up_x - ex) - (roll_rows(ez, -1) - ez),
                    (roll_rows(ey, -1) - ey) - (roll(ex, -1) - ex),
                )
            ):
                old = strip_at(sh, channel)
                value = old - courant * curl
                strips.append(value)
                if not ends:
                    sh[channel * ROWS : (channel + 1) * ROWS, :] = value
            hx, hy, hz = strips
            h_mixed = jnp.where(place == 3, hz, roll(hx, -1))
            if not ends:
                down_x = jnp.where(lane >= 16, roll(hx, 16), 0.0)
                down_y = jnp.where(lane >= 16, roll(hy, 16), 0.0)
                for channel, curl in enumerate(
                    (
                        (hz - roll(hz, 1)) - (hy - down_y),
                        (hx - down_x) - (hz - roll_rows(hz, 1)),
                        (hy - roll_rows(hy, 1)) - (hx - roll(hx, 1)),
                    )
                ):
                    se[channel * ROWS : (channel + 1) * ROWS, :] = (
                        strip_at(se, channel) + strip_at(si, channel) * curl
                    )

            rows = OWN if ends else ROWS
            ex, ey = at(e_all, 0, 0), at(e_all, 1, 0)
            hx_down = hy_down = zero
            for z in range(Z):
                ez = at(e_all, 2, z)
                ex_up = at(e_all, 0, z + 1) if z + 1 < Z else zero
                ey_up = at(e_all, 1, z + 1) if z + 1 < Z else zero
                beyond = roll(e_mixed, 115 - 16 * z)
                dy_ez = jnp.where(last, beyond, roll(ez, -1)) - ez
                dy_ex = roll(jnp.where(first, beyond, ex), -1) - ex
                dx_ez = roll_rows(ez, -1) - ez
                dx_ey = roll_rows(ey, -1) - ey
                fields = []
                for channel, curl in enumerate(
                    (dy_ez - (ey_up - ey), (ex_up - ex) - dx_ez, dx_ey - dy_ex)
                ):
                    old = at(h_all, channel, z)
                    value = old - courant * curl
                    put(h_all, channel, z, value)
                    fields.append(value)
                hx, hy, hz = fields
                beyond = roll(h_mixed, -(16 * z + 3))
                dy_hz = hz - jnp.where(first, beyond, roll(hz, 1))
                dy_hx = hx - roll(jnp.where(last, beyond, hx), 1)
                dx_hz = hz - roll_rows(hz, 1)
                dx_hy = hy - roll_rows(hy, 1)
                total = jnp.zeros((OWN, 128), jnp.float32)
                for channel, (old, curl) in enumerate(
                    (
                        (ex, dy_hz - (hy - hy_down)),
                        (ey, (hx - hx_down) - dx_hz),
                        (ez, dx_hy - dy_hx),
                    )
                ):
                    value = old[:rows] + at(inverse, channel, z)[:rows] * curl[:rows]
                    put(e_all, channel, z, value)
                    stored = forward[t, channel * Z + z].astype(jnp.float32)
                    total = total + contrast[channel] * (value[:OWN] * stored)
                l = z // 2
                gained[l * OWN : (l + 1) * OWN, :] = gained[l * OWN : (l + 1) * OWN, :] + total
                ex, ey = ex_up, ey_up
                hx_down, hy_down = hx, hy

        def middle(t, carry):
            step(t)
            return carry

        lax.fori_loop(0, STEPS, middle, 0)
        for p in range(3 * Z):
            e_final[p * OWN : (p + 1) * OWN, :] = e_all[p * ROWS : p * ROWS + OWN, :]
            h_final[p * OWN : (p + 1) * OWN, :] = h_all[p * ROWS : p * ROWS + OWN, :]
        for l in range(DZ):
            gradient[l * OWN : (l + 1) * OWN, :] = slopes[l] * gained[l * OWN : (l + 1) * OWN, :]

    return kernel


def body(
    density, tile_mask, material, material_table, contrast, electric, magnetic, forward_fields
):
    devices = lax.axis_size("gy")
    count = density.shape[2] * devices
    reach = 4.0 * CY
    constants = filter_constants(count, reach)

    to_prev, to_next, e_own, h_own, d_own, m_own, c_own, table, mtable, contrasts = call(
        pack_kernel,
        [vmem(EXTRA, 128), vmem(EXTRA + 24, 128),
         vmem(PLANES * OWN, 128), vmem(PLANES * OWN, 128), vmem(DZ * OWN, 128),
         vmem(Z * OWN, 128, dtype=jnp.int32), vmem(OWN, 128), vmem(*constants.shape),
         vmem(3, MATS), vmem(1, 3)],
        [electric.reshape(PLANES * OWN, 128), magnetic.reshape(PLANES * OWN, 128),
         density.reshape(DZ * OWN, 128),
         material.reshape(Z * OWN, 128), tile_mask, constants, material_table,
         contrast.reshape(1, 3)],
        scratch=[vmem(*tile_mask.shape, dtype=jnp.int32), pltpu.SemaphoreType.DMA((8,))],
        in_specs=[ANY] * 8,
    )
    from_prev = sent(to_next, "gx", 1)
    from_next = sent(to_prev, "gx", -1)
    e_all, h_all, d_all, c_all, pairs, left, right, m_all, local = call(
        own_kernel,
        [vmem(PLANES * ROWS, 128), vmem(PLANES * ROWS, 128), vmem(DZ * ROWS, 128),
         vmem(ROWS, 128), vmem(4 * ROWS, 128), vmem(2 * ROWS, 128), vmem(2 * ROWS, 128), vmem(Z * ROWS, 128),
         vmem(DZ * ROWS, 256)],
        [e_own, h_own, d_own, m_own, c_own, table],
    )
    e_all, h_all, d_all, c_all, m_all, pairs, left, right, sums = call(
        halo_kernel,
        [vmem(PLANES * ROWS, 128), vmem(PLANES * ROWS, 128), vmem(DZ * ROWS, 128),
         vmem(ROWS, 128), vmem(Z * ROWS, 128), vmem(4 * ROWS, 128),
         vmem(2 * ROWS, 128), vmem(2 * ROWS, 128), vmem(8, 128)],
        [from_next, from_prev, e_all, h_all, d_all, c_all, m_all, pairs, left, right, table],
        aliases={2: 0, 3: 1, 4: 2, 5: 3, 6: 4, 7: 5, 8: 6, 9: 7},
    )
    from_left = sent(right, "gy", 1)
    from_right = sent(left, "gy", -1)
    rest = [sent(sums, "gy", m) for m in range(2, devices - 1)]
    background, local = call(
        background_kernel, [vmem(PLANES * ROWS, 128), vmem(DZ * ROWS, 256)],
        [m_all, d_all, mtable, table, local], aliases={4: 1},
    )
    at = 2 + len(rest)
    outs = call(
        step_kernel(count, reach, len(rest)),
        [jax.ShapeDtypeStruct((PLANES * OWN, 128), jnp.float32),
         jax.ShapeDtypeStruct((PLANES * OWN, 128), jnp.float32),
         jax.ShapeDtypeStruct((DZ * OWN, 128), jnp.float32),
         vmem(PLANES * ROWS, 128), vmem(PLANES * ROWS, 128)],
        [from_right, from_left] + rest + [
            e_all, h_all, d_all, c_all, background, pairs, local, table,
            mtable, contrasts, forward_fields.reshape(STEPS, PLANES, OWN, 128),
        ],
        aliases={at: 3, at + 1: 4},
        scratch=[vmem(PLANES * ROWS, 128), vmem(3 * ROWS, 128), vmem(3 * ROWS, 128),
                 vmem(3 * ROWS, 128), vmem(DZ * OWN, 128)],
    )
    return (
        outs[0].reshape(electric.shape), outs[1].reshape(magnetic.shape),
        outs[2].reshape(density.shape),
    )


def solution(mesh):
    return jax.shard_map(
        body,
        mesh=mesh,
        in_specs=(
            P(None, "gx", "gy"),
            P("gx", "gy"),
            P(None, "gx", "gy"),
            P(),
            P(),
            P(None, None, "gx", "gy"),
            P(None, None, "gx", "gy"),
            P(None, None, None, "gx", "gy"),
        ),
        out_specs=(P(None, None, "gx", "gy"), P(None, None, "gx", "gy"), P(None, "gx", "gy")),
        check_vma=False,
    )
```

```python
import math

import jax
import jax.numpy as jnp
import numpy as np
from jax import lax
from jax.experimental import pallas as pl
from jax.experimental.pallas import tpu as pltpu
from jax.sharding import PartitionSpec as P

CY = 128
Z = 8
DZ = 4
STEPS = 4
TILE = 8
MATS = 4

courant = 0.5
sharpness = 4.0
threshold = 0.5

ROWS = 24
OWN = 16
SLOT = 48
KINDS = 3 * SLOT
LAYERS = KINDS + 24
EXTRA = LAYERS + 16
PLANES = 3 * Z

VM = pl.BlockSpec(memory_space=pltpu.VMEM)
ANY = pl.BlockSpec(memory_space=pl.ANY)


def vmem(*shape, dtype=jnp.float32):
    return pltpu.VMEM(shape, dtype)


def call(kernel, outs, ins, aliases=None, scratch=(), in_specs=None, out_specs=None):
    in_specs = in_specs or [VM] * len(ins)
    ins = [
        pltpu.with_memory_space_constraint(x, pltpu.VMEM if spec is VM else pltpu.HBM)
        for x, spec in zip(ins, in_specs)
    ]
    return pl.pallas_call(
        kernel,
        out_shape=outs,
        in_specs=in_specs,
        out_specs=out_specs or [VM] * len(outs),
        scratch_shapes=list(scratch),
        input_output_aliases=aliases or {},
        compiler_params=pltpu.CompilerParams(vmem_limit_bytes=32 * 1024 * 1024),
    )(*ins)


def lanes(rows):
    return lax.broadcasted_iota(jnp.int32, (rows, 128), 1)


def roll(x, by):
    return pltpu.roll(x, by % x.shape[1], 1)


def roll_rows(x, by):
    return pltpu.roll(x, by % x.shape[0], 0)


def sent(x, axis, by):
    size = lax.axis_size(axis)
    return lax.ppermute(x, axis, [(i, (i + by) % size) for i in range(size)])


def weight(offset, count, reach):
    ahead = np.mod(offset, count).astype(np.float64)
    behind = np.mod(-offset, count).astype(np.float64)
    return np.exp(-ahead / reach) + np.exp(-behind / reach)


def filter_constants(count, reach):
    source = np.arange(CY)
    strip = np.concatenate([np.arange(-4, 4), np.arange(CY - 4, CY + 4)])
    targets = np.concatenate([source, np.tile(strip, Z)])
    table = weight(targets[None, :] - source[:, None], count, reach)
    rows = np.zeros((8, 256))
    rows[0] = np.exp(-targets / reach)
    rows[1] = np.exp(targets / reach)
    rows[2, :CY] = np.exp(source / reach)
    rows[3, :CY] = np.exp(-source / reach)
    return np.concatenate([table, rows], 0).astype(np.float32)


def edge_window(planes):
    lane = lanes(planes[0].shape[0])
    width, by = 8, 16
    while len(planes) > 1:
        kept = ((lane + 4) & 127) < width
        planes = [
            jnp.where(kept, planes[i], roll(planes[i + 1], by)) for i in range(0, len(planes), 2)
        ]
        width, by = width + by, 2 * by
    return planes[0]


def edge_pairs(groups):
    lane = lanes(groups[0][0].shape[0])
    first = (lane & 15) < 8
    found = [edge_window(planes) for planes in groups]
    return [
        jnp.where(first, roll(found[2 * i], 4), roll(found[2 * i + 1], 12)) for i in range(4)
    ]


def edge_messages(pairs):
    quarter = (lanes(pairs[0].shape[0]) >> 2) & 3

    def pick(a, b, c, d):
        return jnp.where(quarter < 2, jnp.where(quarter == 0, a, b), jnp.where(quarter == 2, c, d))

    left, right = [], []
    for one, two in ((pairs[0], pairs[1]), (pairs[2], pairs[3])):
        left.append(pick(roll(one, -4), roll(one, -8), roll(two, 4), two))
        right.append(pick(one, roll(one, -4), roll(two, 8), roll(two, 4)))
    return left, right


def density_planes(layers, cells, rising, falling):
    place = lanes(cells.shape[0]) & 3
    planes = []
    for layer in layers:
        up = jnp.sum(layer * rising, axis=1, keepdims=True)
        down = jnp.sum(layer * falling, axis=1, keepdims=True)
        planes += [layer, jnp.where(place == 0, up, jnp.where(place == 1, down, cells))]
    return planes


def pack_kernel(
    electric, magnetic, density, material, mask,
    to_prev, to_next, e_own, h_own, d_own, m_own, c_all,
    mask_v, sems,
):
    copies = []
    moved = [
        (mask, mask_v), (electric, e_own), (magnetic, h_own), (density, d_own), (material, m_own),
    ]
    for i, (source, target) in enumerate(moved):
        copy = pltpu.make_async_copy(source, target, sems.at[i])
        copy.start()
        copies.append(copy)
    for copy in copies:
        copy.wait()

    cells = cell_rows(mask_v[...])
    c_all[0:TILE, :] = jnp.broadcast_to(cells[0:1], (TILE, 128))
    c_all[TILE:OWN, :] = jnp.broadcast_to(cells[1:2], (TILE, 128))

    def e(channel, row):
        return e_own[pl.ds(channel * Z * OWN + row, Z, stride=OWN), :]

    def h(channel, row):
        return h_own[pl.ds(channel * Z * OWN + row, Z, stride=OWN), :]

    def ahead_part(row):
        part_y = h(1, row) + courant * (e(2, row + 1) - e(2, row))
        part_z = h(2, row) - courant * (e(1, row + 1) - e(1, row))
        return part_y, part_z

    for out, first, mask_row in ((to_next, OWN - 3, 1), (to_prev, 0, 0)):
        for slot in range(3):
            row, at = first + slot, slot * SLOT
            for channel in range(3):
                out[at + 8 * channel : at + 8 * channel + 8, :] = e(channel, row)
                out[at + 24 + 8 * channel : at + 32 + 8 * channel, :] = h(channel, row)
            out[KINDS + 8 * slot : KINDS + 8 * slot + 8, :] = (
                m_own[pl.ds(row, Z, stride=OWN), :].astype(jnp.float32)
            )
            out[LAYERS + 4 * slot : LAYERS + 4 * slot + 4, :] = (
                d_own[pl.ds(row, DZ, stride=OWN), :]
            )
        out[LAYERS + 12 : LAYERS + 16, :] = jnp.broadcast_to(
            cells[mask_row : mask_row + 1], (4, 128)
        )
    part_y, part_z = ahead_part(2)
    to_prev[2 * SLOT + 32 : 2 * SLOT + 40, :] = part_y
    to_prev[2 * SLOT + 40 : 2 * SLOT + 48, :] = part_z
    part_y, part_z = ahead_part(OWN - 4)
    to_next[EXTRA : EXTRA + 8, :] = e(0, OWN - 4)
    to_next[EXTRA + 8 : EXTRA + 16, :] = part_y
    to_next[EXTRA + 16 : EXTRA + 24, :] = part_z


def own_kernel(
    table_in, mtable_in, contrast_in, e_own, h_own, d_own, m_own, c_own,
    table, mtable, contrast, e_all, h_all, d_all, c_all, pairs_out, left_out, right_out,
    m_all, local, sems,
):
    copies = [
        pltpu.make_async_copy(source, target, sems.at[i])
        for i, (source, target) in enumerate(
            ((table_in, table), (mtable_in, mtable), (contrast_in, contrast))
        )
    ]
    for copy in copies:
        copy.start()
    c_all[0:OWN, :] = c_own[...]
    groups = []
    for source, target in ((e_own, e_all), (h_own, h_all)):
        for channel in range(3):
            planes = []
            for z in range(Z):
                p = channel * Z + z
                plane = source[p * OWN : (p + 1) * OWN, :]
                target[p * ROWS : p * ROWS + OWN, :] = plane
                planes.append(plane)
            groups.append(planes)
    planes = []
    for z in range(Z):
        plane = m_own[z * OWN : (z + 1) * OWN, :].astype(jnp.float32)
        m_all[z * ROWS : z * ROWS + OWN, :] = plane
        planes.append(plane)
    groups.append(planes)
    layers = []
    for l in range(DZ):
        layers.append(d_own[l * OWN : (l + 1) * OWN, :])
        d_all[l * ROWS : l * ROWS + OWN, :] = layers[l]
    column = lanes(1).astype(jnp.float32) * (1.0 / (4.0 * CY))
    rising, falling = jnp.exp(column), jnp.exp(-column)
    groups.append(
        density_planes(layers, c_own[...], rising, falling)
    )
    pairs = edge_pairs(groups)
    left, right = edge_messages(pairs)
    for i in range(4):
        pairs_out[i * ROWS : i * ROWS + OWN, :] = pairs[i]
    for i in range(2):
        left_out[i * ROWS : i * ROWS + OWN, :] = left[i]
        right_out[i * ROWS : i * ROWS + OWN, :] = right[i]
    for copy in copies:
        copy.wait()
    smooth = jnp.dot(
        jnp.concatenate(layers, 0), table[0:128, :], precision=lax.Precision.HIGHEST,
        preferred_element_type=jnp.float32,
    )
    for l in range(DZ):
        local[l * ROWS : l * ROWS + OWN, :] = smooth[l * OWN : (l + 1) * OWN]


def halo_kernel(
    from_next, from_prev, e_in, h_in, d_in, c_in, m_in, pairs_in, left_in, right_in, table,
    e_all, h_all, d_all, c_all, m_all, pairs_out, left_out, right_out, sums_out,
):
    for got, first in ((from_next, 16), (from_prev, 21)):
        for slot in range(3):
            at, row = slot * SLOT, first + slot
            for channel in range(3):
                where = pl.ds(channel * Z * ROWS + row, Z, stride=ROWS)
                e_all[where, :] = got[at + 8 * channel : at + 8 * channel + 8, :]
                h_all[where, :] = got[at + 24 + 8 * channel : at + 32 + 8 * channel, :]
            m_all[pl.ds(row, Z, stride=ROWS), :] = got[KINDS + 8 * slot : KINDS + 8 * slot + 8, :]
            d_all[pl.ds(row, DZ, stride=ROWS), :] = got[LAYERS + 4 * slot : LAYERS + 4 * slot + 4, :]
            c_all[row : row + 1, :] = got[LAYERS + 12 : LAYERS + 13, :]
    zeros = jnp.zeros((Z, 128), jnp.float32)
    for channel in range(3):
        at = channel * Z * ROWS
        e_all[pl.ds(at + 19, Z, stride=ROWS), :] = from_next[
            2 * SLOT + 8 * channel : 2 * SLOT + 8 * channel + 8, :
        ]
        h_all[pl.ds(at + 19, Z, stride=ROWS), :] = zeros
        if channel > 0:
            e_all[pl.ds(at + 20, Z, stride=ROWS), :] = from_prev[8 * channel : 8 * channel + 8, :]
            h_all[pl.ds(at + 20, Z, stride=ROWS), :] = from_prev[
                EXTRA + 8 * channel : EXTRA + 8 * channel + 8, :
            ]
        else:
            e_all[pl.ds(at + 20, Z, stride=ROWS), :] = from_prev[EXTRA : EXTRA + 8, :]
            h_all[pl.ds(at + 20, Z, stride=ROWS), :] = zeros
    for row in (19, 20):
        m_all[pl.ds(row, Z, stride=ROWS), :] = zeros
        d_all[pl.ds(row, DZ, stride=ROWS), :] = zeros[0:DZ]
        c_all[row : row + 1, :] = zeros[0:1]

    groups = []
    for target in (e_all, h_all):
        for channel in range(3):
            groups.append(
                [target[(channel * Z + z) * ROWS + OWN : (channel * Z + z + 1) * ROWS, :] for z in range(Z)]
            )
    groups.append([m_all[z * ROWS + OWN : (z + 1) * ROWS, :] for z in range(Z)])
    layers = [d_all[l * ROWS + OWN : (l + 1) * ROWS, :] for l in range(DZ)]
    groups.append(
        density_planes(layers, c_all[OWN:ROWS, :], table[130:131, 0:128], table[131:132, 0:128])
    )
    pairs = edge_pairs(groups)
    left, right = edge_messages(pairs)
    for i in range(4):
        pairs_out[i * ROWS + OWN : (i + 1) * ROWS, :] = pairs[i]
    for i in range(2):
        left_out[i * ROWS + OWN : (i + 1) * ROWS, :] = left[i]
        right_out[i * ROWS + OWN : (i + 1) * ROWS, :] = right[i]
    place = lanes(8) & 15
    packed = left[1]
    packed = jnp.where(place < 12, roll(left_in[ROWS : ROWS + 8, :], -2), packed)
    sums_out[...] = jnp.where(place > 13, roll(left_in[ROWS + 8 : ROWS + OWN, :], 2), packed)


def background_kernel(m_all, d_all, mtable, table, local_in, background, local):
    smooth = jnp.dot(
        jnp.concatenate([d_all[l * ROWS + OWN : (l + 1) * ROWS, :] for l in range(DZ)], 0),
        table[0:128, :], precision=lax.Precision.HIGHEST, preferred_element_type=jnp.float32,
    )
    for l in range(DZ):
        local[l * ROWS + OWN : (l + 1) * ROWS, :] = smooth[l * 8 : (l + 1) * 8]
    entries = mtable[...]
    for z in range(Z):
        kind = m_all[z * ROWS : (z + 1) * ROWS, :]
        for channel in range(3):
            p = channel * Z + z
            background[p * ROWS : (p + 1) * ROWS, :] = looked_up(kind, entries, channel)


def looked_up(kind, entries, channel):
    one = [entries[channel : channel + 1, i : i + 1] for i in range(MATS)]
    return jnp.where(
        kind < 1.5, jnp.where(kind < 0.5, one[0], one[1]), jnp.where(kind < 2.5, one[2], one[3])
    )


def cell_rows(mask):
    spread = lax.broadcasted_iota(jnp.int32, (mask.shape[1], 128), 0) == (
        lanes(mask.shape[1]) // TILE
    )
    return jnp.dot(
        mask.astype(jnp.float32), spread.astype(jnp.float32), preferred_element_type=jnp.float32
    )


def project(values):
    base = math.tanh(sharpness * threshold)
    bottom = base + math.tanh(sharpness * (1.0 - threshold))
    level = jnp.tanh(sharpness * (values - threshold))
    return (base + level) * (1.0 / bottom), (sharpness / bottom) * (1.0 - level * level)


def plane_of(ref, channel, z, rows=ROWS):
    p = channel * Z + z
    return ref[p * ROWS : p * ROWS + rows, :]


def strip_of(ref, channel):
    return ref[channel * ROWS : (channel + 1) * ROWS, :]


def keep(ref, fields):
    for c, field in enumerate(fields):
        ref[c * ROWS : (c + 1) * ROWS, :] = field


def strip_magnetic(old, electric):
    lane = lanes(ROWS)
    ex, ey, ez = electric
    up_x = jnp.where(lane < 112, roll(ex, -16), 0.0)
    up_y = jnp.where(lane < 112, roll(ey, -16), 0.0)
    curls = (
        (roll(ez, -1) - ez) - (up_y - ey),
        (up_x - ex) - (roll_rows(ez, -1) - ez),
        (roll_rows(ey, -1) - ey) - (roll(ex, -1) - ex),
    )
    return [field - courant * curl for field, curl in zip(old, curls)]


def strip_electric(old, magnetic, inverse):
    lane = lanes(ROWS)
    hx, hy, hz = magnetic
    down_x = jnp.where(lane >= 16, roll(hx, 16), 0.0)
    down_y = jnp.where(lane >= 16, roll(hy, 16), 0.0)
    curls = (
        (hz - roll(hz, 1)) - (hy - down_y),
        (hx - down_x) - (hz - roll_rows(hz, 1)),
        (hy - roll_rows(hy, 1)) - (hx - roll(hx, 1)),
    )
    return [old[c] + inverse[c] * curl for c, curl in enumerate(curls)]


def planes_magnetic(e_all, h_in, h_out, strip_e):
    lane = lanes(ROWS)
    last, first = lane == 127, lane == 0
    zero = jnp.zeros((ROWS, 128), jnp.float32)
    mixed = jnp.where((lane & 15) == 12, strip_e[2], roll(strip_e[0], 1))
    ex_up, ey_up = plane_of(e_all, 0, 0), plane_of(e_all, 1, 0)
    for z in range(Z):
        ex, ey, ez = ex_up, ey_up, plane_of(e_all, 2, z)
        ex_up = plane_of(e_all, 0, z + 1) if z + 1 < Z else zero
        ey_up = plane_of(e_all, 1, z + 1) if z + 1 < Z else zero
        beyond = roll(mixed, 115 - 16 * z)
        dy_ez = jnp.where(last, beyond, roll(ez, -1)) - ez
        dy_ex = roll(jnp.where(first, beyond, ex), -1) - ex
        dx_ez = roll_rows(ez, -1) - ez
        dx_ey = roll_rows(ey, -1) - ey
        for channel, curl in enumerate(
            (dy_ez - (ey_up - ey), (ex_up - ex) - dx_ez, dx_ey - dy_ex)
        ):
            p = channel * Z + z
            h_out[p * ROWS : (p + 1) * ROWS, :] = plane_of(h_in, channel, z) - courant * curl


def planes_electric(e_all, h_all, inverse, strip_h, stored_at, contrast, gained, e_out, stride):
    lane = lanes(ROWS)
    last, first = lane == 127, lane == 0
    mixed = jnp.where((lane & 15) == 3, strip_h[2], roll(strip_h[0], -1))
    hx = hy = jnp.zeros((ROWS, 128), jnp.float32)
    for z in range(Z):
        hx_down, hy_down = hx, hy
        hx, hy, hz = (plane_of(h_all, c, z) for c in range(3))
        beyond = roll(mixed, -(16 * z + 3))
        dy_hz = hz - jnp.where(first, beyond, roll(hz, 1))
        dy_hx = hx - roll(jnp.where(last, beyond, hx), 1)
        dx_hz = hz - roll_rows(hz, 1)
        dx_hy = hy - roll_rows(hy, 1)
        total = jnp.zeros((OWN, 128), jnp.float32)
        for channel, curl in enumerate(
            (dy_hz - (hy - hy_down), (hx - hx_down) - dx_hz, dx_hy - dy_hx)
        ):
            p = channel * Z + z
            value = (
                plane_of(e_all, channel, z, stride)
                + plane_of(inverse, channel, z, stride) * curl[:stride]
            )
            e_out[p * stride : (p + 1) * stride, :] = value
            total = total + contrast[channel] * (value[:OWN] * stored_at(p).astype(jnp.float32))
        l = z // 2
        gained[l * OWN : (l + 1) * OWN, :] = gained[l * OWN : (l + 1) * OWN, :] + total


def lane_factor(m, count, reach):
    up, down = math.exp(-CY * m / reach), math.exp(-(count - CY * m) / reach)
    return jnp.where((lanes(ROWS) & 15) == 12, up, down)


def first_kernel(count, reach):
    devices = count // CY

    def kernel(from_right, from_left, pairs, e_all, h_in, h_all, se, sh, traits, sums):
        lane = lanes(ROWS)
        place = lane & 15
        odd = ((lane >> 4) & 1) == 1
        part = place >> 2
        got_left = [from_left[i * ROWS : (i + 1) * ROWS, :] for i in range(2)]
        got_right = [from_right[i * ROWS : (i + 1) * ROWS, :] for i in range(2)]

        def strip(index):
            tile, q = index // 4, index % 4
            pair = pairs[(index // 2) * ROWS : (index // 2 + 1) * ROWS, :]
            if index % 2 == 0:
                own_l, own_r = pair, roll(pair, 8)
            else:
                own_l, own_r = roll(pair, -8), pair
            outer = jnp.where(
                part == 0, roll(got_left[tile], -4 * q), roll(got_right[tile], 12 - 4 * q)
            )
            return jnp.where(part == 1, own_l, jnp.where(part == 2, own_r, outer))

        electric = [strip(c) for c in range(3)]
        keep(se, electric)
        keep(sh, strip_magnetic([strip(3 + c) for c in range(3)], electric))
        raw = strip(7)
        marks = jnp.where(odd, raw, roll(raw, -16))
        keep(
            traits,
            [
                strip(6),
                jnp.where(odd, roll(raw, 16), raw),
                jnp.where((place & 2) == 2, marks, roll(marks, -2)),
            ],
        )
        sums[...] = (
            lane_factor(1, count, reach) * got_left[1]
            + lane_factor(devices - 1, count, reach) * got_right[1]
        )
        planes_magnetic(e_all, h_in, h_all, electric)

    return kernel


def step_kernel(count, reach, others):
    norm_total = 2.0 * float(np.sum(np.exp(-np.arange(count) / reach)))

    def fix(delta):
        if delta == 0:
            return 1.0 - math.exp(-count / reach)
        return (
            math.exp(-delta / reach) + math.exp(-(count - delta) / reach)
            - math.exp(-(count + delta) / reach) - math.exp(delta / reach)
        )

    def kernel(*refs):
        rest = refs[:others]
        (e_in, h_in, se_in, sh_in, traits, sums_in, d_all, c_all, background, local, table, mtable,
         contrast_in, forward,
         e_final, h_final, gradient, e_all, h_all, se, sh,
         inverse, si, gained) = refs[others:]
        entries = mtable[...]
        contrast = [contrast_in[0:1, c : c + 1] for c in range(3)]
        lane = lanes(ROWS)
        place = lane & 15
        layer_of = lane >> 5

        sums = sums_in[...]
        for i, other in enumerate(rest):
            packed = other[...]
            sums = sums + lane_factor(2 + i, count, reach) * jnp.concatenate(
                [roll(packed, 2), roll(packed, -2), packed], 0
            )
        strip_density = strip_of(traits, 1)
        strip_smooth = jnp.zeros((ROWS, 128), jnp.float32)
        designs = []
        cells = c_all[...]
        for l in range(DZ):
            at = (2 * l + 1) * 16 + 12
            up = jnp.broadcast_to(sums[:, at : at + 1], (ROWS, 128))
            down = jnp.broadcast_to(sums[:, at + 1 : at + 2], (ROWS, 128))
            both = local[l * ROWS : (l + 1) * ROWS, :]
            smooth = both[:, :128] + table[128:129, :128] * up + table[129:130, :128] * down
            far = both[:, 128:] + table[128:129, 128:] * up + table[129:130, 128:] * down
            strip_smooth = jnp.where(layer_of == l, far, strip_smooth)
            filtered = 0.5 * d_all[l * ROWS : (l + 1) * ROWS, :] + (0.5 / norm_total) * smooth
            projected, slope = project(filtered)
            designs.append(cells * projected)
            gradient[l * OWN : (l + 1) * OWN, :] = slope[:OWN] * cells[:OWN]
        for delta in range(4):
            value = fix(delta) * strip_density
            ahead = value if delta == 0 else roll(value, delta)
            behind = value if delta == 0 else roll(value, -delta)
            strip_smooth = strip_smooth + jnp.where(place >= 12 + delta, ahead, 0.0)
            strip_smooth = strip_smooth + jnp.where(place < 4 - delta, behind, 0.0)
        projected, _ = project(0.5 * strip_density + (0.5 / norm_total) * strip_smooth)
        strip_design = strip_of(traits, 2) * projected
        keep(
            si,
            [
                courant
                / (looked_up(strip_of(traits, 0), entries, c) + strip_design * contrast[c])
                for c in range(3)
            ],
        )
        for z in range(Z):
            for channel in range(3):
                p = channel * Z + z
                inverse[p * ROWS : (p + 1) * ROWS, :] = courant / (
                    background[p * ROWS : (p + 1) * ROWS, :] + designs[z // 2] * contrast[channel]
                )
        gained[...] = jnp.zeros_like(gained)

        def step(t, carry):
            strip_h = [strip_of(sh, c) for c in range(3)]
            strip_e = strip_electric(
                [strip_of(se, c) for c in range(3)], strip_h, [strip_of(si, c) for c in range(3)]
            )
            keep(se, strip_e)
            keep(sh, strip_magnetic(strip_h, strip_e))
            planes_electric(
                e_all, h_all, inverse, strip_h, lambda p: forward[t, p], contrast, gained,
                e_all, ROWS,
            )
            planes_magnetic(e_all, h_all, h_all, strip_e)
            return carry

        lax.fori_loop(0, STEPS - 1, step, 0)
        for p in range(PLANES):
            h_final[p * OWN : (p + 1) * OWN, :] = h_all[p * ROWS : p * ROWS + OWN, :]
        planes_electric(
            e_all, h_all, inverse, [strip_of(sh, c) for c in range(3)],
            lambda p: forward[STEPS - 1, p], contrast, gained, e_final, OWN,
        )
        gradient[...] = gradient[...] * gained[...]

    return kernel


def body(
    density, tile_mask, material, material_table, contrast, electric, magnetic, forward_fields
):
    devices = lax.axis_size("gy")
    count = density.shape[2] * devices
    reach = 4.0 * CY
    constants = filter_constants(count, reach)

    to_prev, to_next, e_own, h_own, d_own, m_own, c_own = call(
        pack_kernel,
        [vmem(EXTRA, 128), vmem(EXTRA + 24, 128),
         vmem(PLANES * OWN, 128), vmem(PLANES * OWN, 128), vmem(DZ * OWN, 128),
         vmem(Z * OWN, 128, dtype=jnp.int32), vmem(OWN, 128)],
        [electric.reshape(PLANES * OWN, 128), magnetic.reshape(PLANES * OWN, 128),
         density.reshape(DZ * OWN, 128),
         material.reshape(Z * OWN, 128), tile_mask],
        scratch=[vmem(*tile_mask.shape, dtype=jnp.int32), pltpu.SemaphoreType.DMA((5,))],
        in_specs=[ANY] * 5,
    )
    from_prev = sent(to_next, "gx", 1)
    from_next = sent(to_prev, "gx", -1)
    table, mtable, contrasts, e_all, h_all, d_all, c_all, pairs, left, right, m_all, local = call(
        own_kernel,
        [vmem(*constants.shape), vmem(3, MATS), vmem(1, 3), vmem(PLANES * ROWS, 128), vmem(PLANES * ROWS, 128), vmem(DZ * ROWS, 128),
         vmem(ROWS, 128), vmem(4 * ROWS, 128), vmem(2 * ROWS, 128), vmem(2 * ROWS, 128), vmem(Z * ROWS, 128),
         vmem(DZ * ROWS, 256)],
        [constants, material_table, contrast.reshape(1, 3), e_own, h_own, d_own, m_own, c_own],
        scratch=[pltpu.SemaphoreType.DMA((3,))], in_specs=[ANY] * 3 + [VM] * 5,
    )
    e_all, h_all, d_all, c_all, m_all, pairs, left, right, sums = call(
        halo_kernel,
        [vmem(PLANES * ROWS, 128), vmem(PLANES * ROWS, 128), vmem(DZ * ROWS, 128),
         vmem(ROWS, 128), vmem(Z * ROWS, 128), vmem(4 * ROWS, 128),
         vmem(2 * ROWS, 128), vmem(2 * ROWS, 128), vmem(8, 128)],
        [from_next, from_prev, e_all, h_all, d_all, c_all, m_all, pairs, left, right, table],
        aliases={2: 0, 3: 1, 4: 2, 5: 3, 6: 4, 7: 5, 8: 6, 9: 7},
    )
    from_left = sent(right, "gy", 1)
    from_right = sent(left, "gy", -1)
    rest = [sent(sums, "gy", m) for m in range(2, devices - 1)]
    background, local = call(
        background_kernel, [vmem(PLANES * ROWS, 128), vmem(DZ * ROWS, 256)],
        [m_all, d_all, mtable, table, local], aliases={4: 1},
    )
    h_all, se, sh, traits, sums = call(
        first_kernel(count, reach),
        [vmem(PLANES * ROWS, 128), vmem(3 * ROWS, 128), vmem(3 * ROWS, 128),
         vmem(3 * ROWS, 128), vmem(ROWS, 128)],
        [from_right, from_left, pairs, e_all, h_all],
        aliases={4: 0},
    )
    at = len(rest)
    operands = rest + [
        e_all, h_all, se, sh, traits, sums, d_all, c_all, background, local, table, mtable,
        contrasts, forward_fields.reshape(STEPS, PLANES, OWN, 128),
    ]
    outs = call(
        step_kernel(count, reach, at),
        [jax.ShapeDtypeStruct((PLANES * OWN, 128), jnp.float32),
         jax.ShapeDtypeStruct((PLANES * OWN, 128), jnp.float32),
         jax.ShapeDtypeStruct((DZ * OWN, 128), jnp.float32),
         vmem(PLANES * ROWS, 128), vmem(PLANES * ROWS, 128), vmem(3 * ROWS, 128),
         vmem(3 * ROWS, 128)],
        operands,
        aliases={at: 3, at + 1: 4, at + 2: 5, at + 3: 6},
        scratch=[vmem(PLANES * ROWS, 128), vmem(3 * ROWS, 128), vmem(DZ * OWN, 128),
                 ],
    )
    return (
        outs[0].reshape(electric.shape), outs[1].reshape(magnetic.shape),
        outs[2].reshape(density.shape),
    )


def solution(mesh):
    return jax.shard_map(
        body,
        mesh=mesh,
        in_specs=(
            P(None, "gx", "gy"),
            P("gx", "gy"),
            P(None, "gx", "gy"),
            P(),
            P(),
            P(None, None, "gx", "gy"),
            P(None, None, "gx", "gy"),
            P(None, None, None, "gx", "gy"),
        ),
        out_specs=(P(None, None, "gx", "gy"), P(None, None, "gx", "gy"), P(None, "gx", "gy")),
        check_vma=False,
    )
```

```python
import math

import jax
import jax.numpy as jnp
import numpy as np
from jax import lax
from jax.experimental import pallas as pl
from jax.experimental.pallas import tpu as pltpu
from jax.sharding import PartitionSpec as P

CY = 128
Z = 8
DZ = 4
STEPS = 4
TILE = 8
MATS = 4

courant = 0.5
sharpness = 4.0
threshold = 0.5

ROWS = 24
OWN = 16
SLOT = 48
KINDS = 3 * SLOT
LAYERS = KINDS + 24
EXTRA = LAYERS + 16
PLANES = 3 * Z

VM = pl.BlockSpec(memory_space=pltpu.VMEM)
ANY = pl.BlockSpec(memory_space=pl.ANY)


def vmem(*shape, dtype=jnp.float32):
    return pltpu.VMEM(shape, dtype)


def call(kernel, outs, ins, aliases=None, scratch=(), in_specs=None, out_specs=None):
    in_specs = in_specs or [VM] * len(ins)
    ins = [
        pltpu.with_memory_space_constraint(x, pltpu.VMEM if spec is VM else pltpu.HBM)
        for x, spec in zip(ins, in_specs)
    ]
    return pl.pallas_call(
        kernel,
        out_shape=outs,
        in_specs=in_specs,
        out_specs=out_specs or [VM] * len(outs),
        scratch_shapes=list(scratch),
        input_output_aliases=aliases or {},
        compiler_params=pltpu.CompilerParams(vmem_limit_bytes=32 * 1024 * 1024),
    )(*ins)


def lanes(rows):
    return lax.broadcasted_iota(jnp.int32, (rows, 128), 1)


def roll(x, by):
    return pltpu.roll(x, by % x.shape[1], 1)


def roll_rows(x, by):
    return pltpu.roll(x, by % x.shape[0], 0)


def sent(x, axis, by):
    size = lax.axis_size(axis)
    return lax.ppermute(x, axis, [(i, (i + by) % size) for i in range(size)])


def weight(offset, count, reach):
    ahead = np.mod(offset, count).astype(np.float64)
    behind = np.mod(-offset, count).astype(np.float64)
    return np.exp(-ahead / reach) + np.exp(-behind / reach)


def filter_constants(count, reach):
    source = np.arange(CY)
    strip = np.concatenate([np.arange(-4, 4), np.arange(CY - 4, CY + 4)])
    targets = np.concatenate([source, np.tile(strip, Z)])
    table = weight(targets[None, :] - source[:, None], count, reach)
    rows = np.zeros((8, 256))
    rows[0] = np.exp(-targets / reach)
    rows[1] = np.exp(targets / reach)
    rows[2, :CY] = np.exp(source / reach)
    rows[3, :CY] = np.exp(-source / reach)
    return np.concatenate([table, rows], 0).astype(np.float32)


def edge_window(planes):
    lane = lanes(planes[0].shape[0])
    width, by = 8, 16
    while len(planes) > 1:
        kept = ((lane + 4) & 127) < width
        planes = [
            jnp.where(kept, planes[i], roll(planes[i + 1], by)) for i in range(0, len(planes), 2)
        ]
        width, by = width + by, 2 * by
    return planes[0]


def edge_pairs(groups):
    lane = lanes(groups[0][0].shape[0])
    first = (lane & 15) < 8
    found = [edge_window(planes) for planes in groups]
    return [
        jnp.where(first, roll(found[2 * i], 4), roll(found[2 * i + 1], 12)) for i in range(4)
    ]


def edge_messages(pairs):
    quarter = (lanes(pairs[0].shape[0]) >> 2) & 3

    def pick(a, b, c, d):
        return jnp.where(quarter < 2, jnp.where(quarter == 0, a, b), jnp.where(quarter == 2, c, d))

    left, right = [], []
    for one, two in ((pairs[0], pairs[1]), (pairs[2], pairs[3])):
        left.append(pick(roll(one, -4), roll(one, -8), roll(two, 4), two))
        right.append(pick(one, roll(one, -4), roll(two, 8), roll(two, 4)))
    return left, right


def density_planes(layers, cells):
    return [plane for layer in layers for plane in (layer, cells)]


def with_sums(tiles, layers):
    lane = lanes(layers[0].shape[0])
    column = lanes(1).astype(jnp.float32) * (1.0 / (4.0 * CY))
    rising, falling = jnp.exp(column), jnp.exp(-column)
    for l, layer in enumerate(layers):
        at = (2 * l + 1) * 16 + 12
        up = jnp.sum(layer * rising, axis=1, keepdims=True)
        down = jnp.sum(layer * falling, axis=1, keepdims=True)
        tiles = [
            jnp.where(lane == at, up, jnp.where(lane == at + 1, down, tile)) for tile in tiles
        ]
    return tiles


def pack_kernel(
    electric, magnetic, density, material, mask,
    to_prev, to_next, e_own, h_own, d_own, m_own, c_all,
    mask_v, sems,
):
    copies = []
    moved = [
        (electric, e_own), (magnetic, h_own), (density, d_own), (material, m_own), (mask, mask_v),
    ]
    for i, (source, target) in enumerate(moved):
        copy = pltpu.make_async_copy(source, target, sems.at[i])
        copy.start()
        copies.append(copy)
    copies[-1].wait()
    cells = cell_rows(mask_v[...])
    c_all[0:TILE, :] = jnp.broadcast_to(cells[0:1], (TILE, 128))
    c_all[TILE:OWN, :] = jnp.broadcast_to(cells[1:2], (TILE, 128))
    for copy in copies[:-1]:
        copy.wait()

    def e(channel, row):
        return e_own[pl.ds(channel * Z * OWN + row, Z, stride=OWN), :]

    def h(channel, row):
        return h_own[pl.ds(channel * Z * OWN + row, Z, stride=OWN), :]

    def ahead_part(row):
        part_y = h(1, row) + courant * (e(2, row + 1) - e(2, row))
        part_z = h(2, row) - courant * (e(1, row + 1) - e(1, row))
        return part_y, part_z

    for out, first, mask_row in ((to_next, OWN - 3, 1), (to_prev, 0, 0)):
        for slot in range(3):
            row, at = first + slot, slot * SLOT
            for channel in range(3):
                out[at + 8 * channel : at + 8 * channel + 8, :] = e(channel, row)
                out[at + 24 + 8 * channel : at + 32 + 8 * channel, :] = h(channel, row)
            out[KINDS + 8 * slot : KINDS + 8 * slot + 8, :] = (
                m_own[pl.ds(row, Z, stride=OWN), :].astype(jnp.float32)
            )
            out[LAYERS + 4 * slot : LAYERS + 4 * slot + 4, :] = (
                d_own[pl.ds(row, DZ, stride=OWN), :]
            )
        out[LAYERS + 12 : LAYERS + 16, :] = jnp.broadcast_to(
            cells[mask_row : mask_row + 1], (4, 128)
        )
    part_y, part_z = ahead_part(2)
    to_prev[2 * SLOT + 32 : 2 * SLOT + 40, :] = part_y
    to_prev[2 * SLOT + 40 : 2 * SLOT + 48, :] = part_z
    part_y, part_z = ahead_part(OWN - 4)
    to_next[EXTRA : EXTRA + 8, :] = e(0, OWN - 4)
    to_next[EXTRA + 8 : EXTRA + 16, :] = part_y
    to_next[EXTRA + 16 : EXTRA + 24, :] = part_z


def own_kernel(
    table_in, mtable_in, contrast_in, e_own, h_own, d_own, m_own, c_own,
    table, mtable, contrast, e_all, h_all, d_all, c_all, pairs_out, left_out, right_out,
    m_all, local, sems,
):
    copies = [
        pltpu.make_async_copy(source, target, sems.at[i])
        for i, (source, target) in enumerate(
            ((table_in, table), (mtable_in, mtable), (contrast_in, contrast))
        )
    ]
    for copy in copies:
        copy.start()
    c_all[0:OWN, :] = c_own[...]
    groups = []
    for source, target in ((e_own, e_all), (h_own, h_all)):
        for channel in range(3):
            planes = []
            for z in range(Z):
                p = channel * Z + z
                plane = source[p * OWN : (p + 1) * OWN, :]
                target[p * ROWS : p * ROWS + OWN, :] = plane
                planes.append(plane)
            groups.append(planes)
    planes = []
    for z in range(Z):
        plane = m_own[z * OWN : (z + 1) * OWN, :].astype(jnp.float32)
        m_all[z * ROWS : z * ROWS + OWN, :] = plane
        planes.append(plane)
    groups.append(planes)
    layers = []
    for l in range(DZ):
        layers.append(d_own[l * OWN : (l + 1) * OWN, :])
        d_all[l * ROWS : l * ROWS + OWN, :] = layers[l]
    groups.append(density_planes(layers, c_own[...]))
    pairs = edge_pairs(groups)
    left, right = edge_messages(pairs)
    left[1], right[1] = with_sums([left[1], right[1]], layers)
    for i in range(4):
        pairs_out[i * ROWS : i * ROWS + OWN, :] = pairs[i]
    for i in range(2):
        left_out[i * ROWS : i * ROWS + OWN, :] = left[i]
        right_out[i * ROWS : i * ROWS + OWN, :] = right[i]
    for copy in copies:
        copy.wait()
    smooth = jnp.dot(
        jnp.concatenate(layers, 0), table[0:128, :], precision=lax.Precision.HIGHEST,
        preferred_element_type=jnp.float32,
    )
    for l in range(DZ):
        local[l * ROWS : l * ROWS + OWN, :] = smooth[l * OWN : (l + 1) * OWN]


def unpack(got, first, e_all, h_all, d_all, c_all, m_all):
    for slot in range(3):
        at, row = slot * SLOT, first + slot
        for channel in range(3):
            where = pl.ds(channel * Z * ROWS + row, Z, stride=ROWS)
            e_all[where, :] = got[at + 8 * channel : at + 8 * channel + 8, :]
            h_all[where, :] = got[at + 24 + 8 * channel : at + 32 + 8 * channel, :]
        m_all[pl.ds(row, Z, stride=ROWS), :] = got[KINDS + 8 * slot : KINDS + 8 * slot + 8, :]
        d_all[pl.ds(row, DZ, stride=ROWS), :] = got[LAYERS + 4 * slot : LAYERS + 4 * slot + 4, :]
        c_all[row : row + 1, :] = got[LAYERS + 12 : LAYERS + 13, :]


def unpack_next(got, e_all, h_all, d_all, c_all, m_all):
    unpack(got, 16, e_all, h_all, d_all, c_all, m_all)
    zeros = jnp.zeros((Z, 128), jnp.float32)
    for channel in range(3):
        where = pl.ds(channel * Z * ROWS + 19, Z, stride=ROWS)
        e_all[where, :] = got[2 * SLOT + 8 * channel : 2 * SLOT + 8 * channel + 8, :]
        h_all[where, :] = zeros
    m_all[pl.ds(19, Z, stride=ROWS), :] = zeros
    d_all[pl.ds(19, DZ, stride=ROWS), :] = zeros[0:DZ]
    c_all[19:20, :] = zeros[0:1]


def unpack_prev(got, e_all, h_all, d_all, c_all, m_all):
    unpack(got, 21, e_all, h_all, d_all, c_all, m_all)
    zeros = jnp.zeros((Z, 128), jnp.float32)
    for channel in range(3):
        where = pl.ds(channel * Z * ROWS + 20, Z, stride=ROWS)
        extra = got[EXTRA + 8 * channel : EXTRA + 8 * channel + 8, :]
        if channel == 0:
            e_all[where, :] = extra
            h_all[where, :] = zeros
        else:
            e_all[where, :] = got[8 * channel : 8 * channel + 8, :]
            h_all[where, :] = extra
    m_all[pl.ds(20, Z, stride=ROWS), :] = zeros
    d_all[pl.ds(20, DZ, stride=ROWS), :] = zeros[0:DZ]
    c_all[20:21, :] = zeros[0:1]


def early_kernel(got, e_in, h_in, d_in, c_in, m_in, e_all, h_all, d_all, c_all, m_all):
    unpack_prev(got, e_all, h_all, d_all, c_all, m_all)


def halo_kernel(
    got, e_in, h_in, d_in, c_in, m_in, pairs_in, left_in, right_in, table,
    e_all, h_all, d_all, c_all, m_all, pairs_out, left_out, right_out, sums_out,
):
    unpack_next(got, e_all, h_all, d_all, c_all, m_all)

    groups = []
    for target in (e_all, h_all):
        for channel in range(3):
            groups.append(
                [target[(channel * Z + z) * ROWS + OWN : (channel * Z + z + 1) * ROWS, :] for z in range(Z)]
            )
    groups.append([m_all[z * ROWS + OWN : (z + 1) * ROWS, :] for z in range(Z)])
    layers = [d_all[l * ROWS + OWN : (l + 1) * ROWS, :] for l in range(DZ)]
    groups.append(density_planes(layers, c_all[OWN:ROWS, :]))
    pairs = edge_pairs(groups)
    left, right = edge_messages(pairs)
    left[1], right[1] = with_sums([left[1], right[1]], layers)
    for i in range(4):
        pairs_out[i * ROWS + OWN : (i + 1) * ROWS, :] = pairs[i]
    for i in range(2):
        left_out[i * ROWS + OWN : (i + 1) * ROWS, :] = left[i]
        right_out[i * ROWS + OWN : (i + 1) * ROWS, :] = right[i]
    place = lanes(8) & 15
    packed = left[1]
    packed = jnp.where(place < 12, roll(left_in[ROWS : ROWS + 8, :], -2), packed)
    sums_out[...] = jnp.where(place > 13, roll(left_in[ROWS + 8 : ROWS + OWN, :], 2), packed)


def background_kernel(m_all, d_all, mtable, table, local_in, background, local):
    smooth = jnp.dot(
        jnp.concatenate([d_all[l * ROWS + OWN : (l + 1) * ROWS, :] for l in range(DZ)], 0),
        table[0:128, :], precision=lax.Precision.HIGHEST, preferred_element_type=jnp.float32,
    )
    for l in range(DZ):
        local[l * ROWS + OWN : (l + 1) * ROWS, :] = smooth[l * 8 : (l + 1) * 8]
    entries = mtable[...]
    for z in range(Z):
        kind = m_all[z * ROWS : (z + 1) * ROWS, :]
        for channel in range(3):
            p = channel * Z + z
            background[p * ROWS : (p + 1) * ROWS, :] = looked_up(kind, entries, channel)


def looked_up(kind, entries, channel):
    one = [entries[channel : channel + 1, i : i + 1] for i in range(MATS)]
    return jnp.where(
        kind < 1.5, jnp.where(kind < 0.5, one[0], one[1]), jnp.where(kind < 2.5, one[2], one[3])
    )


def cell_rows(mask):
    spread = lax.broadcasted_iota(jnp.int32, (mask.shape[1], 128), 0) == (
        lanes(mask.shape[1]) // TILE
    )
    return jnp.dot(
        mask.astype(jnp.float32), spread.astype(jnp.float32), preferred_element_type=jnp.float32
    )


def project(values):
    base = math.tanh(sharpness * threshold)
    bottom = base + math.tanh(sharpness * (1.0 - threshold))
    level = jnp.tanh(sharpness * (values - threshold))
    return (base + level) * (1.0 / bottom), (sharpness / bottom) * (1.0 - level * level)


def plane_of(ref, channel, z, rows=ROWS):
    p = channel * Z + z
    return ref[p * ROWS : p * ROWS + rows, :]


def strip_of(ref, channel):
    return ref[channel * ROWS : (channel + 1) * ROWS, :]


def keep(ref, fields):
    for c, field in enumerate(fields):
        ref[c * ROWS : (c + 1) * ROWS, :] = field


def strip_magnetic(old, electric):
    lane = lanes(ROWS)
    ex, ey, ez = electric
    up_x = jnp.where(lane < 112, roll(ex, -16), 0.0)
    up_y = jnp.where(lane < 112, roll(ey, -16), 0.0)
    curls = (
        (roll(ez, -1) - ez) - (up_y - ey),
        (up_x - ex) - (roll_rows(ez, -1) - ez),
        (roll_rows(ey, -1) - ey) - (roll(ex, -1) - ex),
    )
    return [field - courant * curl for field, curl in zip(old, curls)]


def strip_electric(old, magnetic, inverse):
    lane = lanes(ROWS)
    hx, hy, hz = magnetic
    down_x = jnp.where(lane >= 16, roll(hx, 16), 0.0)
    down_y = jnp.where(lane >= 16, roll(hy, 16), 0.0)
    curls = (
        (hz - roll(hz, 1)) - (hy - down_y),
        (hx - down_x) - (hz - roll_rows(hz, 1)),
        (hy - roll_rows(hy, 1)) - (hx - roll(hx, 1)),
    )
    return [old[c] + inverse[c] * curl for c, curl in enumerate(curls)]


def planes_magnetic(e_all, h_in, h_out, strip_e):
    lane = lanes(ROWS)
    last, first = lane == 127, lane == 0
    zero = jnp.zeros((ROWS, 128), jnp.float32)
    mixed = jnp.where((lane & 15) == 12, strip_e[2], roll(strip_e[0], 1))
    ex_up, ey_up = plane_of(e_all, 0, 0), plane_of(e_all, 1, 0)
    for z in range(Z):
        ex, ey, ez = ex_up, ey_up, plane_of(e_all, 2, z)
        ex_up = plane_of(e_all, 0, z + 1) if z + 1 < Z else zero
        ey_up = plane_of(e_all, 1, z + 1) if z + 1 < Z else zero
        beyond = roll(mixed, 115 - 16 * z)
        dy_ez = jnp.where(last, beyond, roll(ez, -1)) - ez
        dy_ex = roll(jnp.where(first, beyond, ex), -1) - ex
        dx_ez = roll_rows(ez, -1) - ez
        dx_ey = roll_rows(ey, -1) - ey
        for channel, curl in enumerate(
            (dy_ez - (ey_up - ey), (ex_up - ex) - dx_ez, dx_ey - dy_ex)
        ):
            p = channel * Z + z
            h_out[p * ROWS : (p + 1) * ROWS, :] = plane_of(h_in, channel, z) - courant * curl


def planes_electric(e_all, h_all, inverse, strip_h, stored_at, contrast, gained, e_out, stride):
    lane = lanes(ROWS)
    last, first = lane == 127, lane == 0
    mixed = jnp.where((lane & 15) == 3, strip_h[2], roll(strip_h[0], -1))
    hx = hy = jnp.zeros((ROWS, 128), jnp.float32)
    for z in range(Z):
        hx_down, hy_down = hx, hy
        hx, hy, hz = (plane_of(h_all, c, z) for c in range(3))
        beyond = roll(mixed, -(16 * z + 3))
        dy_hz = hz - jnp.where(first, beyond, roll(hz, 1))
        dy_hx = hx - roll(jnp.where(last, beyond, hx), 1)
        dx_hz = hz - roll_rows(hz, 1)
        dx_hy = hy - roll_rows(hy, 1)
        total = jnp.zeros((OWN, 128), jnp.float32)
        for channel, curl in enumerate(
            (dy_hz - (hy - hy_down), (hx - hx_down) - dx_hz, dx_hy - dy_hx)
        ):
            p = channel * Z + z
            value = (
                plane_of(e_all, channel, z, stride)
                + plane_of(inverse, channel, z, stride) * curl[:stride]
            )
            e_out[p * stride : (p + 1) * stride, :] = value
            total = total + contrast[channel] * (value[:OWN] * stored_at(p).astype(jnp.float32))
        l = z // 2
        gained[l * OWN : (l + 1) * OWN, :] = gained[l * OWN : (l + 1) * OWN, :] + total


def lane_factor(m, count, reach):
    up, down = math.exp(-CY * m / reach), math.exp(-(count - CY * m) / reach)
    return jnp.where((lanes(ROWS) & 15) == 12, up, down)


def norm_of(count, reach):
    return 2.0 * float(np.sum(np.exp(-np.arange(count) / reach)))


def first_kernel(count, reach):
    devices = count // CY
    norm_total = norm_of(count, reach)

    def fix(delta):
        if delta == 0:
            return 1.0 - math.exp(-count / reach)
        return (
            math.exp(-delta / reach) + math.exp(-(count - delta) / reach)
            - math.exp(-(count + delta) / reach) - math.exp(delta / reach)
        )

    def kernel(from_right, from_left, pairs, e_all, h_in, mtable, h_all, se, sh, traits, sums):
        lane = lanes(ROWS)
        place = lane & 15
        odd = ((lane >> 4) & 1) == 1
        part = place >> 2
        got_left = [from_left[i * ROWS : (i + 1) * ROWS, :] for i in range(2)]
        got_right = [from_right[i * ROWS : (i + 1) * ROWS, :] for i in range(2)]

        def strip(index):
            tile, q = index // 4, index % 4
            pair = pairs[(index // 2) * ROWS : (index // 2 + 1) * ROWS, :]
            if index % 2 == 0:
                own_l, own_r = pair, roll(pair, 8)
            else:
                own_l, own_r = roll(pair, -8), pair
            outer = jnp.where(
                part == 0, roll(got_left[tile], -4 * q), roll(got_right[tile], 12 - 4 * q)
            )
            return jnp.where(part == 1, own_l, jnp.where(part == 2, own_r, outer))

        electric = [strip(c) for c in range(3)]
        keep(se, electric)
        keep(sh, strip_magnetic([strip(3 + c) for c in range(3)], electric))
        raw = strip(7)
        marks = jnp.where(odd, raw, roll(raw, -16))
        layers = jnp.where(odd, roll(raw, 16), raw)
        known = jnp.zeros((ROWS, 128), jnp.float32)
        for delta in range(4):
            value = fix(delta) * layers
            ahead = value if delta == 0 else roll(value, delta)
            behind = value if delta == 0 else roll(value, -delta)
            known = known + jnp.where(place >= 12 + delta, ahead, 0.0)
            known = known + jnp.where(place < 4 - delta, behind, 0.0)
        kind = strip(6)
        entries = mtable[...]
        keep(
            traits,
            [
                0.5 * layers + (0.5 / norm_total) * known,
                jnp.where((place & 2) == 2, marks, roll(marks, -2)),
            ]
            + [looked_up(kind, entries, c) for c in range(3)],
        )
        sums[...] = (
            lane_factor(1, count, reach) * got_left[1]
            + lane_factor(devices - 1, count, reach) * got_right[1]
        )
        planes_magnetic(e_all, h_in, h_all, electric)

    return kernel


def step_kernel(count, reach, others):
    norm_total = norm_of(count, reach)

    def kernel(*refs):
        rest = refs[:others]
        (e_in, h_in, se_in, sh_in, traits, sums_in, d_all, c_all, background, local, table,
         contrast_in, forward,
         e_final, h_final, gradient, e_all, h_all, se, sh,
         inverse, si, gained) = refs[others:]
        contrast = [contrast_in[0:1, c : c + 1] for c in range(3)]
        lane = lanes(ROWS)
        layer_of = lane >> 5

        sums = sums_in[...]
        for i, other in enumerate(rest):
            packed = other[...]
            sums = sums + lane_factor(2 + i, count, reach) * jnp.concatenate(
                [roll(packed, 2), roll(packed, -2), packed], 0
            )
        strip_smooth = jnp.zeros((ROWS, 128), jnp.float32)
        designs = []
        cells = c_all[...]
        for l in range(DZ):
            at = (2 * l + 1) * 16 + 12
            up = jnp.broadcast_to(sums[:, at : at + 1], (ROWS, 128))
            down = jnp.broadcast_to(sums[:, at + 1 : at + 2], (ROWS, 128))
            both = local[l * ROWS : (l + 1) * ROWS, :]
            smooth = both[:, :128] + table[128:129, :128] * up + table[129:130, :128] * down
            far = both[:, 128:] + table[128:129, 128:] * up + table[129:130, 128:] * down
            strip_smooth = jnp.where(layer_of == l, far, strip_smooth)
            filtered = 0.5 * d_all[l * ROWS : (l + 1) * ROWS, :] + (0.5 / norm_total) * smooth
            projected, slope = project(filtered)
            designs.append(cells * projected)
            gradient[l * OWN : (l + 1) * OWN, :] = slope[:OWN] * cells[:OWN]
        projected, _ = project(strip_of(traits, 0) + (0.5 / norm_total) * strip_smooth)
        strip_design = strip_of(traits, 1) * projected
        keep(
            si,
            [courant / (strip_of(traits, 2 + c) + strip_design * contrast[c]) for c in range(3)],
        )
        for z in range(Z):
            for channel in range(3):
                p = channel * Z + z
                inverse[p * ROWS : (p + 1) * ROWS, :] = courant / (
                    background[p * ROWS : (p + 1) * ROWS, :] + designs[z // 2] * contrast[channel]
                )
        gained[...] = jnp.zeros_like(gained)

        def step(t, carry):
            strip_h = [strip_of(sh, c) for c in range(3)]
            strip_e = strip_electric(
                [strip_of(se, c) for c in range(3)], strip_h, [strip_of(si, c) for c in range(3)]
            )
            keep(se, strip_e)
            keep(sh, strip_magnetic(strip_h, strip_e))
            planes_electric(
                e_all, h_all, inverse, strip_h, lambda p: forward[t, p], contrast, gained,
                e_all, ROWS,
            )
            planes_magnetic(e_all, h_all, h_all, strip_e)
            return carry

        lax.fori_loop(0, STEPS - 1, step, 0)
        for p in range(PLANES):
            h_final[p * OWN : (p + 1) * OWN, :] = h_all[p * ROWS : p * ROWS + OWN, :]
        planes_electric(
            e_all, h_all, inverse, [strip_of(sh, c) for c in range(3)],
            lambda p: forward[STEPS - 1, p], contrast, gained, e_final, OWN,
        )
        gradient[...] = gradient[...] * gained[...]

    return kernel


def body(
    density, tile_mask, material, material_table, contrast, electric, magnetic, forward_fields
):
    devices = lax.axis_size("gy")
    count = density.shape[2] * devices
    reach = 4.0 * CY
    constants = filter_constants(count, reach)

    to_prev, to_next, e_own, h_own, d_own, m_own, c_own = call(
        pack_kernel,
        [vmem(EXTRA, 128), vmem(EXTRA + 24, 128),
         vmem(PLANES * OWN, 128), vmem(PLANES * OWN, 128), vmem(DZ * OWN, 128),
         vmem(Z * OWN, 128, dtype=jnp.int32), vmem(OWN, 128)],
        [electric.reshape(PLANES * OWN, 128), magnetic.reshape(PLANES * OWN, 128),
         density.reshape(DZ * OWN, 128),
         material.reshape(Z * OWN, 128), tile_mask],
        scratch=[vmem(*tile_mask.shape, dtype=jnp.int32), pltpu.SemaphoreType.DMA((5,))],
        in_specs=[ANY] * 5,
    )
    from_prev = sent(to_next, "gx", 1)
    from_next = sent(to_prev, "gx", -1)
    table, mtable, contrasts, e_all, h_all, d_all, c_all, pairs, left, right, m_all, local = call(
        own_kernel,
        [vmem(*constants.shape), vmem(3, MATS), vmem(1, 3), vmem(PLANES * ROWS, 128), vmem(PLANES * ROWS, 128), vmem(DZ * ROWS, 128),
         vmem(ROWS, 128), vmem(4 * ROWS, 128), vmem(2 * ROWS, 128), vmem(2 * ROWS, 128), vmem(Z * ROWS, 128),
         vmem(DZ * ROWS, 256)],
        [constants, material_table, contrast.reshape(1, 3), e_own, h_own, d_own, m_own, c_own],
        scratch=[pltpu.SemaphoreType.DMA((3,))], in_specs=[ANY] * 3 + [VM] * 5,
    )
    fields = [vmem(PLANES * ROWS, 128), vmem(PLANES * ROWS, 128), vmem(DZ * ROWS, 128),
              vmem(ROWS, 128), vmem(Z * ROWS, 128)]
    e_all, h_all, d_all, c_all, m_all = call(
        early_kernel, fields, [from_prev, e_all, h_all, d_all, c_all, m_all],
        aliases={i + 1: i for i in range(5)},
    )
    e_all, h_all, d_all, c_all, m_all, pairs, left, right, sums = call(
        halo_kernel,
        [vmem(PLANES * ROWS, 128), vmem(PLANES * ROWS, 128), vmem(DZ * ROWS, 128),
         vmem(ROWS, 128), vmem(Z * ROWS, 128), vmem(4 * ROWS, 128),
         vmem(2 * ROWS, 128), vmem(2 * ROWS, 128), vmem(8, 128)],
        [from_next, e_all, h_all, d_all, c_all, m_all, pairs, left, right, table],
        aliases={i + 1: i for i in range(8)},
    )
    from_left = sent(right, "gy", 1)
    from_right = sent(left, "gy", -1)
    rest = [sent(sums, "gy", m) for m in range(2, devices - 1)]
    background, local = call(
        background_kernel, [vmem(PLANES * ROWS, 128), vmem(DZ * ROWS, 256)],
        [m_all, d_all, mtable, table, local], aliases={4: 1},
    )
    h_all, se, sh, traits, sums = call(
        first_kernel(count, reach),
        [vmem(PLANES * ROWS, 128), vmem(3 * ROWS, 128), vmem(3 * ROWS, 128),
         vmem(5 * ROWS, 128), vmem(ROWS, 128)],
        [from_right, from_left, pairs, e_all, h_all, mtable],
        aliases={4: 0},
    )
    at = len(rest)
    operands = rest + [
        e_all, h_all, se, sh, traits, sums, d_all, c_all, background, local, table,
        contrasts, forward_fields.reshape(STEPS, PLANES, OWN, 128),
    ]
    outs = call(
        step_kernel(count, reach, at),
        [jax.ShapeDtypeStruct((PLANES * OWN, 128), jnp.float32),
         jax.ShapeDtypeStruct((PLANES * OWN, 128), jnp.float32),
         jax.ShapeDtypeStruct((DZ * OWN, 128), jnp.float32),
         vmem(PLANES * ROWS, 128), vmem(PLANES * ROWS, 128), vmem(3 * ROWS, 128),
         vmem(3 * ROWS, 128)],
        operands,
        aliases={at: 3, at + 1: 4, at + 2: 5, at + 3: 6},
        scratch=[vmem(PLANES * ROWS, 128), vmem(3 * ROWS, 128), vmem(DZ * OWN, 128),
                 ],
    )
    return (
        outs[0].reshape(electric.shape), outs[1].reshape(magnetic.shape),
        outs[2].reshape(density.shape),
    )


def solution(mesh):
    return jax.shard_map(
        body,
        mesh=mesh,
        in_specs=(
            P(None, "gx", "gy"),
            P("gx", "gy"),
            P(None, "gx", "gy"),
            P(),
            P(),
            P(None, None, "gx", "gy"),
            P(None, None, "gx", "gy"),
            P(None, None, None, "gx", "gy"),
        ),
        out_specs=(P(None, None, "gx", "gy"), P(None, None, "gx", "gy"), P(None, "gx", "gy")),
        check_vma=False,
    )
```

```python
import math

import jax
import jax.numpy as jnp
import numpy as np
from jax import lax
from jax.experimental import pallas as pl
from jax.experimental.pallas import tpu as pltpu
from jax.sharding import PartitionSpec as P

CY = 128
Z = 8
DZ = 4
STEPS = 4
TILE = 8
MATS = 4

courant = 0.5
sharpness = 4.0
threshold = 0.5

ROWS = 24
OWN = 16
SLOT = 48
KINDS = 3 * SLOT
LAYERS = KINDS + 24
EXTRA = LAYERS + 16
PLANES = 3 * Z

VM = pl.BlockSpec(memory_space=pltpu.VMEM)
ANY = pl.BlockSpec(memory_space=pl.ANY)


def vmem(*shape, dtype=jnp.float32):
    return pltpu.VMEM(shape, dtype)


def call(kernel, outs, ins, aliases=None, scratch=(), in_specs=None, out_specs=None):
    in_specs = in_specs or [VM] * len(ins)
    ins = [
        pltpu.with_memory_space_constraint(x, pltpu.VMEM if spec is VM else pltpu.HBM)
        for x, spec in zip(ins, in_specs)
    ]
    return pl.pallas_call(
        kernel,
        out_shape=outs,
        in_specs=in_specs,
        out_specs=out_specs or [VM] * len(outs),
        scratch_shapes=list(scratch),
        input_output_aliases=aliases or {},
        compiler_params=pltpu.CompilerParams(vmem_limit_bytes=32 * 1024 * 1024),
    )(*ins)


def lanes(rows):
    return lax.broadcasted_iota(jnp.int32, (rows, 128), 1)


def roll(x, by):
    return pltpu.roll(x, by % x.shape[1], 1)


def roll_rows(x, by):
    return pltpu.roll(x, by % x.shape[0], 0)


def sent(x, axis, by):
    size = lax.axis_size(axis)
    return lax.ppermute(x, axis, [(i, (i + by) % size) for i in range(size)])


def weight(offset, count, reach):
    ahead = np.mod(offset, count).astype(np.float64)
    behind = np.mod(-offset, count).astype(np.float64)
    return np.exp(-ahead / reach) + np.exp(-behind / reach)


def filter_constants(count, reach):
    source = np.arange(CY)
    strip = np.concatenate([np.arange(-4, 4), np.arange(CY - 4, CY + 4)])
    targets = np.concatenate([source, np.tile(strip, Z)])
    table = weight(targets[None, :] - source[:, None], count, reach)
    rows = np.zeros((8, 256))
    rows[0] = np.exp(-targets / reach)
    rows[1] = np.exp(targets / reach)
    rows[2, :CY] = np.exp(source / reach)
    rows[3, :CY] = np.exp(-source / reach)
    return np.concatenate([table, rows], 0).astype(np.float32)


def edge_window(planes):
    lane = lanes(planes[0].shape[0])
    width, by = 8, 16
    while len(planes) > 1:
        kept = ((lane + 4) & 127) < width
        planes = [
            jnp.where(kept, planes[i], roll(planes[i + 1], by)) for i in range(0, len(planes), 2)
        ]
        width, by = width + by, 2 * by
    return planes[0]


def edge_tiles(groups):
    lane = lanes(groups[0][0].shape[0])
    quarter = (lane >> 2) & 3
    found = [edge_window(planes) for planes in groups]

    def pick(a, b, c, d):
        return jnp.where(quarter < 2, jnp.where(quarter == 0, a, b), jnp.where(quarter == 2, c, d))

    left, right = [], []
    for i in (0, 4):
        one, two, three, four = found[i : i + 4]
        left.append(pick(one, roll(two, 4), roll(three, 8), roll(four, 12)))
        right.append(pick(roll(one, 4), roll(two, 8), roll(three, 12), roll(four, 16)))
    pairs = [
        jnp.where(quarter < 2, roll(found[i], 4), roll(found[i + 1], 12)) for i in range(0, 8, 2)
    ]
    return pairs, left, right


def density_planes(layers, cells):
    return [plane for layer in layers for plane in (layer, cells)]


def with_sums(tiles, layers):
    lane = lanes(layers[0].shape[0])
    column = lanes(1).astype(jnp.float32) * (1.0 / (4.0 * CY))
    rising, falling = jnp.exp(column), jnp.exp(-column)
    for l, layer in enumerate(layers):
        at = (2 * l + 1) * 16 + 12
        up = jnp.sum(layer * rising, axis=1, keepdims=True)
        down = jnp.sum(layer * falling, axis=1, keepdims=True)
        tiles = [
            jnp.where(lane == at, up, jnp.where(lane == at + 1, down, tile)) for tile in tiles
        ]
    return tiles


def pack_kernel(
    electric, magnetic, density, material, mask,
    to_prev, to_next, e_own, h_own, d_own, m_own, c_all,
    mask_v, sems,
):
    copies = []
    moved = [
        (electric, e_own), (magnetic, h_own), (density, d_own), (material, m_own), (mask, mask_v),
    ]
    for i, (source, target) in enumerate(moved):
        copy = pltpu.make_async_copy(source, target, sems.at[i])
        copy.start()
        copies.append(copy)
    copies[-1].wait()
    cells = cell_rows(mask_v[...])
    c_all[0:TILE, :] = jnp.broadcast_to(cells[0:1], (TILE, 128))
    c_all[TILE:OWN, :] = jnp.broadcast_to(cells[1:2], (TILE, 128))
    for copy in copies[:-1]:
        copy.wait()

    def e(channel, row):
        return e_own[pl.ds(channel * Z * OWN + row, Z, stride=OWN), :]

    def h(channel, row):
        return h_own[pl.ds(channel * Z * OWN + row, Z, stride=OWN), :]

    def ahead_part(row):
        part_y = h(1, row) + courant * (e(2, row + 1) - e(2, row))
        part_z = h(2, row) - courant * (e(1, row + 1) - e(1, row))
        return part_y, part_z

    for out, first, mask_row in ((to_next, OWN - 3, 1), (to_prev, 0, 0)):
        for slot in range(3):
            row, at = first + slot, slot * SLOT
            for channel in range(3):
                out[at + 8 * channel : at + 8 * channel + 8, :] = e(channel, row)
                out[at + 24 + 8 * channel : at + 32 + 8 * channel, :] = h(channel, row)
            out[KINDS + 8 * slot : KINDS + 8 * slot + 8, :] = (
                m_own[pl.ds(row, Z, stride=OWN), :].astype(jnp.float32)
            )
            out[LAYERS + 4 * slot : LAYERS + 4 * slot + 4, :] = (
                d_own[pl.ds(row, DZ, stride=OWN), :]
            )
        out[LAYERS + 12 : LAYERS + 16, :] = jnp.broadcast_to(
            cells[mask_row : mask_row + 1], (4, 128)
        )
    part_y, part_z = ahead_part(2)
    to_prev[2 * SLOT + 32 : 2 * SLOT + 40, :] = part_y
    to_prev[2 * SLOT + 40 : 2 * SLOT + 48, :] = part_z
    part_y, part_z = ahead_part(OWN - 4)
    to_next[EXTRA : EXTRA + 8, :] = e(0, OWN - 4)
    to_next[EXTRA + 8 : EXTRA + 16, :] = part_y
    to_next[EXTRA + 16 : EXTRA + 24, :] = part_z


def own_kernel(
    table_in, mtable_in, contrast_in, e_own, h_own, d_own, m_own, c_own,
    table, mtable, contrast, e_all, h_all, d_all, c_all, pairs_out, left_out, right_out,
    m_all, local, sems,
):
    copies = [
        pltpu.make_async_copy(source, target, sems.at[i])
        for i, (source, target) in enumerate(
            ((table_in, table), (mtable_in, mtable), (contrast_in, contrast))
        )
    ]
    for copy in copies:
        copy.start()
    c_all[0:OWN, :] = c_own[...]
    groups = []
    for source, target in ((e_own, e_all), (h_own, h_all)):
        for channel in range(3):
            planes = []
            for z in range(Z):
                p = channel * Z + z
                plane = source[p * OWN : (p + 1) * OWN, :]
                target[p * ROWS : p * ROWS + OWN, :] = plane
                planes.append(plane)
            groups.append(planes)
    planes = []
    for z in range(Z):
        plane = m_own[z * OWN : (z + 1) * OWN, :].astype(jnp.float32)
        m_all[z * ROWS : z * ROWS + OWN, :] = plane
        planes.append(plane)
    groups.append(planes)
    layers = []
    for l in range(DZ):
        layers.append(d_own[l * OWN : (l + 1) * OWN, :])
        d_all[l * ROWS : l * ROWS + OWN, :] = layers[l]
    groups.append(density_planes(layers, c_own[...]))
    pairs, left, right = edge_tiles(groups)
    left[1], right[1] = with_sums([left[1], right[1]], layers)
    for i in range(4):
        pairs_out[i * ROWS : i * ROWS + OWN, :] = pairs[i]
    for i in range(2):
        left_out[i * ROWS : i * ROWS + OWN, :] = left[i]
        right_out[i * ROWS : i * ROWS + OWN, :] = right[i]
    for copy in copies:
        copy.wait()
    smooth = jnp.dot(
        jnp.concatenate(layers, 0), table[0:128, :], precision=lax.Precision.HIGHEST,
        preferred_element_type=jnp.float32,
    )
    for l in range(DZ):
        local[l * ROWS : l * ROWS + OWN, :] = smooth[l * OWN : (l + 1) * OWN]


def unpack(got, first, e_all, h_all, d_all, c_all, m_all):
    for slot in range(3):
        at, row = slot * SLOT, first + slot
        for channel in range(3):
            where = pl.ds(channel * Z * ROWS + row, Z, stride=ROWS)
            e_all[where, :] = got[at + 8 * channel : at + 8 * channel + 8, :]
            h_all[where, :] = got[at + 24 + 8 * channel : at + 32 + 8 * channel, :]
        m_all[pl.ds(row, Z, stride=ROWS), :] = got[KINDS + 8 * slot : KINDS + 8 * slot + 8, :]
        d_all[pl.ds(row, DZ, stride=ROWS), :] = got[LAYERS + 4 * slot : LAYERS + 4 * slot + 4, :]
        c_all[row : row + 1, :] = got[LAYERS + 12 : LAYERS + 13, :]


def unpack_next(got, e_all, h_all, d_all, c_all, m_all):
    unpack(got, 16, e_all, h_all, d_all, c_all, m_all)
    zeros = jnp.zeros((Z, 128), jnp.float32)
    for channel in range(3):
        where = pl.ds(channel * Z * ROWS + 19, Z, stride=ROWS)
        e_all[where, :] = got[2 * SLOT + 8 * channel : 2 * SLOT + 8 * channel + 8, :]
        h_all[where, :] = zeros
    m_all[pl.ds(19, Z, stride=ROWS), :] = zeros
    d_all[pl.ds(19, DZ, stride=ROWS), :] = zeros[0:DZ]
    c_all[19:20, :] = zeros[0:1]


def unpack_prev(got, e_all, h_all, d_all, c_all, m_all):
    unpack(got, 21, e_all, h_all, d_all, c_all, m_all)
    zeros = jnp.zeros((Z, 128), jnp.float32)
    for channel in range(3):
        where = pl.ds(channel * Z * ROWS + 20, Z, stride=ROWS)
        extra = got[EXTRA + 8 * channel : EXTRA + 8 * channel + 8, :]
        if channel == 0:
            e_all[where, :] = extra
            h_all[where, :] = zeros
        else:
            e_all[where, :] = got[8 * channel : 8 * channel + 8, :]
            h_all[where, :] = extra
    m_all[pl.ds(20, Z, stride=ROWS), :] = zeros
    d_all[pl.ds(20, DZ, stride=ROWS), :] = zeros[0:DZ]
    c_all[20:21, :] = zeros[0:1]


def early_kernel(got, e_in, h_in, d_in, c_in, m_in, e_all, h_all, d_all, c_all, m_all):
    unpack_prev(got, e_all, h_all, d_all, c_all, m_all)


def halo_kernel(
    got, e_in, h_in, d_in, c_in, m_in, pairs_in, left_in, right_in, table,
    e_all, h_all, d_all, c_all, m_all, pairs_out, left_out, right_out, sums_out,
):
    unpack_next(got, e_all, h_all, d_all, c_all, m_all)

    groups = []
    for target in (e_all, h_all):
        for channel in range(3):
            groups.append(
                [target[(channel * Z + z) * ROWS + OWN : (channel * Z + z + 1) * ROWS, :] for z in range(Z)]
            )
    groups.append([m_all[z * ROWS + OWN : (z + 1) * ROWS, :] for z in range(Z)])
    layers = [d_all[l * ROWS + OWN : (l + 1) * ROWS, :] for l in range(DZ)]
    groups.append(density_planes(layers, c_all[OWN:ROWS, :]))
    pairs, left, right = edge_tiles(groups)
    left[1], right[1] = with_sums([left[1], right[1]], layers)
    for i in range(4):
        pairs_out[i * ROWS + OWN : (i + 1) * ROWS, :] = pairs[i]
    for i in range(2):
        left_out[i * ROWS + OWN : (i + 1) * ROWS, :] = left[i]
        right_out[i * ROWS + OWN : (i + 1) * ROWS, :] = right[i]
    place = lanes(8) & 15
    packed = left[1]
    packed = jnp.where(place < 12, roll(left_in[ROWS : ROWS + 8, :], -2), packed)
    sums_out[...] = jnp.where(place > 13, roll(left_in[ROWS + 8 : ROWS + OWN, :], 2), packed)


def background_kernel(m_all, d_all, mtable, table, local_in, background, local):
    smooth = jnp.dot(
        jnp.concatenate([d_all[l * ROWS + OWN : (l + 1) * ROWS, :] for l in range(DZ)], 0),
        table[0:128, :], precision=lax.Precision.HIGHEST, preferred_element_type=jnp.float32,
    )
    for l in range(DZ):
        local[l * ROWS + OWN : (l + 1) * ROWS, :] = smooth[l * 8 : (l + 1) * 8]
    entries = mtable[...]
    for z in range(Z):
        kind = m_all[z * ROWS : (z + 1) * ROWS, :]
        for channel in range(3):
            p = channel * Z + z
            background[p * ROWS : (p + 1) * ROWS, :] = looked_up(kind, entries, channel)


def looked_up(kind, entries, channel):
    one = [entries[channel : channel + 1, i : i + 1] for i in range(MATS)]
    return jnp.where(
        kind < 1.5, jnp.where(kind < 0.5, one[0], one[1]), jnp.where(kind < 2.5, one[2], one[3])
    )


def cell_rows(mask):
    spread = lax.broadcasted_iota(jnp.int32, (mask.shape[1], 128), 0) == (
        lanes(mask.shape[1]) // TILE
    )
    return jnp.dot(
        mask.astype(jnp.float32), spread.astype(jnp.float32), preferred_element_type=jnp.float32
    )


def project(values):
    base = math.tanh(sharpness * threshold)
    bottom = base + math.tanh(sharpness * (1.0 - threshold))
    level = jnp.tanh(sharpness * (values - threshold))
    return (base + level) * (1.0 / bottom), (sharpness / bottom) * (1.0 - level * level)


def plane_of(ref, channel, z, rows=ROWS):
    p = channel * Z + z
    return ref[p * ROWS : p * ROWS + rows, :]


def strip_of(ref, channel):
    return ref[channel * ROWS : (channel + 1) * ROWS, :]


def keep(ref, fields):
    for c, field in enumerate(fields):
        ref[c * ROWS : (c + 1) * ROWS, :] = field


def strip_magnetic(old, electric):
    lane = lanes(ROWS)
    ex, ey, ez = electric
    up_x = jnp.where(lane < 112, roll(ex, -16), 0.0)
    up_y = jnp.where(lane < 112, roll(ey, -16), 0.0)
    curls = (
        (roll(ez, -1) - ez) - (up_y - ey),
        (up_x - ex) - (roll_rows(ez, -1) - ez),
        (roll_rows(ey, -1) - ey) - (roll(ex, -1) - ex),
    )
    return [field - curl for field, curl in zip(old, curls)]


def strip_electric(old, magnetic, inverse):
    lane = lanes(ROWS)
    hx, hy, hz = magnetic
    down_x = jnp.where(lane >= 16, roll(hx, 16), 0.0)
    down_y = jnp.where(lane >= 16, roll(hy, 16), 0.0)
    curls = (
        (hz - roll(hz, 1)) - (hy - down_y),
        (hx - down_x) - (hz - roll_rows(hz, 1)),
        (hy - roll_rows(hy, 1)) - (hx - roll(hx, 1)),
    )
    return [old[c] + inverse[c] * curl for c, curl in enumerate(curls)]


def planes_magnetic(e_all, h_in, h_out, strip_e, scale=1.0):
    lane = lanes(ROWS)
    last, first = lane == 127, lane == 0
    zero = jnp.zeros((ROWS, 128), jnp.float32)
    mixed = jnp.where((lane & 15) == 12, strip_e[2], roll(strip_e[0], 1))
    ex_up, ey_up = plane_of(e_all, 0, 0), plane_of(e_all, 1, 0)
    for z in range(Z):
        ex, ey, ez = ex_up, ey_up, plane_of(e_all, 2, z)
        ex_up = plane_of(e_all, 0, z + 1) if z + 1 < Z else zero
        ey_up = plane_of(e_all, 1, z + 1) if z + 1 < Z else zero
        beyond = roll(mixed, 115 - 16 * z)
        dy_ez = jnp.where(last, beyond, roll(ez, -1)) - ez
        dy_ex = roll(jnp.where(first, beyond, ex), -1) - ex
        dx_ez = roll_rows(ez, -1) - ez
        dx_ey = roll_rows(ey, -1) - ey
        for channel, curl in enumerate(
            (dy_ez - (ey_up - ey), (ex_up - ex) - dx_ez, dx_ey - dy_ex)
        ):
            p = channel * Z + z
            old = plane_of(h_in, channel, z)
            h_out[p * ROWS : (p + 1) * ROWS, :] = (old if scale == 1.0 else scale * old) - curl


def planes_electric(e_all, h_all, inverse, strip_h, stored_at, contrast, gained, e_out, stride):
    lane = lanes(ROWS)
    last, first = lane == 127, lane == 0
    mixed = jnp.where((lane & 15) == 3, strip_h[2], roll(strip_h[0], -1))
    hx = hy = jnp.zeros((ROWS, 128), jnp.float32)
    for z in range(Z):
        hx_down, hy_down = hx, hy
        hx, hy, hz = (plane_of(h_all, c, z) for c in range(3))
        beyond = roll(mixed, -(16 * z + 3))
        dy_hz = hz - jnp.where(first, beyond, roll(hz, 1))
        dy_hx = hx - roll(jnp.where(last, beyond, hx), 1)
        dx_hz = hz - roll_rows(hz, 1)
        dx_hy = hy - roll_rows(hy, 1)
        total = jnp.zeros((OWN, 128), jnp.float32)
        for channel, curl in enumerate(
            (dy_hz - (hy - hy_down), (hx - hx_down) - dx_hz, dx_hy - dy_hx)
        ):
            p = channel * Z + z
            value = (
                plane_of(e_all, channel, z, stride)
                + plane_of(inverse, channel, z, stride) * curl[:stride]
            )
            e_out[p * stride : (p + 1) * stride, :] = value
            total = total + contrast[channel] * (value[:OWN] * stored_at(p).astype(jnp.float32))
        l = z // 2
        gained[l * OWN : (l + 1) * OWN, :] = gained[l * OWN : (l + 1) * OWN, :] + total


def lane_factor(m, count, reach):
    up, down = math.exp(-CY * m / reach), math.exp(-(count - CY * m) / reach)
    return jnp.where((lanes(ROWS) & 15) == 12, up, down)


def norm_of(count, reach):
    return 2.0 * float(np.sum(np.exp(-np.arange(count) / reach)))


def first_kernel(count, reach):
    devices = count // CY
    norm_total = norm_of(count, reach)

    def fix(delta):
        if delta == 0:
            return 1.0 - math.exp(-count / reach)
        return (
            math.exp(-delta / reach) + math.exp(-(count - delta) / reach)
            - math.exp(-(count + delta) / reach) - math.exp(delta / reach)
        )

    def kernel(from_right, from_left, pairs, e_all, h_in, mtable, h_all, se, sh, traits, sums):
        lane = lanes(ROWS)
        place = lane & 15
        odd = ((lane >> 4) & 1) == 1
        part = place >> 2
        got_left = [from_left[i * ROWS : (i + 1) * ROWS, :] for i in range(2)]
        got_right = [from_right[i * ROWS : (i + 1) * ROWS, :] for i in range(2)]

        def strip(index):
            tile, q = index // 4, index % 4
            pair = pairs[(index // 2) * ROWS : (index // 2 + 1) * ROWS, :]
            if index % 2 == 0:
                own_l, own_r = pair, roll(pair, 8)
            else:
                own_l, own_r = roll(pair, -8), pair
            outer = jnp.where(
                part == 0, roll(got_left[tile], -4 * q), roll(got_right[tile], 12 - 4 * q)
            )
            return jnp.where(part == 1, own_l, jnp.where(part == 2, own_r, outer))

        electric = [strip(c) for c in range(3)]
        keep(se, electric)
        keep(sh, strip_magnetic([strip(3 + c) * (1.0 / courant) for c in range(3)], electric))
        raw = strip(7)
        marks = jnp.where(odd, raw, roll(raw, -16))
        layers = jnp.where(odd, roll(raw, 16), raw)
        known = jnp.zeros((ROWS, 128), jnp.float32)
        for delta in range(4):
            value = fix(delta) * layers
            ahead = value if delta == 0 else roll(value, delta)
            behind = value if delta == 0 else roll(value, -delta)
            known = known + jnp.where(place >= 12 + delta, ahead, 0.0)
            known = known + jnp.where(place < 4 - delta, behind, 0.0)
        kind = strip(6)
        entries = mtable[...]
        keep(
            traits,
            [
                0.5 * layers + (0.5 / norm_total) * known,
                jnp.where((place & 2) == 2, marks, roll(marks, -2)),
            ]
            + [looked_up(kind, entries, c) for c in range(3)],
        )
        sums[...] = (
            lane_factor(1, count, reach) * got_left[1]
            + lane_factor(devices - 1, count, reach) * got_right[1]
        )
        planes_magnetic(e_all, h_in, h_all, electric, 1.0 / courant)

    return kernel


def step_kernel(count, reach, others):
    norm_total = norm_of(count, reach)

    def kernel(*refs):
        rest = refs[:others]
        (e_in, h_in, se_in, sh_in, traits, sums_in, d_all, c_all, background, local, table,
         contrast_in, forward,
         e_final, h_final, gradient, e_all, h_all, se, sh,
         inverse, si, gained) = refs[others:]
        contrast = [contrast_in[0:1, c : c + 1] for c in range(3)]
        lane = lanes(ROWS)
        layer_of = lane >> 5

        sums = sums_in[...]
        for i, other in enumerate(rest):
            packed = other[...]
            sums = sums + lane_factor(2 + i, count, reach) * jnp.concatenate(
                [roll(packed, 2), roll(packed, -2), packed], 0
            )
        strip_smooth = jnp.zeros((ROWS, 128), jnp.float32)
        designs = []
        cells = c_all[...]
        for l in range(DZ):
            at = (2 * l + 1) * 16 + 12
            up = jnp.broadcast_to(sums[:, at : at + 1], (ROWS, 128))
            down = jnp.broadcast_to(sums[:, at + 1 : at + 2], (ROWS, 128))
            both = local[l * ROWS : (l + 1) * ROWS, :]
            smooth = both[:, :128] + table[128:129, :128] * up + table[129:130, :128] * down
            far = both[:, 128:] + table[128:129, 128:] * up + table[129:130, 128:] * down
            strip_smooth = jnp.where(layer_of == l, far, strip_smooth)
            filtered = 0.5 * d_all[l * ROWS : (l + 1) * ROWS, :] + (0.5 / norm_total) * smooth
            projected, slope = project(filtered)
            designs.append(cells * projected)
            gradient[l * OWN : (l + 1) * OWN, :] = slope[:OWN] * cells[:OWN]
        projected, _ = project(strip_of(traits, 0) + (0.5 / norm_total) * strip_smooth)
        strip_design = strip_of(traits, 1) * projected
        keep(
            si,
            [courant * courant / (strip_of(traits, 2 + c) + strip_design * contrast[c]) for c in range(3)],
        )
        for z in range(Z):
            for channel in range(3):
                p = channel * Z + z
                inverse[p * ROWS : (p + 1) * ROWS, :] = courant * courant / (
                    background[p * ROWS : (p + 1) * ROWS, :] + designs[z // 2] * contrast[channel]
                )
        gained[...] = jnp.zeros_like(gained)

        def step(t, carry):
            strip_h = [strip_of(sh, c) for c in range(3)]
            strip_e = strip_electric(
                [strip_of(se, c) for c in range(3)], strip_h, [strip_of(si, c) for c in range(3)]
            )
            keep(se, strip_e)
            keep(sh, strip_magnetic(strip_h, strip_e))
            planes_electric(
                e_all, h_all, inverse, strip_h, lambda p: forward[t, p], contrast, gained,
                e_all, ROWS,
            )
            planes_magnetic(e_all, h_all, h_all, strip_e)
            return carry

        lax.fori_loop(0, STEPS - 1, step, 0)
        for p in range(PLANES):
            h_final[p * OWN : (p + 1) * OWN, :] = courant * h_all[p * ROWS : p * ROWS + OWN, :]
        planes_electric(
            e_all, h_all, inverse, [strip_of(sh, c) for c in range(3)],
            lambda p: forward[STEPS - 1, p], contrast, gained, e_final, OWN,
        )
        gradient[...] = gradient[...] * gained[...]

    return kernel


def body(
    density, tile_mask, material, material_table, contrast, electric, magnetic, forward_fields
):
    devices = lax.axis_size("gy")
    count = density.shape[2] * devices
    reach = 4.0 * CY
    constants = filter_constants(count, reach)

    to_prev, to_next, e_own, h_own, d_own, m_own, c_own = call(
        pack_kernel,
        [vmem(EXTRA, 128), vmem(EXTRA + 24, 128),
         vmem(PLANES * OWN, 128), vmem(PLANES * OWN, 128), vmem(DZ * OWN, 128),
         vmem(Z * OWN, 128, dtype=jnp.int32), vmem(OWN, 128)],
        [electric.reshape(PLANES * OWN, 128), magnetic.reshape(PLANES * OWN, 128),
         density.reshape(DZ * OWN, 128),
         material.reshape(Z * OWN, 128), tile_mask],
        scratch=[vmem(*tile_mask.shape, dtype=jnp.int32), pltpu.SemaphoreType.DMA((5,))],
        in_specs=[ANY] * 5,
    )
    from_prev = sent(to_next, "gx", 1)
    from_next = sent(to_prev, "gx", -1)
    table, mtable, contrasts, e_all, h_all, d_all, c_all, pairs, left, right, m_all, local = call(
        own_kernel,
        [vmem(*constants.shape), vmem(3, MATS), vmem(1, 3), vmem(PLANES * ROWS, 128), vmem(PLANES * ROWS, 128), vmem(DZ * ROWS, 128),
         vmem(ROWS, 128), vmem(4 * ROWS, 128), vmem(2 * ROWS, 128), vmem(2 * ROWS, 128), vmem(Z * ROWS, 128),
         vmem(DZ * ROWS, 256)],
        [constants, material_table, contrast.reshape(1, 3), e_own, h_own, d_own, m_own, c_own],
        scratch=[pltpu.SemaphoreType.DMA((3,))], in_specs=[ANY] * 3 + [VM] * 5,
    )
    fields = [vmem(PLANES * ROWS, 128), vmem(PLANES * ROWS, 128), vmem(DZ * ROWS, 128),
              vmem(ROWS, 128), vmem(Z * ROWS, 128)]
    e_all, h_all, d_all, c_all, m_all = call(
        early_kernel, fields, [from_prev, e_all, h_all, d_all, c_all, m_all],
        aliases={i + 1: i for i in range(5)},
    )
    e_all, h_all, d_all, c_all, m_all, pairs, left, right, sums = call(
        halo_kernel,
        [vmem(PLANES * ROWS, 128), vmem(PLANES * ROWS, 128), vmem(DZ * ROWS, 128),
         vmem(ROWS, 128), vmem(Z * ROWS, 128), vmem(4 * ROWS, 128),
         vmem(2 * ROWS, 128), vmem(2 * ROWS, 128), vmem(8, 128)],
        [from_next, e_all, h_all, d_all, c_all, m_all, pairs, left, right, table],
        aliases={i + 1: i for i in range(8)},
    )
    from_left = sent(right, "gy", 1)
    from_right = sent(left, "gy", -1)
    rest = [sent(sums, "gy", m) for m in range(2, devices - 1)]
    background, local = call(
        background_kernel, [vmem(PLANES * ROWS, 128), vmem(DZ * ROWS, 256)],
        [m_all, d_all, mtable, table, local], aliases={4: 1},
    )
    h_all, se, sh, traits, sums = call(
        first_kernel(count, reach),
        [vmem(PLANES * ROWS, 128), vmem(3 * ROWS, 128), vmem(3 * ROWS, 128),
         vmem(5 * ROWS, 128), vmem(ROWS, 128)],
        [from_right, from_left, pairs, e_all, h_all, mtable],
        aliases={4: 0},
    )
    at = len(rest)
    operands = rest + [
        e_all, h_all, se, sh, traits, sums, d_all, c_all, background, local, table,
        contrasts, forward_fields.reshape(STEPS, PLANES, OWN, 128),
    ]
    outs = call(
        step_kernel(count, reach, at),
        [jax.ShapeDtypeStruct((PLANES * OWN, 128), jnp.float32),
         jax.ShapeDtypeStruct((PLANES * OWN, 128), jnp.float32),
         jax.ShapeDtypeStruct((DZ * OWN, 128), jnp.float32),
         vmem(PLANES * ROWS, 128), vmem(PLANES * ROWS, 128), vmem(3 * ROWS, 128),
         vmem(3 * ROWS, 128)],
        operands,
        aliases={at: 3, at + 1: 4, at + 2: 5, at + 3: 6},
        scratch=[vmem(PLANES * ROWS, 128), vmem(3 * ROWS, 128), vmem(DZ * OWN, 128),
                 ],
    )
    return (
        outs[0].reshape(electric.shape), outs[1].reshape(magnetic.shape),
        outs[2].reshape(density.shape),
    )


def solution(mesh):
    return jax.shard_map(
        body,
        mesh=mesh,
        in_specs=(
            P(None, "gx", "gy"),
            P("gx", "gy"),
            P(None, "gx", "gy"),
            P(),
            P(),
            P(None, None, "gx", "gy"),
            P(None, None, "gx", "gy"),
            P(None, None, None, "gx", "gy"),
        ),
        out_specs=(P(None, None, "gx", "gy"), P(None, None, "gx", "gy"), P(None, "gx", "gy")),
        check_vma=False,
    )
```

```python
import math

import jax
import jax.numpy as jnp
import numpy as np
from jax import lax
from jax.experimental import pallas as pl
from jax.experimental.pallas import tpu as pltpu
from jax.sharding import PartitionSpec as P

CY = 128
Z = 8
DZ = 4
STEPS = 4
TILE = 8
MATS = 4

courant = 0.5
sharpness = 4.0
threshold = 0.5

ROWS = 24
OWN = 16
SLOT = 48
KINDS = 3 * SLOT
LAYERS = KINDS + 24
EXTRA = LAYERS + 16
PLANES = 3 * Z

VM = pl.BlockSpec(memory_space=pltpu.VMEM)
ANY = pl.BlockSpec(memory_space=pl.ANY)


def vmem(*shape, dtype=jnp.float32):
    return pltpu.VMEM(shape, dtype)


def call(kernel, outs, ins, aliases=None, scratch=(), in_specs=None, out_specs=None):
    in_specs = in_specs or [VM] * len(ins)
    ins = [
        pltpu.with_memory_space_constraint(x, pltpu.VMEM if spec is VM else pltpu.HBM)
        for x, spec in zip(ins, in_specs)
    ]
    return pl.pallas_call(
        kernel,
        out_shape=outs,
        in_specs=in_specs,
        out_specs=out_specs or [VM] * len(outs),
        scratch_shapes=list(scratch),
        input_output_aliases=aliases or {},
        compiler_params=pltpu.CompilerParams(vmem_limit_bytes=32 * 1024 * 1024),
    )(*ins)


def lanes(rows):
    return lax.broadcasted_iota(jnp.int32, (rows, 128), 1)


def roll(x, by):
    return pltpu.roll(x, by % x.shape[1], 1)


def roll_rows(x, by):
    return pltpu.roll(x, by % x.shape[0], 0)


def sent(x, axis, by):
    size = lax.axis_size(axis)
    return lax.ppermute(x, axis, [(i, (i + by) % size) for i in range(size)])


def weight(offset, count, reach):
    ahead = np.mod(offset, count).astype(np.float64)
    behind = np.mod(-offset, count).astype(np.float64)
    return np.exp(-ahead / reach) + np.exp(-behind / reach)


def filter_constants(count, reach):
    source = np.arange(CY)
    strip = np.concatenate([np.arange(-4, 4), np.arange(CY - 4, CY + 4)])
    targets = np.concatenate([source, np.tile(strip, Z)])
    table = weight(targets[None, :] - source[:, None], count, reach)
    rows = np.zeros((8, 256))
    rows[0] = np.exp(-targets / reach)
    rows[1] = np.exp(targets / reach)
    rows[2, :CY] = np.exp(source / reach)
    rows[3, :CY] = np.exp(-source / reach)
    return np.concatenate([table, rows], 0).astype(np.float32)


def edge_window(planes):
    lane = lanes(planes[0].shape[0])
    width, by = 8, 16
    while len(planes) > 1:
        kept = ((lane + 4) & 127) < width
        planes = [
            jnp.where(kept, planes[i], roll(planes[i + 1], by)) for i in range(0, len(planes), 2)
        ]
        width, by = width + by, 2 * by
    return planes[0]


def edge_tiles(groups):
    lane = lanes(groups[0][0].shape[0])
    quarter = (lane >> 2) & 3
    found = [edge_window(planes) for planes in groups]

    def pick(a, b, c, d):
        return jnp.where(quarter < 2, jnp.where(quarter == 0, a, b), jnp.where(quarter == 2, c, d))

    left, right = [], []
    for i in (0, 4):
        one, two, three, four = found[i : i + 4]
        left.append(pick(one, roll(two, 4), roll(three, 8), roll(four, 12)))
        right.append(pick(roll(one, 4), roll(two, 8), roll(three, 12), roll(four, 16)))
    pairs = [
        jnp.where(quarter < 2, roll(found[i], 4), roll(found[i + 1], 12)) for i in range(0, 8, 2)
    ]
    return pairs, left, right


def density_planes(layers, cells):
    return [plane for layer in layers for plane in (layer, cells)]


def with_sums(tiles, layers):
    lane = lanes(layers[0].shape[0])
    column = lanes(1).astype(jnp.float32) * (1.0 / (4.0 * CY))
    rising, falling = jnp.exp(column), jnp.exp(-column)
    for l, layer in enumerate(layers):
        at = (2 * l + 1) * 16 + 12
        up = jnp.sum(layer * rising, axis=1, keepdims=True)
        down = jnp.sum(layer * falling, axis=1, keepdims=True)
        tiles = [
            jnp.where(lane == at, up, jnp.where(lane == at + 1, down, tile)) for tile in tiles
        ]
    return tiles


def pack_kernel(
    electric, magnetic, density, material, mask,
    to_prev, to_next, e_own, h_own, d_own, m_own, c_all,
    mask_v, sems,
):
    copies = []
    moved = [
        (electric, e_own), (magnetic, h_own), (density, d_own), (material, m_own), (mask, mask_v),
    ]
    for i, (source, target) in enumerate(moved):
        copy = pltpu.make_async_copy(source, target, sems.at[i])
        copy.start()
        copies.append(copy)
    copies[-1].wait()
    cells = cell_rows(mask_v[...])
    c_all[0:TILE, :] = jnp.broadcast_to(cells[0:1], (TILE, 128))
    c_all[TILE:OWN, :] = jnp.broadcast_to(cells[1:2], (TILE, 128))
    for copy in copies[:-1]:
        copy.wait()

    def e(channel, row):
        return e_own[pl.ds(channel * Z * OWN + row, Z, stride=OWN), :]

    def h(channel, row):
        return h_own[pl.ds(channel * Z * OWN + row, Z, stride=OWN), :]

    def ahead_part(row):
        part_y = h(1, row) + courant * (e(2, row + 1) - e(2, row))
        part_z = h(2, row) - courant * (e(1, row + 1) - e(1, row))
        return part_y, part_z

    for out, first, mask_row in ((to_next, OWN - 3, 1), (to_prev, 0, 0)):
        for slot in range(3):
            row, at = first + slot, slot * SLOT
            for channel in range(3):
                out[at + 8 * channel : at + 8 * channel + 8, :] = e(channel, row)
                out[at + 24 + 8 * channel : at + 32 + 8 * channel, :] = h(channel, row)
            out[KINDS + 8 * slot : KINDS + 8 * slot + 8, :] = (
                m_own[pl.ds(row, Z, stride=OWN), :].astype(jnp.float32)
            )
            out[LAYERS + 4 * slot : LAYERS + 4 * slot + 4, :] = (
                d_own[pl.ds(row, DZ, stride=OWN), :]
            )
        out[LAYERS + 12 : LAYERS + 16, :] = jnp.broadcast_to(
            cells[mask_row : mask_row + 1], (4, 128)
        )
    part_y, part_z = ahead_part(2)
    to_prev[2 * SLOT + 32 : 2 * SLOT + 40, :] = part_y
    to_prev[2 * SLOT + 40 : 2 * SLOT + 48, :] = part_z
    part_y, part_z = ahead_part(OWN - 4)
    to_next[EXTRA : EXTRA + 8, :] = e(0, OWN - 4)
    to_next[EXTRA + 8 : EXTRA + 16, :] = part_y
    to_next[EXTRA + 16 : EXTRA + 24, :] = part_z


def own_kernel(
    table_in, mtable_in, contrast_in, e_own, h_own, d_own, m_own, c_own,
    table, mtable, contrast, e_all, h_all, d_all, c_all, pairs_out, left_out, right_out,
    m_all, local, sems,
):
    copies = [
        pltpu.make_async_copy(source, target, sems.at[i])
        for i, (source, target) in enumerate(
            ((table_in, table), (mtable_in, mtable), (contrast_in, contrast))
        )
    ]
    for copy in copies:
        copy.start()
    c_all[0:OWN, :] = c_own[...]
    groups = []
    for source, target in ((e_own, e_all), (h_own, h_all)):
        for channel in range(3):
            planes = []
            for z in range(Z):
                p = channel * Z + z
                plane = source[p * OWN : (p + 1) * OWN, :]
                target[p * ROWS : p * ROWS + OWN, :] = plane
                planes.append(plane)
            groups.append(planes)
    planes = []
    for z in range(Z):
        plane = m_own[z * OWN : (z + 1) * OWN, :].astype(jnp.float32)
        m_all[z * ROWS : z * ROWS + OWN, :] = plane
        planes.append(plane)
    groups.append(planes)
    layers = []
    for l in range(DZ):
        layers.append(d_own[l * OWN : (l + 1) * OWN, :])
        d_all[l * ROWS : l * ROWS + OWN, :] = layers[l]
    groups.append(density_planes(layers, c_own[...]))
    pairs, left, right = edge_tiles(groups)
    left[1], right[1] = with_sums([left[1], right[1]], layers)
    for i in range(4):
        pairs_out[i * ROWS : i * ROWS + OWN, :] = pairs[i]
    for i in range(2):
        left_out[i * ROWS : i * ROWS + OWN, :] = left[i]
        right_out[i * ROWS : i * ROWS + OWN, :] = right[i]
    for copy in copies:
        copy.wait()
    smooth = jnp.dot(
        jnp.concatenate(layers, 0), table[0:128, :], precision=lax.Precision.HIGHEST,
        preferred_element_type=jnp.float32,
    )
    for l in range(DZ):
        local[l * ROWS : l * ROWS + OWN, :] = smooth[l * OWN : (l + 1) * OWN]


def unpack(got, first, e_all, h_all, d_all, c_all, m_all):
    for slot in range(3):
        at, row = slot * SLOT, first + slot
        for channel in range(3):
            where = pl.ds(channel * Z * ROWS + row, Z, stride=ROWS)
            e_all[where, :] = got[at + 8 * channel : at + 8 * channel + 8, :]
            h_all[where, :] = got[at + 24 + 8 * channel : at + 32 + 8 * channel, :]
        m_all[pl.ds(row, Z, stride=ROWS), :] = got[KINDS + 8 * slot : KINDS + 8 * slot + 8, :]
        d_all[pl.ds(row, DZ, stride=ROWS), :] = got[LAYERS + 4 * slot : LAYERS + 4 * slot + 4, :]
        c_all[row : row + 1, :] = got[LAYERS + 12 : LAYERS + 13, :]


def unpack_next(got, e_all, h_all, d_all, c_all, m_all):
    unpack(got, 16, e_all, h_all, d_all, c_all, m_all)
    zeros = jnp.zeros((Z, 128), jnp.float32)
    for channel in range(3):
        where = pl.ds(channel * Z * ROWS + 19, Z, stride=ROWS)
        e_all[where, :] = got[2 * SLOT + 8 * channel : 2 * SLOT + 8 * channel + 8, :]
        h_all[where, :] = zeros
    m_all[pl.ds(19, Z, stride=ROWS), :] = zeros
    d_all[pl.ds(19, DZ, stride=ROWS), :] = zeros[0:DZ]
    c_all[19:20, :] = zeros[0:1]


def unpack_prev(got, e_all, h_all, d_all, c_all, m_all):
    unpack(got, 21, e_all, h_all, d_all, c_all, m_all)
    zeros = jnp.zeros((Z, 128), jnp.float32)
    for channel in range(3):
        where = pl.ds(channel * Z * ROWS + 20, Z, stride=ROWS)
        extra = got[EXTRA + 8 * channel : EXTRA + 8 * channel + 8, :]
        if channel == 0:
            e_all[where, :] = extra
            h_all[where, :] = zeros
        else:
            e_all[where, :] = got[8 * channel : 8 * channel + 8, :]
            h_all[where, :] = extra
    m_all[pl.ds(20, Z, stride=ROWS), :] = zeros
    d_all[pl.ds(20, DZ, stride=ROWS), :] = zeros[0:DZ]
    c_all[20:21, :] = zeros[0:1]


def early_kernel(got, e_in, h_in, d_in, c_in, m_in, e_all, h_all, d_all, c_all, m_all):
    unpack_prev(got, e_all, h_all, d_all, c_all, m_all)


def halo_kernel(
    got, e_in, h_in, d_in, c_in, m_in, pairs_in, left_in, right_in, table,
    e_all, h_all, d_all, c_all, m_all, pairs_out, left_out, right_out, sums_out,
):
    unpack_next(got, e_all, h_all, d_all, c_all, m_all)

    groups = []
    for target in (e_all, h_all):
        for channel in range(3):
            groups.append(
                [target[(channel * Z + z) * ROWS + OWN : (channel * Z + z + 1) * ROWS, :] for z in range(Z)]
            )
    groups.append([m_all[z * ROWS + OWN : (z + 1) * ROWS, :] for z in range(Z)])
    layers = [d_all[l * ROWS + OWN : (l + 1) * ROWS, :] for l in range(DZ)]
    groups.append(density_planes(layers, c_all[OWN:ROWS, :]))
    pairs, left, right = edge_tiles(groups)
    left[1], right[1] = with_sums([left[1], right[1]], layers)
    for i in range(4):
        pairs_out[i * ROWS + OWN : (i + 1) * ROWS, :] = pairs[i]
    for i in range(2):
        left_out[i * ROWS + OWN : (i + 1) * ROWS, :] = left[i]
        right_out[i * ROWS + OWN : (i + 1) * ROWS, :] = right[i]
    place = lanes(8) & 15
    packed = left[1]
    packed = jnp.where(place < 12, roll(left_in[ROWS : ROWS + 8, :], -2), packed)
    sums_out[...] = jnp.where(place > 13, roll(left_in[ROWS + 8 : ROWS + OWN, :], 2), packed)


def background_kernel(
    forward_in, contrast_in, m_all, d_all, mtable, table, local_in,
    background, local, forward, fetched, sem,
):
    copy = pltpu.make_async_copy(forward_in, fetched, sem)
    copy.start()
    smooth = jnp.dot(
        jnp.concatenate([d_all[l * ROWS + OWN : (l + 1) * ROWS, :] for l in range(DZ)], 0),
        table[0:128, :], precision=lax.Precision.HIGHEST, preferred_element_type=jnp.float32,
    )
    for l in range(DZ):
        local[l * ROWS + OWN : (l + 1) * ROWS, :] = smooth[l * 8 : (l + 1) * 8]
    entries = mtable[...]
    for z in range(Z):
        kind = m_all[z * ROWS : (z + 1) * ROWS, :]
        for channel in range(3):
            p = channel * Z + z
            background[p * ROWS : (p + 1) * ROWS, :] = looked_up(kind, entries, channel)
    contrast = [contrast_in[0:1, c : c + 1] for c in range(3)]
    copy.wait()

    def scale(t, carry):
        for p in range(PLANES):
            forward[t, p] = contrast[p // Z] * fetched[t, p].astype(jnp.float32)
        return carry

    lax.fori_loop(0, STEPS, scale, 0)


def looked_up(kind, entries, channel):
    one = [entries[channel : channel + 1, i : i + 1] for i in range(MATS)]
    return jnp.where(
        kind < 1.5, jnp.where(kind < 0.5, one[0], one[1]), jnp.where(kind < 2.5, one[2], one[3])
    )


def cell_rows(mask):
    spread = lax.broadcasted_iota(jnp.int32, (mask.shape[1], 128), 0) == (
        lanes(mask.shape[1]) // TILE
    )
    return jnp.dot(
        mask.astype(jnp.float32), spread.astype(jnp.float32), preferred_element_type=jnp.float32
    )


def project(values):
    base = math.tanh(sharpness * threshold)
    bottom = base + math.tanh(sharpness * (1.0 - threshold))
    level = jnp.tanh(sharpness * (values - threshold))
    return (base + level) * (1.0 / bottom), (sharpness / bottom) * (1.0 - level * level)


def plane_of(ref, channel, z, rows=ROWS):
    p = channel * Z + z
    return ref[p * ROWS : p * ROWS + rows, :]


def strip_of(ref, channel):
    return ref[channel * ROWS : (channel + 1) * ROWS, :]


def keep(ref, fields):
    for c, field in enumerate(fields):
        ref[c * ROWS : (c + 1) * ROWS, :] = field


def strip_magnetic(old, electric):
    lane = lanes(ROWS)
    ex, ey, ez = electric
    up_x = jnp.where(lane < 112, roll(ex, -16), 0.0)
    up_y = jnp.where(lane < 112, roll(ey, -16), 0.0)
    curls = (
        (roll(ez, -1) - ez) - (up_y - ey),
        (up_x - ex) - (roll_rows(ez, -1) - ez),
        (roll_rows(ey, -1) - ey) - (roll(ex, -1) - ex),
    )
    return [field - curl for field, curl in zip(old, curls)]


def strip_electric(old, magnetic, inverse):
    lane = lanes(ROWS)
    hx, hy, hz = magnetic
    down_x = jnp.where(lane >= 16, roll(hx, 16), 0.0)
    down_y = jnp.where(lane >= 16, roll(hy, 16), 0.0)
    curls = (
        (hz - roll(hz, 1)) - (hy - down_y),
        (hx - down_x) - (hz - roll_rows(hz, 1)),
        (hy - roll_rows(hy, 1)) - (hx - roll(hx, 1)),
    )
    return [old[c] + inverse[c] * curl for c, curl in enumerate(curls)]


def planes_magnetic(e_all, h_in, h_out, strip_e, scale=1.0):
    lane = lanes(ROWS)
    last, first = lane == 127, lane == 0
    zero = jnp.zeros((ROWS, 128), jnp.float32)
    mixed = jnp.where((lane & 15) == 12, strip_e[2], roll(strip_e[0], 1))
    ex_up, ey_up = plane_of(e_all, 0, 0), plane_of(e_all, 1, 0)
    for z in range(Z):
        ex, ey, ez = ex_up, ey_up, plane_of(e_all, 2, z)
        ex_up = plane_of(e_all, 0, z + 1) if z + 1 < Z else zero
        ey_up = plane_of(e_all, 1, z + 1) if z + 1 < Z else zero
        beyond = roll(mixed, 115 - 16 * z)
        dy_ez = jnp.where(last, beyond, roll(ez, -1)) - ez
        dy_ex = roll(jnp.where(first, beyond, ex), -1) - ex
        dx_ez = roll_rows(ez, -1) - ez
        dx_ey = roll_rows(ey, -1) - ey
        for channel, curl in enumerate(
            (dy_ez - (ey_up - ey), (ex_up - ex) - dx_ez, dx_ey - dy_ex)
        ):
            p = channel * Z + z
            old = plane_of(h_in, channel, z)
            h_out[p * ROWS : (p + 1) * ROWS, :] = (old if scale == 1.0 else scale * old) - curl


def planes_electric(e_all, h_all, inverse, strip_h, stored_at, gained, e_out, stride):
    lane = lanes(ROWS)
    last, first = lane == 127, lane == 0
    mixed = jnp.where((lane & 15) == 3, strip_h[2], roll(strip_h[0], -1))
    hx = hy = jnp.zeros((ROWS, 128), jnp.float32)
    for z in range(Z):
        hx_down, hy_down = hx, hy
        hx, hy, hz = (plane_of(h_all, c, z) for c in range(3))
        beyond = roll(mixed, -(16 * z + 3))
        dy_hz = hz - jnp.where(first, beyond, roll(hz, 1))
        dy_hx = hx - roll(jnp.where(last, beyond, hx), 1)
        dx_hz = hz - roll_rows(hz, 1)
        dx_hy = hy - roll_rows(hy, 1)
        total = jnp.zeros((OWN, 128), jnp.float32)
        for channel, curl in enumerate(
            (dy_hz - (hy - hy_down), (hx - hx_down) - dx_hz, dx_hy - dy_hx)
        ):
            p = channel * Z + z
            value = (
                plane_of(e_all, channel, z, stride)
                + plane_of(inverse, channel, z, stride) * curl[:stride]
            )
            e_out[p * stride : (p + 1) * stride, :] = value
            total = total + value[:OWN] * stored_at(p)
        l = z // 2
        gained[l * OWN : (l + 1) * OWN, :] = gained[l * OWN : (l + 1) * OWN, :] + total


def lane_factor(m, count, reach):
    up, down = math.exp(-CY * m / reach), math.exp(-(count - CY * m) / reach)
    return jnp.where((lanes(ROWS) & 15) == 12, up, down)


def norm_of(count, reach):
    return 2.0 * float(np.sum(np.exp(-np.arange(count) / reach)))


def first_kernel(count, reach):
    devices = count // CY
    norm_total = norm_of(count, reach)

    def fix(delta):
        if delta == 0:
            return 1.0 - math.exp(-count / reach)
        return (
            math.exp(-delta / reach) + math.exp(-(count - delta) / reach)
            - math.exp(-(count + delta) / reach) - math.exp(delta / reach)
        )

    def kernel(from_right, from_left, pairs, e_all, h_in, mtable, h_all, se, sh, traits, sums):
        lane = lanes(ROWS)
        place = lane & 15
        odd = ((lane >> 4) & 1) == 1
        part = place >> 2
        got_left = [from_left[i * ROWS : (i + 1) * ROWS, :] for i in range(2)]
        got_right = [from_right[i * ROWS : (i + 1) * ROWS, :] for i in range(2)]

        def strip(index):
            tile, q = index // 4, index % 4
            pair = pairs[(index // 2) * ROWS : (index // 2 + 1) * ROWS, :]
            if index % 2 == 0:
                own_l, own_r = pair, roll(pair, 8)
            else:
                own_l, own_r = roll(pair, -8), pair
            outer = jnp.where(
                part == 0, roll(got_left[tile], -4 * q), roll(got_right[tile], 12 - 4 * q)
            )
            return jnp.where(part == 1, own_l, jnp.where(part == 2, own_r, outer))

        electric = [strip(c) for c in range(3)]
        keep(se, electric)
        keep(sh, strip_magnetic([strip(3 + c) * (1.0 / courant) for c in range(3)], electric))
        raw = strip(7)
        marks = jnp.where(odd, raw, roll(raw, -16))
        layers = jnp.where(odd, roll(raw, 16), raw)
        known = jnp.zeros((ROWS, 128), jnp.float32)
        for delta in range(4):
            value = fix(delta) * layers
            ahead = value if delta == 0 else roll(value, delta)
            behind = value if delta == 0 else roll(value, -delta)
            known = known + jnp.where(place >= 12 + delta, ahead, 0.0)
            known = known + jnp.where(place < 4 - delta, behind, 0.0)
        kind = strip(6)
        entries = mtable[...]
        keep(
            traits,
            [
                0.5 * layers + (0.5 / norm_total) * known,
                jnp.where((place & 2) == 2, marks, roll(marks, -2)),
            ]
            + [looked_up(kind, entries, c) for c in range(3)],
        )
        sums[...] = (
            lane_factor(1, count, reach) * got_left[1]
            + lane_factor(devices - 1, count, reach) * got_right[1]
        )
        planes_magnetic(e_all, h_in, h_all, electric, 1.0 / courant)

    return kernel


def step_kernel(count, reach, others):
    norm_total = norm_of(count, reach)

    def kernel(*refs):
        rest = refs[:others]
        (e_in, h_in, se_in, sh_in, traits, sums_in, d_all, c_all, background, local, table,
         contrast_in, forward,
         e_final, h_final, gradient, e_all, h_all, se, sh,
         inverse, si, gained) = refs[others:]
        contrast = [contrast_in[0:1, c : c + 1] for c in range(3)]
        lane = lanes(ROWS)
        layer_of = lane >> 5

        sums = sums_in[...]
        for i, other in enumerate(rest):
            packed = other[...]
            sums = sums + lane_factor(2 + i, count, reach) * jnp.concatenate(
                [roll(packed, 2), roll(packed, -2), packed], 0
            )
        strip_smooth = jnp.zeros((ROWS, 128), jnp.float32)
        designs = []
        cells = c_all[...]
        for l in range(DZ):
            at = (2 * l + 1) * 16 + 12
            up = jnp.broadcast_to(sums[:, at : at + 1], (ROWS, 128))
            down = jnp.broadcast_to(sums[:, at + 1 : at + 2], (ROWS, 128))
            both = local[l * ROWS : (l + 1) * ROWS, :]
            smooth = both[:, :128] + table[128:129, :128] * up + table[129:130, :128] * down
            far = both[:, 128:] + table[128:129, 128:] * up + table[129:130, 128:] * down
            strip_smooth = jnp.where(layer_of == l, far, strip_smooth)
            filtered = 0.5 * d_all[l * ROWS : (l + 1) * ROWS, :] + (0.5 / norm_total) * smooth
            projected, slope = project(filtered)
            designs.append(cells * projected)
            gradient[l * OWN : (l + 1) * OWN, :] = slope[:OWN] * cells[:OWN]
        projected, _ = project(strip_of(traits, 0) + (0.5 / norm_total) * strip_smooth)
        strip_design = strip_of(traits, 1) * projected
        keep(
            si,
            [courant * courant / (strip_of(traits, 2 + c) + strip_design * contrast[c]) for c in range(3)],
        )
        for z in range(Z):
            for channel in range(3):
                p = channel * Z + z
                inverse[p * ROWS : (p + 1) * ROWS, :] = courant * courant / (
                    background[p * ROWS : (p + 1) * ROWS, :] + designs[z // 2] * contrast[channel]
                )
        gained[...] = jnp.zeros_like(gained)

        def step(t, carry):
            strip_h = [strip_of(sh, c) for c in range(3)]
            planes_electric(
                e_all, h_all, inverse, strip_h, lambda p: forward[t, p], gained,
                e_all, ROWS,
            )
            strip_e = strip_electric(
                [strip_of(se, c) for c in range(3)], strip_h, [strip_of(si, c) for c in range(3)]
            )
            keep(se, strip_e)
            planes_magnetic(e_all, h_all, h_all, strip_e)
            keep(sh, strip_magnetic(strip_h, strip_e))
            return carry

        lax.fori_loop(0, STEPS - 1, step, 0)
        for p in range(PLANES):
            h_final[p * OWN : (p + 1) * OWN, :] = courant * h_all[p * ROWS : p * ROWS + OWN, :]
        planes_electric(
            e_all, h_all, inverse, [strip_of(sh, c) for c in range(3)],
            lambda p: forward[STEPS - 1, p], gained, e_final, OWN,
        )
        gradient[...] = gradient[...] * gained[...]

    return kernel


def body(
    density, tile_mask, material, material_table, contrast, electric, magnetic, forward_fields
):
    devices = lax.axis_size("gy")
    count = density.shape[2] * devices
    reach = 4.0 * CY
    constants = filter_constants(count, reach)

    to_prev, to_next, e_own, h_own, d_own, m_own, c_own = call(
        pack_kernel,
        [vmem(EXTRA, 128), vmem(EXTRA + 24, 128),
         vmem(PLANES * OWN, 128), vmem(PLANES * OWN, 128), vmem(DZ * OWN, 128),
         vmem(Z * OWN, 128, dtype=jnp.int32), vmem(OWN, 128)],
        [electric.reshape(PLANES * OWN, 128), magnetic.reshape(PLANES * OWN, 128),
         density.reshape(DZ * OWN, 128),
         material.reshape(Z * OWN, 128), tile_mask],
        scratch=[vmem(*tile_mask.shape, dtype=jnp.int32), pltpu.SemaphoreType.DMA((5,))],
        in_specs=[ANY] * 5,
    )
    from_prev = sent(to_next, "gx", 1)
    from_next = sent(to_prev, "gx", -1)
    table, mtable, contrasts, e_all, h_all, d_all, c_all, pairs, left, right, m_all, local = call(
        own_kernel,
        [vmem(*constants.shape), vmem(3, MATS), vmem(1, 3), vmem(PLANES * ROWS, 128), vmem(PLANES * ROWS, 128), vmem(DZ * ROWS, 128),
         vmem(ROWS, 128), vmem(4 * ROWS, 128), vmem(2 * ROWS, 128), vmem(2 * ROWS, 128), vmem(Z * ROWS, 128),
         vmem(DZ * ROWS, 256)],
        [constants, material_table, contrast.reshape(1, 3), e_own, h_own, d_own, m_own, c_own],
        scratch=[pltpu.SemaphoreType.DMA((3,))], in_specs=[ANY] * 3 + [VM] * 5,
    )
    fields = [vmem(PLANES * ROWS, 128), vmem(PLANES * ROWS, 128), vmem(DZ * ROWS, 128),
              vmem(ROWS, 128), vmem(Z * ROWS, 128)]
    e_all, h_all, d_all, c_all, m_all = call(
        early_kernel, fields, [from_prev, e_all, h_all, d_all, c_all, m_all],
        aliases={i + 1: i for i in range(5)},
    )
    e_all, h_all, d_all, c_all, m_all, pairs, left, right, sums = call(
        halo_kernel,
        [vmem(PLANES * ROWS, 128), vmem(PLANES * ROWS, 128), vmem(DZ * ROWS, 128),
         vmem(ROWS, 128), vmem(Z * ROWS, 128), vmem(4 * ROWS, 128),
         vmem(2 * ROWS, 128), vmem(2 * ROWS, 128), vmem(8, 128)],
        [from_next, e_all, h_all, d_all, c_all, m_all, pairs, left, right, table],
        aliases={i + 1: i for i in range(8)},
    )
    from_left = sent(right, "gy", 1)
    from_right = sent(left, "gy", -1)
    rest = [sent(sums, "gy", m) for m in range(2, devices - 1)]
    background, local, forward = call(
        background_kernel,
        [vmem(PLANES * ROWS, 128), vmem(DZ * ROWS, 256), vmem(STEPS, PLANES, OWN, 128)],
        [forward_fields.reshape(STEPS, PLANES, OWN, 128), contrasts, m_all, d_all, mtable, table,
         local],
        aliases={6: 1},
        scratch=[vmem(STEPS, PLANES, OWN, 128, dtype=jnp.bfloat16), pltpu.SemaphoreType.DMA],
        in_specs=[ANY] + [VM] * 6,
    )
    h_all, se, sh, traits, sums = call(
        first_kernel(count, reach),
        [vmem(PLANES * ROWS, 128), vmem(3 * ROWS, 128), vmem(3 * ROWS, 128),
         vmem(5 * ROWS, 128), vmem(ROWS, 128)],
        [from_right, from_left, pairs, e_all, h_all, mtable],
        aliases={4: 0},
    )
    at = len(rest)
    operands = rest + [
        e_all, h_all, se, sh, traits, sums, d_all, c_all, background, local, table,
        contrasts, forward,
    ]
    outs = call(
        step_kernel(count, reach, at),
        [jax.ShapeDtypeStruct((PLANES * OWN, 128), jnp.float32),
         jax.ShapeDtypeStruct((PLANES * OWN, 128), jnp.float32),
         jax.ShapeDtypeStruct((DZ * OWN, 128), jnp.float32),
         vmem(PLANES * ROWS, 128), vmem(PLANES * ROWS, 128), vmem(3 * ROWS, 128),
         vmem(3 * ROWS, 128)],
        operands,
        aliases={at: 3, at + 1: 4, at + 2: 5, at + 3: 6},
        scratch=[vmem(PLANES * ROWS, 128), vmem(3 * ROWS, 128), vmem(DZ * OWN, 128),
                 ],
    )
    return (
        outs[0].reshape(electric.shape), outs[1].reshape(magnetic.shape),
        outs[2].reshape(density.shape),
    )


def solution(mesh):
    return jax.shard_map(
        body,
        mesh=mesh,
        in_specs=(
            P(None, "gx", "gy"),
            P("gx", "gy"),
            P(None, "gx", "gy"),
            P(),
            P(),
            P(None, None, "gx", "gy"),
            P(None, None, "gx", "gy"),
            P(None, None, None, "gx", "gy"),
        ),
        out_specs=(P(None, None, "gx", "gy"), P(None, None, "gx", "gy"), P(None, "gx", "gy")),
        check_vma=False,
    )
```

```python
import math

import jax
import jax.numpy as jnp
import numpy as np
from jax import lax
from jax.experimental import pallas as pl
from jax.experimental.pallas import tpu as pltpu
from jax.sharding import PartitionSpec as P

CY = 128
Z = 8
DZ = 4
STEPS = 4
TILE = 8
MATS = 4

courant = 0.5
sharpness = 4.0
threshold = 0.5

ROWS = 24
OWN = 16
SLOT = 48
KINDS = 3 * SLOT
LAYERS = KINDS + 24
EXTRA = LAYERS + 16
PLANES = 3 * Z

VM = pl.BlockSpec(memory_space=pltpu.VMEM)
ANY = pl.BlockSpec(memory_space=pl.ANY)


def vmem(*shape, dtype=jnp.float32):
    return pltpu.VMEM(shape, dtype)


def call(kernel, outs, ins, aliases=None, scratch=(), in_specs=None, out_specs=None):
    in_specs = in_specs or [VM] * len(ins)
    ins = [
        pltpu.with_memory_space_constraint(x, pltpu.VMEM if spec is VM else pltpu.HBM)
        for x, spec in zip(ins, in_specs)
    ]
    return pl.pallas_call(
        kernel,
        out_shape=outs,
        in_specs=in_specs,
        out_specs=out_specs or [VM] * len(outs),
        scratch_shapes=list(scratch),
        input_output_aliases=aliases or {},
        compiler_params=pltpu.CompilerParams(vmem_limit_bytes=32 * 1024 * 1024),
    )(*ins)


def lanes(rows):
    return lax.broadcasted_iota(jnp.int32, (rows, 128), 1)


def roll(x, by):
    return pltpu.roll(x, by % x.shape[1], 1)


def roll_rows(x, by):
    return pltpu.roll(x, by % x.shape[0], 0)


def sent(x, axis, by):
    size = lax.axis_size(axis)
    return lax.ppermute(x, axis, [(i, (i + by) % size) for i in range(size)])


def weight(offset, count, reach):
    ahead = np.mod(offset, count).astype(np.float64)
    behind = np.mod(-offset, count).astype(np.float64)
    return np.exp(-ahead / reach) + np.exp(-behind / reach)


def filter_constants(count, reach):
    source = np.arange(CY)
    strip = np.concatenate([np.arange(-4, 4), np.arange(CY - 4, CY + 4)])
    targets = np.concatenate([source, np.tile(strip, Z)])
    table = weight(targets[None, :] - source[:, None], count, reach)
    rows = np.zeros((8, 256))
    rows[0] = np.exp(-targets / reach)
    rows[1] = np.exp(targets / reach)
    rows[2, :CY] = np.exp(source / reach)
    rows[3, :CY] = np.exp(-source / reach)
    return np.concatenate([table, rows], 0).astype(np.float32)


def edge_window(planes):
    lane = lanes(planes[0].shape[0])
    width, by = 8, 16
    while len(planes) > 1:
        kept = ((lane + 4) & 127) < width
        planes = [
            jnp.where(kept, planes[i], roll(planes[i + 1], by)) for i in range(0, len(planes), 2)
        ]
        width, by = width + by, 2 * by
    return planes[0]


def edge_tiles(groups):
    lane = lanes(groups[0][0].shape[0])
    quarter = (lane >> 2) & 3
    found = [edge_window(planes) for planes in groups]

    def pick(a, b, c, d):
        return jnp.where(quarter < 2, jnp.where(quarter == 0, a, b), jnp.where(quarter == 2, c, d))

    left, right = [], []
    for i in (0, 4):
        one, two, three, four = found[i : i + 4]
        left.append(pick(one, roll(two, 4), roll(three, 8), roll(four, 12)))
        right.append(pick(roll(one, 4), roll(two, 8), roll(three, 12), roll(four, 16)))
    pairs = [
        jnp.where(quarter < 2, roll(found[i], 4), roll(found[i + 1], 12)) for i in range(0, 8, 2)
    ]
    return pairs, left, right


def density_planes(layers, cells):
    return [plane for layer in layers for plane in (layer, cells)]


def with_sums(tiles, layers):
    lane = lanes(layers[0].shape[0])
    column = lanes(1).astype(jnp.float32) * (1.0 / (4.0 * CY))
    rising, falling = jnp.exp(column), jnp.exp(-column)
    for l, layer in enumerate(layers):
        at = (2 * l + 1) * 16 + 12
        up = jnp.sum(layer * rising, axis=1, keepdims=True)
        down = jnp.sum(layer * falling, axis=1, keepdims=True)
        tiles = [
            jnp.where(lane == at, up, jnp.where(lane == at + 1, down, tile)) for tile in tiles
        ]
    return tiles


def pack_kernel(
    electric, magnetic, density, material, mask,
    to_prev, to_next, e_own, h_own, d_own, m_own, c_all,
    mask_v, sems,
):
    copies = []
    moved = [
        (electric, e_own), (magnetic, h_own), (density, d_own), (material, m_own), (mask, mask_v),
    ]
    for i, (source, target) in enumerate(moved):
        copy = pltpu.make_async_copy(source, target, sems.at[i])
        copy.start()
        copies.append(copy)
    copies[-1].wait()
    cells = cell_rows(mask_v[...])
    c_all[0:TILE, :] = jnp.broadcast_to(cells[0:1], (TILE, 128))
    c_all[TILE:OWN, :] = jnp.broadcast_to(cells[1:2], (TILE, 128))
    for copy in copies[:-1]:
        copy.wait()

    def e(channel, row):
        return e_own[pl.ds(channel * Z * OWN + row, Z, stride=OWN), :]

    def h(channel, row):
        return h_own[pl.ds(channel * Z * OWN + row, Z, stride=OWN), :]

    def ahead_part(row):
        part_y = h(1, row) + courant * (e(2, row + 1) - e(2, row))
        part_z = h(2, row) - courant * (e(1, row + 1) - e(1, row))
        return part_y, part_z

    for out, first, mask_row in ((to_next, OWN - 3, 1), (to_prev, 0, 0)):
        for slot in range(3):
            row, at = first + slot, slot * SLOT
            for channel in range(3):
                out[at + 8 * channel : at + 8 * channel + 8, :] = e(channel, row)
                out[at + 24 + 8 * channel : at + 32 + 8 * channel, :] = h(channel, row)
            out[KINDS + 8 * slot : KINDS + 8 * slot + 8, :] = (
                m_own[pl.ds(row, Z, stride=OWN), :].astype(jnp.float32)
            )
            out[LAYERS + 4 * slot : LAYERS + 4 * slot + 4, :] = (
                d_own[pl.ds(row, DZ, stride=OWN), :]
            )
        out[LAYERS + 12 : LAYERS + 16, :] = jnp.broadcast_to(
            cells[mask_row : mask_row + 1], (4, 128)
        )
    part_y, part_z = ahead_part(2)
    to_prev[2 * SLOT + 32 : 2 * SLOT + 40, :] = part_y
    to_prev[2 * SLOT + 40 : 2 * SLOT + 48, :] = part_z
    part_y, part_z = ahead_part(OWN - 4)
    to_next[EXTRA : EXTRA + 8, :] = e(0, OWN - 4)
    to_next[EXTRA + 8 : EXTRA + 16, :] = part_y
    to_next[EXTRA + 16 : EXTRA + 24, :] = part_z


def own_kernel(
    table_in, mtable_in, contrast_in, e_own, h_own, d_own, m_own, c_own,
    table, mtable, contrast, e_all, h_all, d_all, c_all, pairs_out, left_out, right_out,
    m_all, local, sems,
):
    copies = [
        pltpu.make_async_copy(source, target, sems.at[i])
        for i, (source, target) in enumerate(
            ((table_in, table), (mtable_in, mtable), (contrast_in, contrast))
        )
    ]
    for copy in copies:
        copy.start()
    c_all[0:OWN, :] = c_own[...]
    groups = []
    for source, target in ((e_own, e_all), (h_own, h_all)):
        for channel in range(3):
            planes = []
            for z in range(Z):
                p = channel * Z + z
                plane = source[p * OWN : (p + 1) * OWN, :]
                target[p * ROWS : p * ROWS + OWN, :] = plane
                planes.append(plane)
            groups.append(planes)
    planes = []
    for z in range(Z):
        plane = m_own[z * OWN : (z + 1) * OWN, :].astype(jnp.float32)
        m_all[z * ROWS : z * ROWS + OWN, :] = plane
        planes.append(plane)
    groups.append(planes)
    layers = []
    for l in range(DZ):
        layers.append(d_own[l * OWN : (l + 1) * OWN, :])
        d_all[l * ROWS : l * ROWS + OWN, :] = layers[l]
    groups.append(density_planes(layers, c_own[...]))
    pairs, left, right = edge_tiles(groups)
    left[1], right[1] = with_sums([left[1], right[1]], layers)
    for i in range(4):
        pairs_out[i * ROWS : i * ROWS + OWN, :] = pairs[i]
    for i in range(2):
        left_out[i * ROWS : i * ROWS + OWN, :] = left[i]
        right_out[i * ROWS : i * ROWS + OWN, :] = right[i]
    for copy in copies:
        copy.wait()
    smooth = jnp.dot(
        jnp.concatenate(layers, 0), table[0:128, :], precision=lax.Precision.HIGHEST,
        preferred_element_type=jnp.float32,
    )
    for l in range(DZ):
        local[l * ROWS : l * ROWS + OWN, :] = smooth[l * OWN : (l + 1) * OWN]


def unpack(got, first, e_all, h_all, d_all, c_all, m_all):
    for slot in range(3):
        at, row = slot * SLOT, first + slot
        for channel in range(3):
            where = pl.ds(channel * Z * ROWS + row, Z, stride=ROWS)
            e_all[where, :] = got[at + 8 * channel : at + 8 * channel + 8, :]
            h_all[where, :] = got[at + 24 + 8 * channel : at + 32 + 8 * channel, :]
        m_all[pl.ds(row, Z, stride=ROWS), :] = got[KINDS + 8 * slot : KINDS + 8 * slot + 8, :]
        d_all[pl.ds(row, DZ, stride=ROWS), :] = got[LAYERS + 4 * slot : LAYERS + 4 * slot + 4, :]
        c_all[row : row + 1, :] = got[LAYERS + 12 : LAYERS + 13, :]


def unpack_next(got, e_all, h_all, d_all, c_all, m_all):
    unpack(got, 16, e_all, h_all, d_all, c_all, m_all)
    zeros = jnp.zeros((Z, 128), jnp.float32)
    for channel in range(3):
        where = pl.ds(channel * Z * ROWS + 19, Z, stride=ROWS)
        e_all[where, :] = got[2 * SLOT + 8 * channel : 2 * SLOT + 8 * channel + 8, :]
        h_all[where, :] = zeros
    m_all[pl.ds(19, Z, stride=ROWS), :] = zeros
    d_all[pl.ds(19, DZ, stride=ROWS), :] = zeros[0:DZ]
    c_all[19:20, :] = zeros[0:1]


def unpack_prev(got, e_all, h_all, d_all, c_all, m_all):
    unpack(got, 21, e_all, h_all, d_all, c_all, m_all)
    zeros = jnp.zeros((Z, 128), jnp.float32)
    for channel in range(3):
        where = pl.ds(channel * Z * ROWS + 20, Z, stride=ROWS)
        extra = got[EXTRA + 8 * channel : EXTRA + 8 * channel + 8, :]
        if channel == 0:
            e_all[where, :] = extra
            h_all[where, :] = zeros
        else:
            e_all[where, :] = got[8 * channel : 8 * channel + 8, :]
            h_all[where, :] = extra
    m_all[pl.ds(20, Z, stride=ROWS), :] = zeros
    d_all[pl.ds(20, DZ, stride=ROWS), :] = zeros[0:DZ]
    c_all[20:21, :] = zeros[0:1]


def early_kernel(got, e_in, h_in, d_in, c_in, m_in, e_all, h_all, d_all, c_all, m_all):
    unpack_prev(got, e_all, h_all, d_all, c_all, m_all)


def halo_kernel(
    got, e_in, h_in, d_in, c_in, m_in, pairs_in, left_in, right_in, table,
    e_all, h_all, d_all, c_all, m_all, pairs_out, left_out, right_out, sums_out,
):
    unpack_next(got, e_all, h_all, d_all, c_all, m_all)

    groups = []
    for target in (e_all, h_all):
        for channel in range(3):
            groups.append(
                [target[(channel * Z + z) * ROWS + OWN : (channel * Z + z + 1) * ROWS, :] for z in range(Z)]
            )
    groups.append([m_all[z * ROWS + OWN : (z + 1) * ROWS, :] for z in range(Z)])
    layers = [d_all[l * ROWS + OWN : (l + 1) * ROWS, :] for l in range(DZ)]
    groups.append(density_planes(layers, c_all[OWN:ROWS, :]))
    pairs, left, right = edge_tiles(groups)
    left[1], right[1] = with_sums([left[1], right[1]], layers)
    for i in range(4):
        pairs_out[i * ROWS + OWN : (i + 1) * ROWS, :] = pairs[i]
    for i in range(2):
        left_out[i * ROWS + OWN : (i + 1) * ROWS, :] = left[i]
        right_out[i * ROWS + OWN : (i + 1) * ROWS, :] = right[i]
    place = lanes(8) & 15
    packed = left[1]
    packed = jnp.where(place < 12, roll(left_in[ROWS : ROWS + 8, :], -2), packed)
    sums_out[...] = jnp.where(place > 13, roll(left_in[ROWS + 8 : ROWS + OWN, :], 2), packed)


def background_kernel(m_all, d_all, mtable, table, local_in, background, local):
    smooth = jnp.dot(
        jnp.concatenate([d_all[l * ROWS + OWN : (l + 1) * ROWS, :] for l in range(DZ)], 0),
        table[0:128, :], precision=lax.Precision.HIGHEST, preferred_element_type=jnp.float32,
    )
    for l in range(DZ):
        local[l * ROWS + OWN : (l + 1) * ROWS, :] = smooth[l * 8 : (l + 1) * 8]
    entries = mtable[...]
    for z in range(Z):
        kind = m_all[z * ROWS : (z + 1) * ROWS, :]
        for channel in range(3):
            p = channel * Z + z
            background[p * ROWS : (p + 1) * ROWS, :] = looked_up(kind, entries, channel)


def looked_up(kind, entries, channel):
    one = [entries[channel : channel + 1, i : i + 1] for i in range(MATS)]
    return jnp.where(
        kind < 1.5, jnp.where(kind < 0.5, one[0], one[1]), jnp.where(kind < 2.5, one[2], one[3])
    )


def cell_rows(mask):
    spread = lax.broadcasted_iota(jnp.int32, (mask.shape[1], 128), 0) == (
        lanes(mask.shape[1]) // TILE
    )
    return jnp.dot(
        mask.astype(jnp.float32), spread.astype(jnp.float32), preferred_element_type=jnp.float32
    )


def project(values):
    base = math.tanh(sharpness * threshold)
    bottom = base + math.tanh(sharpness * (1.0 - threshold))
    level = jnp.tanh(sharpness * (values - threshold))
    return (base + level) * (1.0 / bottom), (sharpness / bottom) * (1.0 - level * level)


def plane_of(ref, channel, z, rows=ROWS):
    p = channel * Z + z
    return ref[p * ROWS : p * ROWS + rows, :]


def strip_of(ref, channel):
    return ref[channel * ROWS : (channel + 1) * ROWS, :]


def keep(ref, fields):
    for c, field in enumerate(fields):
        ref[c * ROWS : (c + 1) * ROWS, :] = field


def strip_magnetic(old, electric):
    lane = lanes(ROWS)
    ex, ey, ez = electric
    up_x = jnp.where(lane < 112, roll(ex, -16), 0.0)
    up_y = jnp.where(lane < 112, roll(ey, -16), 0.0)
    curls = (
        (roll(ez, -1) - ez) - (up_y - ey),
        (up_x - ex) - (roll_rows(ez, -1) - ez),
        (roll_rows(ey, -1) - ey) - (roll(ex, -1) - ex),
    )
    return [field - curl for field, curl in zip(old, curls)]


def strip_electric(old, magnetic, inverse):
    lane = lanes(ROWS)
    hx, hy, hz = magnetic
    down_x = jnp.where(lane >= 16, roll(hx, 16), 0.0)
    down_y = jnp.where(lane >= 16, roll(hy, 16), 0.0)
    curls = (
        (hz - roll(hz, 1)) - (hy - down_y),
        (hx - down_x) - (hz - roll_rows(hz, 1)),
        (hy - roll_rows(hy, 1)) - (hx - roll(hx, 1)),
    )
    return [old[c] + inverse[c] * curl for c, curl in enumerate(curls)]


def planes_magnetic(e_all, h_in, h_out, strip_e, scale=1.0):
    lane = lanes(ROWS)
    last, first = lane == 127, lane == 0
    zero = jnp.zeros((ROWS, 128), jnp.float32)
    mixed = jnp.where((lane & 15) == 12, strip_e[2], roll(strip_e[0], 1))
    ex_up, ey_up = plane_of(e_all, 0, 0), plane_of(e_all, 1, 0)
    for z in range(Z):
        ex, ey, ez = ex_up, ey_up, plane_of(e_all, 2, z)
        ex_up = plane_of(e_all, 0, z + 1) if z + 1 < Z else zero
        ey_up = plane_of(e_all, 1, z + 1) if z + 1 < Z else zero
        beyond = roll(mixed, 115 - 16 * z)
        dy_ez = jnp.where(last, beyond, roll(ez, -1)) - ez
        dy_ex = roll(jnp.where(first, beyond, ex), -1) - ex
        dx_ez = roll_rows(ez, -1) - ez
        dx_ey = roll_rows(ey, -1) - ey
        for channel, curl in enumerate(
            (dy_ez - (ey_up - ey), (ex_up - ex) - dx_ez, dx_ey - dy_ex)
        ):
            p = channel * Z + z
            old = plane_of(h_in, channel, z)
            h_out[p * ROWS : (p + 1) * ROWS, :] = (old if scale == 1.0 else scale * old) - curl


def planes_electric(e_all, h_all, inverse, strip_h, stored_at, contrast, gained, e_out, stride):
    lane = lanes(ROWS)
    last, first = lane == 127, lane == 0
    mixed = jnp.where((lane & 15) == 3, strip_h[2], roll(strip_h[0], -1))
    hx = hy = jnp.zeros((ROWS, 128), jnp.float32)
    for z in range(Z):
        hx_down, hy_down = hx, hy
        hx, hy, hz = (plane_of(h_all, c, z) for c in range(3))
        beyond = roll(mixed, -(16 * z + 3))
        dy_hz = hz - jnp.where(first, beyond, roll(hz, 1))
        dy_hx = hx - roll(jnp.where(last, beyond, hx), 1)
        dx_hz = hz - roll_rows(hz, 1)
        dx_hy = hy - roll_rows(hy, 1)
        total = jnp.zeros((OWN, 128), jnp.float32)
        for channel, curl in enumerate(
            (dy_hz - (hy - hy_down), (hx - hx_down) - dx_hz, dx_hy - dy_hx)
        ):
            p = channel * Z + z
            value = (
                plane_of(e_all, channel, z, stride)
                + plane_of(inverse, channel, z, stride) * curl[:stride]
            )
            e_out[p * stride : (p + 1) * stride, :] = value
            total = total + contrast[channel] * (value[:OWN] * stored_at(p).astype(jnp.float32))
        l = z // 2
        gained[l * OWN : (l + 1) * OWN, :] = gained[l * OWN : (l + 1) * OWN, :] + total


def lane_factor(m, count, reach):
    up, down = math.exp(-CY * m / reach), math.exp(-(count - CY * m) / reach)
    return jnp.where((lanes(ROWS) & 15) == 12, up, down)


def norm_of(count, reach):
    return 2.0 * float(np.sum(np.exp(-np.arange(count) / reach)))


def first_kernel(count, reach):
    devices = count // CY
    norm_total = norm_of(count, reach)

    def fix(delta):
        if delta == 0:
            return 1.0 - math.exp(-count / reach)
        return (
            math.exp(-delta / reach) + math.exp(-(count - delta) / reach)
            - math.exp(-(count + delta) / reach) - math.exp(delta / reach)
        )

    def kernel(from_right, from_left, pairs, e_all, h_in, mtable, h_all, se, sh, traits, sums):
        lane = lanes(ROWS)
        place = lane & 15
        odd = ((lane >> 4) & 1) == 1
        part = place >> 2
        got_left = [from_left[i * ROWS : (i + 1) * ROWS, :] for i in range(2)]
        got_right = [from_right[i * ROWS : (i + 1) * ROWS, :] for i in range(2)]

        def strip(index):
            tile, q = index // 4, index % 4
            pair = pairs[(index // 2) * ROWS : (index // 2 + 1) * ROWS, :]
            if index % 2 == 0:
                own_l, own_r = pair, roll(pair, 8)
            else:
                own_l, own_r = roll(pair, -8), pair
            outer = jnp.where(
                part == 0, roll(got_left[tile], -4 * q), roll(got_right[tile], 12 - 4 * q)
            )
            return jnp.where(part == 1, own_l, jnp.where(part == 2, own_r, outer))

        electric = [strip(c) for c in range(3)]
        keep(se, electric)
        keep(sh, strip_magnetic([strip(3 + c) * (1.0 / courant) for c in range(3)], electric))
        raw = strip(7)
        marks = jnp.where(odd, raw, roll(raw, -16))
        layers = jnp.where(odd, roll(raw, 16), raw)
        known = jnp.zeros((ROWS, 128), jnp.float32)
        for delta in range(4):
            value = fix(delta) * layers
            ahead = value if delta == 0 else roll(value, delta)
            behind = value if delta == 0 else roll(value, -delta)
            known = known + jnp.where(place >= 12 + delta, ahead, 0.0)
            known = known + jnp.where(place < 4 - delta, behind, 0.0)
        kind = strip(6)
        entries = mtable[...]
        keep(
            traits,
            [
                0.5 * layers + (0.5 / norm_total) * known,
                jnp.where((place & 2) == 2, marks, roll(marks, -2)),
            ]
            + [looked_up(kind, entries, c) for c in range(3)],
        )
        sums[...] = (
            lane_factor(1, count, reach) * got_left[1]
            + lane_factor(devices - 1, count, reach) * got_right[1]
        )
        planes_magnetic(e_all, h_in, h_all, electric, 1.0 / courant)

    return kernel


def step_kernel(count, reach, others):
    norm_total = norm_of(count, reach)

    def kernel(*refs):
        rest = refs[:others]
        (e_in, h_in, se_in, sh_in, traits, sums_in, d_all, c_all, background, local, table,
         contrast_in, forward,
         e_final, h_final, gradient, e_all, h_all, se, sh,
         inverse, si, gained) = refs[others:]
        contrast = [contrast_in[0:1, c : c + 1] for c in range(3)]
        lane = lanes(ROWS)
        layer_of = lane >> 5

        sums = sums_in[...]
        for i, other in enumerate(rest):
            packed = other[...]
            sums = sums + lane_factor(2 + i, count, reach) * jnp.concatenate(
                [roll(packed, 2), roll(packed, -2), packed], 0
            )
        strip_smooth = jnp.zeros((ROWS, 128), jnp.float32)
        designs = []
        cells = c_all[...]
        for l in range(DZ):
            at = (2 * l + 1) * 16 + 12
            up = jnp.broadcast_to(sums[:, at : at + 1], (ROWS, 128))
            down = jnp.broadcast_to(sums[:, at + 1 : at + 2], (ROWS, 128))
            both = local[l * ROWS : (l + 1) * ROWS, :]
            smooth = both[:, :128] + table[128:129, :128] * up + table[129:130, :128] * down
            far = both[:, 128:] + table[128:129, 128:] * up + table[129:130, 128:] * down
            strip_smooth = jnp.where(layer_of == l, far, strip_smooth)
            filtered = 0.5 * d_all[l * ROWS : (l + 1) * ROWS, :] + (0.5 / norm_total) * smooth
            projected, slope = project(filtered)
            designs.append(cells * projected)
            gradient[l * OWN : (l + 1) * OWN, :] = slope[:OWN] * cells[:OWN]
        projected, _ = project(strip_of(traits, 0) + (0.5 / norm_total) * strip_smooth)
        strip_design = strip_of(traits, 1) * projected
        keep(
            si,
            [courant * courant / (strip_of(traits, 2 + c) + strip_design * contrast[c]) for c in range(3)],
        )
        for z in range(Z):
            for channel in range(3):
                p = channel * Z + z
                inverse[p * ROWS : (p + 1) * ROWS, :] = courant * courant / (
                    background[p * ROWS : (p + 1) * ROWS, :] + designs[z // 2] * contrast[channel]
                )
        gained[...] = jnp.zeros_like(gained)

        def step(t, carry):
            strip_h = [strip_of(sh, c) for c in range(3)]
            planes_electric(
                e_all, h_all, inverse, strip_h, lambda p: forward[t, p], contrast, gained,
                e_all, ROWS,
            )
            strip_e = strip_electric(
                [strip_of(se, c) for c in range(3)], strip_h, [strip_of(si, c) for c in range(3)]
            )
            keep(se, strip_e)
            planes_magnetic(e_all, h_all, h_all, strip_e)
            keep(sh, strip_magnetic(strip_h, strip_e))
            return carry

        lax.fori_loop(0, STEPS - 1, step, 0)
        for p in range(PLANES):
            h_final[p * OWN : (p + 1) * OWN, :] = courant * h_all[p * ROWS : p * ROWS + OWN, :]
        planes_electric(
            e_all, h_all, inverse, [strip_of(sh, c) for c in range(3)],
            lambda p: forward[STEPS - 1, p], contrast, gained, e_final, OWN,
        )
        gradient[...] = gradient[...] * gained[...]

    return kernel


def body(
    density, tile_mask, material, material_table, contrast, electric, magnetic, forward_fields
):
    devices = lax.axis_size("gy")
    count = density.shape[2] * devices
    reach = 4.0 * CY
    constants = filter_constants(count, reach)

    to_prev, to_next, e_own, h_own, d_own, m_own, c_own = call(
        pack_kernel,
        [vmem(EXTRA, 128), vmem(EXTRA + 24, 128),
         vmem(PLANES * OWN, 128), vmem(PLANES * OWN, 128), vmem(DZ * OWN, 128),
         vmem(Z * OWN, 128, dtype=jnp.int32), vmem(OWN, 128)],
        [electric.reshape(PLANES * OWN, 128), magnetic.reshape(PLANES * OWN, 128),
         density.reshape(DZ * OWN, 128),
         material.reshape(Z * OWN, 128), tile_mask],
        scratch=[vmem(*tile_mask.shape, dtype=jnp.int32), pltpu.SemaphoreType.DMA((5,))],
        in_specs=[ANY] * 5,
    )
    from_prev = sent(to_next, "gx", 1)
    from_next = sent(to_prev, "gx", -1)
    table, mtable, contrasts, e_all, h_all, d_all, c_all, pairs, left, right, m_all, local = call(
        own_kernel,
        [vmem(*constants.shape), vmem(3, MATS), vmem(1, 3), vmem(PLANES * ROWS, 128), vmem(PLANES * ROWS, 128), vmem(DZ * ROWS, 128),
         vmem(ROWS, 128), vmem(4 * ROWS, 128), vmem(2 * ROWS, 128), vmem(2 * ROWS, 128), vmem(Z * ROWS, 128),
         vmem(DZ * ROWS, 256)],
        [constants, material_table, contrast.reshape(1, 3), e_own, h_own, d_own, m_own, c_own],
        scratch=[pltpu.SemaphoreType.DMA((3,))], in_specs=[ANY] * 3 + [VM] * 5,
    )
    fields = [vmem(PLANES * ROWS, 128), vmem(PLANES * ROWS, 128), vmem(DZ * ROWS, 128),
              vmem(ROWS, 128), vmem(Z * ROWS, 128)]
    e_all, h_all, d_all, c_all, m_all = call(
        early_kernel, fields, [from_prev, e_all, h_all, d_all, c_all, m_all],
        aliases={i + 1: i for i in range(5)},
    )
    e_all, h_all, d_all, c_all, m_all, pairs, left, right, sums = call(
        halo_kernel,
        [vmem(PLANES * ROWS, 128), vmem(PLANES * ROWS, 128), vmem(DZ * ROWS, 128),
         vmem(ROWS, 128), vmem(Z * ROWS, 128), vmem(4 * ROWS, 128),
         vmem(2 * ROWS, 128), vmem(2 * ROWS, 128), vmem(8, 128)],
        [from_next, e_all, h_all, d_all, c_all, m_all, pairs, left, right, table],
        aliases={i + 1: i for i in range(8)},
    )
    from_left = sent(right, "gy", 1)
    from_right = sent(left, "gy", -1)
    rest = [sent(sums, "gy", m) for m in range(2, devices - 1)]
    background, local = call(
        background_kernel, [vmem(PLANES * ROWS, 128), vmem(DZ * ROWS, 256)],
        [m_all, d_all, mtable, table, local], aliases={4: 1},
    )
    h_all, se, sh, traits, sums = call(
        first_kernel(count, reach),
        [vmem(PLANES * ROWS, 128), vmem(3 * ROWS, 128), vmem(3 * ROWS, 128),
         vmem(5 * ROWS, 128), vmem(ROWS, 128)],
        [from_right, from_left, pairs, e_all, h_all, mtable],
        aliases={4: 0},
    )
    at = len(rest)
    operands = rest + [
        e_all, h_all, se, sh, traits, sums, d_all, c_all, background, local, table,
        contrasts, forward_fields.reshape(STEPS, PLANES, OWN, 128),
    ]
    outs = call(
        step_kernel(count, reach, at),
        [jax.ShapeDtypeStruct((PLANES * OWN, 128), jnp.float32),
         jax.ShapeDtypeStruct((PLANES * OWN, 128), jnp.float32),
         jax.ShapeDtypeStruct((DZ * OWN, 128), jnp.float32),
         vmem(PLANES * ROWS, 128), vmem(PLANES * ROWS, 128), vmem(3 * ROWS, 128),
         vmem(3 * ROWS, 128)],
        operands,
        aliases={at: 3, at + 1: 4, at + 2: 5, at + 3: 6},
        scratch=[vmem(PLANES * ROWS, 128), vmem(3 * ROWS, 128), vmem(DZ * OWN, 128),
                 ],
    )
    return (
        outs[0].reshape(electric.shape), outs[1].reshape(magnetic.shape),
        outs[2].reshape(density.shape),
    )


def solution(mesh):
    return jax.shard_map(
        body,
        mesh=mesh,
        in_specs=(
            P(None, "gx", "gy"),
            P("gx", "gy"),
            P(None, "gx", "gy"),
            P(),
            P(),
            P(None, None, "gx", "gy"),
            P(None, None, "gx", "gy"),
            P(None, None, None, "gx", "gy"),
        ),
        out_specs=(P(None, None, "gx", "gy"), P(None, None, "gx", "gy"), P(None, "gx", "gy")),
        check_vma=False,
    )
```
